32 devices in a mesh: dp: 8 (over y, x, core), mp: 4 (over z).
Axes of the slice: x: 2, y: 2, z: 4, core: 2. Of those that a mesh axis runs over, the one named last changes fastest.
Arguments:
- tokens: bfloat16 [16, 1024, 768], P('dp', 'mp'), may hold values from -6 to 6
- cotangent: bfloat16 [16, 1024, 768], P('dp', 'mp'), may hold values from -6 to 6
- w_query: bfloat16 [768, 768], P('dp', 'mp'), may hold values from -0.21875 to 0.21875
- w_key: bfloat16 [768, 768], P('dp', 'mp'), may hold values from -0.21875 to 0.21875
- w_value: bfloat16 [768, 768], P('dp', 'mp'), may hold values from -0.21875 to 0.21875
- w_out: bfloat16 [768, 768], P('mp', 'dp'), may hold values from -1.75 to 1.75
- w_inner: bfloat16 [768, 3072], P('dp', 'mp'), may hold values from -0.21875 to 0.21875
- w_outer: bfloat16 [3072, 768], P('mp', 'dp'), may hold values from -0.109375 to 0.109375
- gain_attn: bfloat16 [768], P('dp'), may hold values from 0.099609375 to 1.8984375
- shift_attn: bfloat16 [768], P('dp'), may hold values from -3 to 3
- gain_ffn: bfloat16 [768], P('dp'), may hold values from 0.099609375 to 1.8984375
- shift_ffn: bfloat16 [768], P('dp'), may hold values from -3 to 3
- seq_lengths: int32 [16], P('dp'), may hold values from 256 to 1024, as said below
- rand_blocks: int32 [12, 16, 3], P('mp'), may hold values from 1 to 14, as said below
Outputs:
- output: bfloat16 [16, 1024, 768], P('dp', 'mp')
- grad_tokens: bfloat16 [16, 1024, 768], P('dp', 'mp')
- grad_w_query: float32 [768, 768], P('dp', 'mp')
- grad_w_key: float32 [768, 768], P('dp', 'mp')
- grad_w_value: float32 [768, 768], P('dp', 'mp')
- grad_w_out: float32 [768, 768], P('mp', 'dp')
- grad_w_inner: float32 [768, 3072], P('dp', 'mp')
- grad_w_outer: float32 [3072, 768], P('mp', 'dp')
- grad_gain_attn: float32 [768], P('dp')
- grad_shift_attn: float32 [768], P('dp')
- grad_gain_ffn: float32 [768], P('dp')
- grad_shift_ffn: float32 [768], P('dp')
The draws below stay inside these ranges and needn't reach their ends.
Inputs may be any that keep to these rules, and one draw needn't show every extreme that they name: `seq_lengths`: valid positions of each sequence; the first sequence has 1024 and the second 1024 // 4. `rand_blocks`: for each head and block row r: three different block numbers, none equal to 0 or 15 and none within one of r.
All inputs are finite; a program needn't handle non-finite values.
Results may differ from the reference program's by a relative error of at most 0.017.
Values may be sent and summed in bfloat16 or wider, within the bound.
A program may use at most 128 MiB of HBM per device.

```python
import math
import jax
import jax.numpy as jnp
from jax import lax

D = 768
HEADS = 12
HEAD = 64
FF = 3072
BLOCK = 64
RAND = 3
BLOCKS_PER_SEQ = 16
L = 1024
SEQS = 16


def draw_seq_lengths(key, part):
    drawn = jax.random.randint(key, (SEQS,), L // 4, L + 1)
    places = jnp.arange(SEQS)
    drawn = jnp.where(places == 0, L, drawn)
    drawn = jnp.where(places == 1, L // 4, drawn)
    return drawn.astype(jnp.int32)


def draw_rand_blocks(key, part):
    device_ranks = jax.random.randint(key, (HEADS, BLOCKS_PER_SEQ, BLOCKS_PER_SEQ), 0, 65536)
    row_block = jnp.arange(BLOCKS_PER_SEQ)[None, :, None]
    column_block = jnp.arange(BLOCKS_PER_SEQ)[None, None, :]
    device_ranks = device_ranks * BLOCKS_PER_SEQ + column_block
    extra_keys = 65536 * BLOCKS_PER_SEQ
    device_ranks = jnp.where((row_block == 0) & (column_block == BLOCKS_PER_SEQ - 2), device_ranks + extra_keys, device_ranks)
    device_ranks = jnp.where((row_block == BLOCKS_PER_SEQ - 1) & (column_block == 1), device_ranks + extra_keys, device_ranks)
    excluded = (column_block == 0) | (column_block == BLOCKS_PER_SEQ - 1) | (jnp.abs(row_block - column_block) <= 1)
    device_ranks = jnp.where(excluded, -1, device_ranks)
    _, chosen = lax.top_k(device_ranks, RAND)
    return chosen.astype(jnp.int32)


def levels(rng, shape, pieces, least, largest):
    factor_of = 1.0
    for position, blocks in pieces:
        heights = jax.random.uniform(jax.random.fold_in(jax.random.fold_in(rng, 6), position), (blocks,), jnp.float32, least / len(pieces), largest / len(pieces))
        factor_of = factor_of * jnp.repeat(jnp.exp(heights), shape[position] // blocks).reshape((-1,) + (1,) * (len(shape) - 1 - position))
    return factor_of


def noise(own_key, dims, scale, limit, split=(), kind=jnp.bfloat16):
    array = scale * jax.random.normal(own_key, dims, jnp.float32)
    if split:
        array = array * levels(own_key, dims, split, -0.22, 0.18)
    return jnp.clip(array, -limit, limit).astype(kind)


def setup_inputs(seed: int = 0) -> dict:
    splits = jax.random.split(jax.random.key(seed), 15)
    tokens = noise(splits[0], (SEQS, L, D), 1.0, 6.0, ((0, 8), (1, 4)))
    cotangent = noise(splits[1], (SEQS, L, D), 1.0, 6.0, ((0, 8), (1, 4)))
    w_query = noise(splits[2], (D, D), D ** -0.5, 0.21875, ((0, 8), (1, 4)))
    w_key = noise(splits[3], (D, D), D ** -0.5, 0.21875, ((0, 8), (1, 4)))
    w_value = noise(splits[4], (D, D), D ** -0.5, 0.21875, ((0, 8), (1, 4)))
    w_out = noise(splits[5], (D, D), (D // 64) ** -0.5, 1.75, ((0, 4), (1, 8)))
    w_inner = noise(splits[6], (D, FF), D ** -0.5, 0.21875, ((0, 8), (1, 4)))
    w_outer = noise(splits[7], (FF, D), FF ** -0.5, 0.109375, ((0, 4), (1, 8)))
    gain_attn = jnp.clip(1.0 + 0.18 * jax.random.normal(splits[8], (D,), jnp.float32), 0.099609375, 1.8984375).astype(jnp.bfloat16)
    shift_attn = noise(splits[9], (D,), 0.5, 3.0, ((0, 8),))
    gain_ffn = jnp.clip(1.0 + 0.18 * jax.random.normal(splits[10], (D,), jnp.float32), 0.099609375, 1.8984375).astype(jnp.bfloat16)
    shift_ffn = noise(splits[11], (D,), 0.5, 3.0, ((0, 8),))
    seq_lengths = draw_seq_lengths(jax.random.fold_in(splits[14], 71), 0)
    rand_blocks = draw_rand_blocks(jax.random.fold_in(splits[14], 71), 0)
    return {"tokens": tokens, "cotangent": cotangent, "w_query": w_query, "w_key": w_key, "w_value": w_value, "w_out": w_out, "w_inner": w_inner, "w_outer": w_outer, "gain_attn": gain_attn, "shift_attn": shift_attn, "gain_ffn": gain_ffn, "shift_ffn": shift_ffn, "seq_lengths": seq_lengths, "rand_blocks": rand_blocks}


EPS = 1e-06
NEG = -1000000000.0
HIGH = lax.Precision.HIGHEST

@jax.custom_vjp
def low(v):
    return lax.optimization_barrier(v.astype(jnp.bfloat16)).astype(jnp.float32)

@jax.custom_vjp
def low_back(v):
    return v

def low_keep(v):
    return (low(v), None)

def low_pass(kept, grad):
    return (grad,)

def back_keep(v):
    return (v, None)

def back_low(kept, grad):
    return (low(grad),)
low.defvjp(low_keep, low_pass)
low_back.defvjp(back_keep, back_low)

def norm_rows(values, gain, shift):
    centre = values - lax.optimization_barrier(jnp.mean(values, -1, keepdims=True))
    spread = lax.optimization_barrier(jnp.mean(centre * centre, -1, keepdims=True))
    return centre * lax.rsqrt(spread + EPS) * gain + shift

def pattern(rand_blocks):
    blocks = jnp.arange(BLOCKS_PER_SEQ)
    rand_hits = jnp.any(rand_blocks[:, :, :, None] == blocks[None, None, None, :], axis=2)
    row_block = blocks[:, None]
    column_block = blocks[None, :]
    edge_row = (row_block == 0) | (row_block == BLOCKS_PER_SEQ - 1)
    edge_col = (column_block == 0) | (column_block == BLOCKS_PER_SEQ - 1)
    near_blocks = edge_row | edge_col | (jnp.abs(row_block - column_block) <= 1)
    allowed = rand_hits | near_blocks[None]
    return jnp.repeat(jnp.repeat(allowed, BLOCK, axis=1), BLOCK, axis=2)

def project(left_side, right_side):
    return jnp.dot(left_side, right_side, precision=HIGH)

def one_sequence(params, allowed, inputs, length):
    w_query, w_key, w_value, w_out, w_inner, w_outer, gain_attn, shift_attn, gain_ffn, shift_ffn = params
    score_scale = 1.0 / math.sqrt(HEAD)
    queries = low(low_back(project(inputs, w_query))).reshape(L, HEADS, HEAD)
    key_rows = low(low_back(project(inputs, w_key))).reshape(L, HEADS, HEAD)
    value_rows = low(low_back(project(inputs, w_value))).reshape(L, HEADS, HEAD)
    raw_scores = jnp.einsum('qhe,khe->hqk', queries, key_rows, precision=HIGH)
    scores = low_back(raw_scores * score_scale)
    key_ok = jnp.arange(L) < length
    masked = jnp.where(allowed & key_ok[None, None, :], scores, NEG)
    totals = jax.nn.logsumexp(masked, axis=-1, keepdims=True)
    soft_probs = low(jnp.exp(masked - totals))
    mixed_heads = jnp.einsum('hqk,khe->qhe', soft_probs, value_rows, precision=HIGH).reshape(L, D)
    context_output = low(low_back(mixed_heads))
    branch = low_back(project(context_output, w_out))
    hidden = norm_rows(inputs + branch, gain_attn, shift_attn)
    inner_pre = low_back(project(low(hidden), w_inner))
    active_tokens = low(jax.nn.gelu(inner_pre, approximate=False))
    outer_out = low_back(project(active_tokens, w_outer))
    result = norm_rows(hidden + outer_out, gain_ffn, shift_ffn)
    valid_rows = (jnp.arange(L) < length).astype(jnp.float32)
    return result * valid_rows[:, None]

def reference(tokens, cotangent, w_query, w_key, w_value, w_out, w_inner, w_outer, gain_attn, shift_attn, gain_ffn, shift_ffn, seq_lengths, rand_blocks):
    allowed = pattern(rand_blocks)

    def forward(inputs, *params):

        def per_seq(pair_item):
            return one_sequence(params, allowed, pair_item[0], pair_item[1])
        return lax.map(jax.checkpoint(per_seq), (inputs, seq_lengths))
    floats = [array_in.astype(jnp.float32) for array_in in (tokens, w_query, w_key, w_value, w_out, w_inner, w_outer, gain_attn, shift_attn, gain_ffn, shift_ffn)]
    result, pull_back = jax.vjp(forward, *floats)
    gradients = pull_back(cotangent.astype(jnp.float32))
    return (result.astype(jnp.bfloat16), gradients[0].astype(jnp.bfloat16), gradients[1], gradients[2], gradients[3], gradients[4], gradients[5], gradients[6], gradients[7], gradients[8], gradients[9], gradients[10])
```

```python
import math

import jax
import jax.numpy as jnp
from jax import lax
from jax.experimental import pallas as pl
from jax.experimental.pallas import tpu as pltpu
from jax.sharding import PartitionSpec as P

EPS = 1e-06
NEG = -1000000000.0
MESH = pl.DeviceIdType.MESH
F32 = jnp.float32
BF16 = jnp.bfloat16
ANY = pl.BlockSpec(memory_space=pl.ANY)
VMEM = pl.BlockSpec(memory_space=pltpu.VMEM)
DMA = pltpu.SemaphoreType.DMA


class Place:
    def __init__(self):
        self.d = lax.axis_index("dp")
        self.m = lax.axis_index("mp")
        self.c = lax.rem(self.d, 2)
        self.base = self.d - self.c
        self.sib = self.d + 1 - 2 * self.c
        bx = lax.rem(lax.div(self.d, 2), 2)
        by = lax.rem(lax.div(self.d, 4), 2)
        self.xp = self.d + 2 - 4 * bx
        self.yp = self.d + 4 - 8 * by
        self.bx = self.xp - self.c
        self.by = self.yp - self.c
        self.bd = self.bx + 4 - 8 * by
        self.h = lax.div(self.m, 2)
        self.a = lax.rem(self.m, 2)


def remote(src, dst, ssem, rsem, dev):
    return pltpu.make_async_remote_copy(
        src_ref=src, dst_ref=dst, send_sem=ssem, recv_sem=rsem, device_id=dev, device_id_type=MESH
    )


def push(src, dst, ssem, rsem, dev, same):
    @pl.when(same)
    def _():
        pltpu.make_async_copy(src, dst, rsem).start()

    @pl.when(jnp.logical_not(same))
    def _():
        remote(src, dst, ssem, rsem, dev).start()


def pushed(src, dst, ssem, rsem, dev, same):
    @pl.when(jnp.logical_not(same))
    def _():
        remote(src, dst, ssem, rsem, dev).wait_send()


def got(dst, ssem, rsem, dev):
    remote(dst, dst, ssem, rsem, dev).wait_recv()


def greet(peers):
    barrier = pltpu.get_barrier_semaphore()
    for dev in peers:
        pl.semaphore_signal(barrier, inc=1, device_id=dev, device_id_type=MESH)
    pl.semaphore_wait(barrier, len(peers))


def column_peers(p, mp):
    peers = []
    for k in range(1, mp):
        z = lax.rem(p.m + k, mp)
        peers += [(p.base, z), (p.base + 1, z)]
    return peers


class Gather:
    def __init__(self, p, src, dst, sems, mp):
        self.p, self.src, self.dst, self.mp = p, src, dst, mp
        self.zs, self.zr, self.xs, self.xr, self.ys, self.yr = sems
        self.n = src.shape[0]

    def rows(self, a, first, count):
        return self.dst.at[a, pl.ds(first * self.n, count * self.n), :]

    def z_args(self, k):
        p = self.p
        z = lax.rem(p.m + k, self.mp)
        same = (p.h == p.c) if k == 0 else None
        return (self.src, self.rows(p.a, p.d, 1), self.zs.at[k], self.zr.at[2 * p.c + p.a], (p.base + p.h, z)), same

    def z_send(self):
        for k in (2, 1, 3, 0):
            args, same = self.z_args(k)
            if same is None:
                remote(*args).start()
            else:
                push(*args, same)

    def z_recv(self):
        p = self.p
        for core in range(2):
            for a in range(2):
                got(self.rows(a, p.base + core, 1), self.zs.at[0], self.zr.at[2 * core + a], (p.d, p.m))

    def hop(self, axis, step, a):
        p = self.p
        peer = p.xp if axis == 0 else p.yp
        first = p.base if step == 0 else (p.by if axis == 0 else p.bx)
        part = self.rows(a, first, 2)
        s, r = (self.xs, self.xr) if axis == 0 else (self.ys, self.yr)
        i = 2 if step else a
        return remote(part, part, s.at[i], r.at[i], (peer, p.m))

    def xy_send(self):
        for a in range(2):
            self.hop(0, 0, a).start()
            self.hop(1, 0, 1 - a).start()

    def arrived(self, axis, step, a):
        p = self.p
        first = (p.bx if axis == 0 else p.by) if step == 0 else p.bd
        s, r = (self.xs, self.xr) if axis == 0 else (self.ys, self.yr)
        i = 2 if step else a
        got(self.rows(a, first, 2), s.at[i], r.at[i], (p.d, p.m))

    def forward(self):
        self.arrived(0, 0, 0)
        self.hop(1, 1, 0).start()
        self.arrived(1, 0, 1)
        self.hop(0, 1, 1).start()

    def finish(self):
        self.arrived(0, 0, 1)
        self.arrived(1, 0, 0)
        self.arrived(1, 1, 0)
        self.arrived(0, 1, 1)
        for k in range(self.mp):
            args, same = self.z_args(k)
            if same is None:
                remote(*args).wait_send()
            else:
                pushed(*args, same)
        for a in range(2):
            self.hop(0, 0, a).wait_send()
            self.hop(1, 0, a).wait_send()
        self.hop(1, 1, 0).wait_send()
        self.hop(0, 1, 1).wait_send()


def gather_sems(mp):
    return [DMA((mp,)), DMA((4,)), DMA((3,)), DMA((3,)), DMA((3,)), DMA((3,))]


class Tokens:
    def __init__(self, p, tok, x, sems):
        self.p, self.tok, self.x = p, tok, x
        self.s, self.r, self.fs, self.fr = sems
        self.piece = tok.shape[1] // 2

    def args(self, i, half):
        p, n = self.p, self.piece
        z = 2 * p.c + i
        dev = (p.base + half, z)
        dst = self.x.at[pl.ds((2 * p.m + half) * n, n), :]
        src = self.tok.at[i, pl.ds(half * n, n), :]
        return (src, dst, self.s.at[2 * i + half], self.r.at[p.m], dev), jnp.logical_and(p.c == half, p.m == z)

    def send(self):
        for i in range(2):
            for half in range(2):
                args, same = self.args(i, half)
                push(*args, same)

    def part(self, q, core):
        return self.x.at[pl.ds((2 * q + core) * self.piece, self.piece), :]

    def forward(self, mp):
        p = self.p
        for q in range(mp):
            got(self.part(q, p.c), self.s.at[0], self.r.at[q], (p.d, p.m))
            remote(self.part(q, p.c), self.part(q, p.c), self.fs.at[q], self.fr.at[q], (p.sib, p.m)).start()

    def finish(self, mp):
        p = self.p
        for q in range(mp):
            got(self.part(q, 1 - p.c), self.fs.at[q], self.fr.at[q], (p.d, p.m))
            remote(self.part(q, p.c), self.part(q, p.c), self.fs.at[q], self.fr.at[q], (p.sib, p.m)).wait_send()
        for i in range(2):
            for half in range(2):
                args, same = self.args(i, half)
                pushed(*args, same)


class Quarters:
    def __init__(self, p, src, dst, sems):
        self.p, self.src, self.dst = p, src, dst
        self.s, self.r = sems
        self.n = src.shape[1]

    def args(self, i):
        p = self.p
        z = 2 * p.c + i
        dst = self.dst.at[pl.ds(p.a * self.n, self.n), :]
        same = jnp.logical_and(p.h == p.c, p.m == z)
        return (self.src.at[i], dst, self.s.at[i], self.r.at[p.a], (p.base + p.h, z)), same

    def send(self):
        for i in range(2):
            args, same = self.args(i)
            push(*args, same)

    def finish(self):
        p = self.p
        for a in range(2):
            got(self.dst.at[pl.ds(a * self.n, self.n), :], self.s.at[a], self.r.at[a], (p.d, p.m))
        for i in range(2):
            args, same = self.args(i)
            pushed(*args, same)


class Homewards:
    def __init__(self, p, src, dst, sems):
        self.p, self.src, self.dst = p, src, dst
        self.s, self.r = sems
        self.n = dst.shape[1]

    def args(self, q):
        p = self.p
        src = self.src.at[pl.ds(q * self.n, self.n), :]
        owner = p.base + p.h
        same = jnp.logical_and(owner == p.d, p.m == 2 * p.c + q)
        return (src, self.dst.at[p.a], self.s.at[q], self.r.at[p.a], (owner, 2 * p.c + q)), same

    def send(self):
        for q in range(2):
            args, same = self.args(q)
            push(*args, same)

    def finish(self):
        p = self.p
        for i in range(2):
            got(self.dst.at[i], self.s.at[i], self.r.at[i], (p.d, p.m))
        for q in range(2):
            args, same = self.args(q)
            pushed(*args, same)


class Scatter:
    def __init__(self, p, src, out, bufs, sems, mp):
        self.p, self.src, self.out, self.mp = p, src, out, mp
        self.r1, self.r2, self.r3, self.total = bufs
        self.xs, self.xr, self.ys, self.yr, self.zs, self.zr = sems
        self.n = out.shape[1]

    def rows(self, a, first):
        return self.src.at[a, pl.ds(first * self.n, 2 * self.n), :]

    def hop(self, kind, axis):
        p = self.p
        peer = p.xp if axis == 0 else p.yp
        s, r = (self.xs, self.xr) if axis == 0 else (self.ys, self.yr)
        if kind == 0:
            a = 1 if axis == 0 else 0
            src, dst = self.rows(a, p.bd), self.r1.at[axis]
        elif kind == 1:
            a = 1 if axis == 0 else 0
            src, dst = self.rows(a, p.bx if axis == 0 else p.by), self.r2.at[axis]
        else:
            src, dst = self.r1.at[1 - axis], self.r3.at[axis]
        return remote(src, dst, s.at[kind], r.at[kind], (peer, p.m))

    def first(self):
        for axis in range(2):
            self.hop(0, axis).start()
        for axis in range(2):
            self.hop(1, axis).start()

    def second(self):
        p = self.p
        for axis in range(2):
            other = 1 - axis
            self.hop(0, axis).wait_recv()
            a = 1 if axis == 0 else 0
            rows = pl.ds((p.by if axis == 0 else p.bx) * self.n, 2 * self.n)
            self.r1[axis] = (self.src[a, rows, :].astype(F32) + self.r1[axis].astype(F32)).astype(BF16)
            self.hop(2, other).start()

    def third(self):
        p = self.p
        rows = pl.ds(p.base * self.n, 2 * self.n)
        for axis in range(2):
            self.hop(1, axis).wait_recv()
            self.hop(2, axis).wait_recv()
        for a in range(2):
            self.total[a] = (
                self.src[a, rows, :].astype(F32)
                + self.r2[1 - a].astype(F32)
                + self.r3[a].astype(F32)
            ).astype(BF16)
        for a in range(2):
            for core in range(2):
                args, same = self.z_args(a, core)
                push(*args, same)

    def z_args(self, a, core):
        p = self.p
        i = 2 * a + core
        owner = (p.base + core, 2 * p.c + a)
        same = jnp.logical_and(p.c == core, p.m == 2 * p.c + a)
        src = self.total.at[a, pl.ds(core * self.n, self.n), :]
        return (src, self.out.at[p.m], self.zs.at[i], self.zr.at[p.m], owner), same

    def finish(self):
        p = self.p
        for z in range(self.mp):
            got(self.out.at[z], self.zs.at[0], self.zr.at[z], (p.d, p.m))
        for axis in range(2):
            for kind in range(3):
                self.hop(kind, axis).wait_send()
        for a in range(2):
            for core in range(2):
                args, same = self.z_args(a, core)
                pushed(*args, same)


def scatter_bufs(n, width):
    return [pltpu.VMEM((2, 2 * n, width), BF16)] * 4


def scatter_sems(mp):
    return [DMA((3,)), DMA((3,)), DMA((3,)), DMA((3,)), DMA((4,)), DMA((mp,))]


def fetch_kernel(mp, tok, cot, pa, pb, pc, vec, x, ct, ga, gb, gc, gvd, gvz, *sems):
    p = Place()
    vs, vr, us, ur = sems[:4]
    tokens = Tokens(p, tok, x, sems[4:8])
    cots = Quarters(p, cot, ct, sems[8:10])
    weights = [Gather(p, s, g, sems[10 + 6 * i : 16 + 6 * i], mp) for i, (s, g) in enumerate(((pa, ga), (pb, gb), (pc, gc)))]
    plane = [lax.rem(p.d + k, 8) for k in range(1, 8)]
    greet(column_peers(p, mp) + [(d, p.m) for d in plane])
    weights[0].z_send()
    tokens.send()
    vcopies = [remote(vec, gvd.at[p.d], vs.at[k], vr.at[p.d], (d, p.m)) for k, d in enumerate(plane)]
    ucopies = [remote(vec, gvz.at[p.m], us.at[k - 1], ur.at[p.m], (p.d, lax.rem(p.m + k, mp))) for k in range(1, mp)]
    own = [pltpu.make_async_copy(vec, gvd.at[p.d], vr.at[p.d]), pltpu.make_async_copy(vec, gvz.at[p.m], ur.at[p.m])]
    for copy in vcopies + ucopies + own:
        copy.start()
    weights[0].z_recv()
    weights[0].xy_send()
    weights[1].z_send()
    tokens.forward(mp)
    weights[0].forward()
    weights[1].z_recv()
    weights[1].xy_send()
    weights[2].z_send()
    cots.send()
    weights[1].forward()
    weights[2].z_recv()
    weights[2].xy_send()
    weights[2].forward()
    tokens.finish(mp)
    cots.finish()
    for w in weights:
        w.finish()
    for d in range(8):
        got(gvd.at[d], vs.at[0], vr.at[d], (p.d, p.m))
    for z in range(mp):
        got(gvz.at[z], us.at[0], ur.at[z], (p.d, p.m))
    for copy in vcopies + ucopies:
        copy.wait_send()


def fetch(mp, tok, cot, pa, pb, pc, vec):
    rows, width = pa.shape
    seq = tok.shape[1] * mp
    shape = jax.ShapeDtypeStruct
    gathered = shape((2, 8 * rows, width), BF16)
    return pl.pallas_call(
        lambda *refs: fetch_kernel(mp, *refs),
        name="fetch",
        out_shape=[
            shape((seq, tok.shape[2]), BF16),
            shape((seq // 2, tok.shape[2]), BF16),
            gathered,
            gathered,
            gathered,
            shape((8,) + vec.shape, F32),
            shape((mp,) + vec.shape, F32),
        ],
        in_specs=[ANY] * 6,
        out_specs=[ANY] * 7,
        scratch_shapes=[
            DMA((7,)), DMA((8,)), DMA((mp - 1,)), DMA((mp,)),
            DMA((4,)), DMA((mp,)), DMA((mp,)), DMA((mp,)),
            DMA((2,)), DMA((2,)),
            *gather_sems(mp), *gather_sems(mp), *gather_sems(mp),
        ],
        compiler_params=pltpu.CompilerParams(collective_id=0, has_side_effects=True),
    )(tok, cot, pa, pb, pc, vec)


def deliver_kernel(mp, da, db, dc, out, gtok, ra, rb, rc, hout, hgtok, *scr):
    p = Place()
    weights = []
    for i, (s, o) in enumerate(((da, ra), (db, rb), (dc, rc))):
        weights.append(Scatter(p, s, o, scr[4 * i : 4 * i + 4], scr[12 + 6 * i : 18 + 6 * i], mp))
    home = Homewards(p, out, hout, scr[30:32])
    home_g = Homewards(p, gtok, hgtok, scr[32:34])
    greet(column_peers(p, mp) + [(p.sib, p.m), (p.xp, p.m), (p.yp, p.m)])
    home.send()
    home_g.send()
    for w in weights:
        w.first()
    for w in weights:
        w.second()
        w.third()
    for w in weights:
        w.finish()
    home.finish()
    home_g.finish()


def deliver(mp, da, db, dc, out, gtok, rows, quarter):
    width = da.shape[2]
    shape = jax.ShapeDtypeStruct
    part = shape((mp, rows, width), BF16)
    piece = shape((2, quarter, out.shape[1]), BF16)
    return pl.pallas_call(
        lambda *refs: deliver_kernel(mp, *refs),
        name="deliver",
        out_shape=[part, part, part, piece, piece],
        in_specs=[VMEM] * 3 + [ANY] * 2,
        out_specs=[ANY] * 5,
        scratch_shapes=[
            *scatter_bufs(rows, width), *scatter_bufs(rows, width), *scatter_bufs(rows, width),
            *scatter_sems(mp), *scatter_sems(mp), *scatter_sems(mp),
            DMA((2,)), DMA((2,)), DMA((2,)), DMA((2,)),
        ],
        compiler_params=pltpu.CompilerParams(collective_id=1, has_side_effects=True, vmem_limit_bytes=48 << 20),
    )(da, db, dc, out, gtok)


def attend_kernel(q_ref, k_ref, v_ref, bias_ref, hot_ref, ctx_ref, lse_ref, qa, ka):
    seq = q_ref.shape[2]
    head = q_ref.shape[1]
    scale = 1.0 / math.sqrt(head)
    blocks = bias_ref.shape[2]
    step = min(256, seq)
    qa[0:head, :] = (q_ref[0].astype(F32) * scale).astype(BF16)
    qa[head : head + blocks, :] = bias_ref[0, 0]
    low = lax.broadcasted_iota(jnp.int32, (qa.shape[0] - head - blocks, seq), 0)
    qa[head + blocks :, :] = jnp.where(low == 0, NEG, 0.0).astype(BF16)
    ka[0:head, :] = k_ref[0]
    ka[head:, :] = hot_ref[...]
    for i in range(seq // step):
        cols = slice(i * step, (i + 1) * step)
        scores = lax.dot_general(ka[...], qa[:, cols], (((0,), (0,)), ((), ())), preferred_element_type=F32)
        peak = jnp.max(scores, 0, keepdims=True)
        weights = jnp.exp(scores - peak)
        total = jnp.sum(weights, 0, keepdims=True)
        mixed = jnp.dot(v_ref[0], weights.astype(BF16), preferred_element_type=F32)
        ctx_ref[0, :, cols] = (mixed / total).astype(BF16)
        lse_ref[0, 0, :, cols] = peak + jnp.log(total)


def head_specs(head, seq, per, blocks, hot_rows):
    row = lambda part: pl.BlockSpec((1, head, seq), lambda m, h: (m, part * per + h, 0))
    return (
        [row(0), row(1), row(2)],
        pl.BlockSpec((1, 1, blocks, seq), lambda m, h: (m, h, 0, 0)),
        pl.BlockSpec((hot_rows, seq), lambda m, h: (0, 0)),
        pl.BlockSpec((1, 1, 1, seq), lambda m, h: (m, h, 0, 0)),
        row(0),
    )


def attend(qkv, bias, hot, head):
    groups, width, seq = qkv.shape
    per = width // (3 * head)
    rows, bias_spec, hot_spec, line, out = head_specs(head, seq, per, bias.shape[2], hot.shape[0])
    deep = head + hot.shape[0]
    return pl.pallas_call(
        attend_kernel,
        name="attend",
        grid=(groups, per),
        out_shape=[
            jax.ShapeDtypeStruct((groups, per * head, seq), BF16),
            jax.ShapeDtypeStruct((groups, per, 1, seq), F32),
        ],
        in_specs=rows + [bias_spec, hot_spec],
        out_specs=[out, line],
        scratch_shapes=[pltpu.VMEM((deep, seq), BF16), pltpu.VMEM((deep, seq), BF16)],
        compiler_params=pltpu.CompilerParams(vmem_limit_bytes=48 << 20),
    )(qkv, qkv, qkv, bias, hot)


def attend_back_kernel(q_ref, k_ref, v_ref, bias_ref, hot_ref, lse_ref, g_ref, dq_ref, dk_ref, dv_ref, qa, ka, ak, av):
    seq = q_ref.shape[2]
    head = q_ref.shape[1]
    scale = 1.0 / math.sqrt(head)
    blocks = bias_ref.shape[2]
    step = min(256, seq)
    qa[0:head, :] = (q_ref[0].astype(F32) * scale).astype(BF16)
    qa[head : head + blocks, :] = bias_ref[0, 0]
    low = lax.broadcasted_iota(jnp.int32, (qa.shape[0] - head - blocks, seq), 0)
    qa[head + blocks :, :] = jnp.where(low == 0, NEG, 0.0).astype(BF16)
    ka[0:head, :] = k_ref[0]
    ka[head:, :] = hot_ref[...]
    for i in range(seq // step):
        cols = slice(i * step, (i + 1) * step)
        scores = lax.dot_general(ka[...], qa[:, cols], (((0,), (0,)), ((), ())), preferred_element_type=F32)
        probs = jnp.exp(scores - lse_ref[0, 0, :, cols])
        grad = g_ref[0, :, cols]
        grad_probs = lax.dot_general(v_ref[0], grad, (((0,), (0,)), ((), ())), preferred_element_type=F32)
        inner = jnp.sum(probs * grad_probs, 0, keepdims=True)
        grad_scores = (probs * (grad_probs - inner)).astype(BF16)
        dq_ref[0, :, cols] = (jnp.dot(k_ref[0], grad_scores, preferred_element_type=F32) * scale).astype(BF16)
        gk = lax.dot_general(qa[0:head, cols], grad_scores, (((1,), (1,)), ((), ())), preferred_element_type=F32)
        gv = lax.dot_general(grad, probs.astype(BF16), (((1,), (1,)), ((), ())), preferred_element_type=F32)
        if i == 0:
            ak[...] = gk
            av[...] = gv
        else:
            ak[...] += gk
            av[...] += gv
    dk_ref[0] = ak[...].astype(BF16)
    dv_ref[0] = av[...].astype(BF16)


def attend_back(qkv, bias, hot, lse, grad, head):
    groups, width, seq = qkv.shape
    per = width // (3 * head)
    rows, bias_spec, hot_spec, line, out = head_specs(head, seq, per, bias.shape[2], hot.shape[0])
    deep = head + hot.shape[0]
    return pl.pallas_call(
        attend_back_kernel,
        name="attend_back",
        grid=(groups, per),
        out_shape=[jax.ShapeDtypeStruct((groups, per * head, seq), BF16)] * 3,
        in_specs=rows + [bias_spec, hot_spec, line, out],
        out_specs=[out] * 3,
        scratch_shapes=[
            pltpu.VMEM((deep, seq), BF16),
            pltpu.VMEM((deep, seq), BF16),
            pltpu.VMEM((head, seq), F32),
            pltpu.VMEM((head, seq), F32),
        ],
        compiler_params=pltpu.CompilerParams(vmem_limit_bytes=48 << 20),
    )(qkv, qkv, qkv, bias, hot, lse, grad)


def fetch_plain(dp, mp, tok, cot, pa, pb, pc, vec):
    d, m = lax.axis_index("dp"), lax.axis_index("mp")
    core = d % 2
    swap = [(i, i ^ 1) for i in range(dp)]

    def sequence(rows):
        whole = lax.all_gather(rows, "mp", axis=1, tiled=True)
        other = lax.ppermute(whole, "dp", swap)
        return jnp.where(m // 2 == core, whole, other)[m % 2]

    def weight(part):
        plane = lax.all_gather(part, "dp", axis=0, tiled=True)
        return lax.dynamic_slice_in_dim(lax.all_gather(plane, "mp"), 2 * core, 2, 0)

    half = tok.shape[1] * mp // 2
    ct = lax.dynamic_slice_in_dim(sequence(cot), core * half, half, 0)
    return (
        sequence(tok), ct, weight(pa), weight(pb), weight(pc), lax.all_gather(vec, "dp"), lax.all_gather(vec, "mp"),
    )


def deliver_plain(dp, mp, da, db, dc, out, gtok, rows, quarter):
    d, m = lax.axis_index("dp"), lax.axis_index("mp")
    core = d % 2
    swap = [(i, i ^ 1) for i in range(dp)]

    def grad(part):
        wide = jnp.zeros((mp,) + part.shape[1:], F32)
        wide = lax.dynamic_update_slice_in_dim(wide, part.astype(F32), 2 * core, 0)
        mine = lax.psum_scatter(wide, "mp", scatter_dimension=0, tiled=True)[0]
        return lax.psum_scatter(mine, "dp", scatter_dimension=0, tiled=True)[None]

    def home(half):
        both = jnp.zeros((2,) + half.shape, half.dtype)
        both = lax.dynamic_update_slice_in_dim(both, half[None], core, 0)
        both = lax.dynamic_update_slice_in_dim(both, lax.ppermute(half, "dp", swap)[None], 1 - core, 0)
        all_rows = lax.all_gather(both.reshape(mp, quarter, -1), "mp")
        mine = lax.dynamic_slice_in_dim(all_rows, 2 * core, 2, 0)
        return lax.dynamic_slice_in_dim(mine, m, 1, 1)[:, 0]

    return grad(da), grad(db), grad(dc), home(out), home(gtok)


def layer(
    dp, mp, tokens, cotangent, w_query, w_key, w_value, w_out, w_inner, w_outer,
    gain_attn, shift_attn, gain_ffn, shift_ffn, seq_lengths, rand_blocks,
):
    d, m = lax.axis_index("dp"), lax.axis_index("mp")
    core = d % 2
    swap = [(i, i ^ 1) for i in range(dp)]
    quarter, width = tokens.shape[1:]
    seq = quarter * mp
    half = seq // 2
    per, nblocks, picks = rand_blocks.shape
    cols = w_query.shape[1]
    head = cols // per
    block = seq // nblocks
    rows = w_query.shape[0]
    vec_rows = [v.astype(F32) for v in (gain_attn, shift_attn, gain_ffn, shift_ffn)]
    vec_rows += [seq_lengths.astype(F32)]
    flat = rand_blocks.astype(F32).reshape(-1)
    vec_rows += [flat[:128], flat[128:]]
    vec = jnp.stack([jnp.pad(v, (0, 128 - v.shape[0])) for v in vec_rows] + [jnp.zeros(128, F32)])
    pa = jnp.concatenate([w_query, w_key, w_value, w_out.T], 1)
    kernels = dp == 8 and mp == 4 and rows % 16 == 0 and pa.shape[1] % 128 == 0
    sizes = (mp,) if kernels else (dp, mp)
    x, ct, ga, gb, gc, gvd, gvz = (fetch if kernels else fetch_plain)(
        *sizes, tokens, cotangent, pa, w_inner, w_outer.T, vec
    )
    norms = jnp.swapaxes(gvd[:, :4, :rows], 0, 1).reshape(4, width)
    g1, b1, g2, b2 = (norms[i][None] for i in range(4))
    owner = d - core + m // 2
    lens = lax.dynamic_slice_in_dim(gvd[:, 4, :2], owner, 1, 0)[0]
    length = jnp.where(m % 2 == 0, lens[0], lens[1]).astype(jnp.int32)
    picked = lax.dynamic_slice_in_dim(gvz, 2 * core, 2, 0)
    picked = picked[:, 5:7].reshape(2, 256)[:, : per * nblocks * picks].astype(jnp.int32)
    picked = picked.reshape(2, per, nblocks, picks)

    r = jnp.arange(nblocks)
    near = (r[:, None] == 0) | (r[:, None] == nblocks - 1) | (r[None] == 0) | (r[None] == nblocks - 1)
    near = near | (jnp.abs(r[:, None] - r[None]) <= 1)
    hits = jnp.any(picked[:, :, :, :, None] == r, axis=3) | near
    bias = jnp.where(jnp.swapaxes(hits, 2, 3), 0.0, NEG).astype(BF16)
    bias = jnp.repeat(bias, block, axis=3)
    pos = jnp.arange(seq)
    hot = jnp.concatenate([pos[None] // block == r[:, None], pos[None] >= length, jnp.zeros((15, seq), bool)], 0)
    hot = hot.astype(BF16)

    def mine(values):
        return lax.dynamic_slice_in_dim(values, core * half, half, 0)

    def theirs(values):
        return lax.dynamic_slice_in_dim(values, (1 - core) * half, half, 0)

    def pair_sum(partial):
        return mine(partial) + lax.ppermute(theirs(partial).astype(BF16), "dp", swap).astype(F32)

    def pair_join(values):
        other = lax.ppermute(values, "dp", swap)
        lo = jnp.where(core == 0, values, other)
        hi = jnp.where(core == 0, other, values)
        return jnp.concatenate([lo, hi], 0)

    def dot(spec, a, b):
        return jnp.einsum(spec, a, b, preferred_element_type=F32)

    a_qkv, a_out = ga[:, :, : 3 * cols], ga[:, :, 3 * cols :]
    qkv = dot("mrc,tr->mct", a_qkv, x).astype(BF16)
    ctx, lse = attend(qkv, bias, hot, head)
    attn = pair_sum(dot("mct,mdc->td", ctx, a_out))
    x_mine = mine(x).astype(F32)

    def norm(z):
        centre = z - jnp.mean(z, -1, keepdims=True)
        inv = lax.rsqrt(jnp.mean(centre * centre, -1, keepdims=True) + EPS)
        return centre * inv, inv

    n1, inv1 = norm(x_mine + attn)
    hidden = n1 * g1 + b1
    hidden_b = pair_join(hidden.astype(BF16))
    inner = dot("td,mdk->tmk", hidden_b, gb)
    cumul = 0.5 * (1.0 + lax.erf(inner * (1.0 / math.sqrt(2.0))))
    active = (inner * cumul).astype(BF16)
    slope = cumul + inner * jnp.exp(-0.5 * inner * inner) * (1.0 / math.sqrt(2.0 * math.pi))
    n2, inv2 = norm(hidden + pair_sum(dot("tmk,mdk->td", active, gc)))
    valid = (core * half + jnp.arange(half) < length).astype(F32)[:, None]
    out = ((n2 * g2 + b2) * valid).astype(BF16)

    def norm_back(e, n, inv):
        return (e - jnp.mean(e, -1, keepdims=True) - n * jnp.mean(e * n, -1, keepdims=True)) * inv

    gy = ct.astype(F32) * valid
    g_mid = norm_back(gy * g2, n2, inv2)
    d_gain2, d_shift2 = jnp.sum(gy * n2, 0), jnp.sum(gy, 0)
    g_ffn = pair_join(g_mid.astype(BF16))
    d_c = dot("td,tmk->mdk", g_ffn, active).astype(BF16)
    g_inner = (dot("td,mdk->tmk", g_ffn, gc) * slope).astype(BF16)
    d_b = dot("td,tmk->mdk", hidden_b, g_inner).astype(BF16)
    g_hidden = g_mid + pair_sum(dot("tmk,mdk->td", g_inner, gb))
    d_gain1, d_shift1 = jnp.sum(g_hidden * n1, 0), jnp.sum(g_hidden, 0)
    g_res = norm_back(g_hidden * g1, n1, inv1)
    g_attn = pair_join(g_res.astype(BF16))
    d_out = dot("td,mct->mdc", g_attn, ctx).astype(BF16)
    g_ctx = dot("td,mdc->mct", g_attn, a_out).astype(BF16)
    dq, dk, dv = attend_back(qkv, bias, hot, lse, g_ctx, head)
    dqkv = jnp.concatenate([dq, dk, dv], 1)
    d_qkv = dot("tr,mct->mrc", x, dqkv).astype(BF16)
    d_a = jnp.concatenate([d_qkv, d_out], 2)
    gtok = (g_res + pair_sum(dot("mct,mrc->tr", dqkv, a_qkv))).astype(BF16)
    ra, rb, rc, out, gtok = (deliver if kernels else deliver_plain)(*sizes, d_a, d_b, d_c, out, gtok, rows, quarter)
    ra, rb, rc = (jnp.sum(v.astype(F32), 0) for v in (ra, rb, rc))
    sums = lax.psum(jnp.stack([d_gain1, d_shift1, d_gain2, d_shift2]), ("dp", "mp"))
    sums = lax.dynamic_slice_in_dim(sums, d * rows, rows, 1)
    return (
        out, gtok, ra[:, :cols], ra[:, cols : 2 * cols], ra[:, 2 * cols : 3 * cols], ra[:, 3 * cols :].T, rb, rc.T,
        sums[0], sums[1], sums[2], sums[3],
    )


def solution(mesh):
    dp, mp = mesh.shape["dp"], mesh.shape["mp"]
    act, vec = P("dp", "mp", None), P("dp")
    w_in, w_back = P("dp", "mp"), P("mp", "dp")

    def step(*args):
        return layer(dp, mp, *args)

    return jax.shard_map(
        step,
        mesh=mesh,
        in_specs=(act, act, w_in, w_in, w_in, w_back, w_in, w_back, vec, vec, vec, vec, vec, P("mp", None, None)),
        out_specs=(act, act, w_in, w_in, w_in, w_back, w_in, w_back, vec, vec, vec, vec),
        check_vma=False,
    )
```

```python
import math

import jax
import jax.numpy as jnp
from jax import lax
from jax.experimental import pallas as pl
from jax.experimental.pallas import tpu as pltpu
from jax.sharding import PartitionSpec as P

EPS = 1e-06
NEG = -1000000000.0
MESH = pl.DeviceIdType.MESH
F32 = jnp.float32
BF16 = jnp.bfloat16
ANY = pl.BlockSpec(memory_space=pl.ANY)
VMEM = pl.BlockSpec(memory_space=pltpu.VMEM)
DMA = pltpu.SemaphoreType.DMA


class Place:
    def __init__(self):
        self.d = lax.axis_index("dp")
        self.m = lax.axis_index("mp")
        self.c = lax.rem(self.d, 2)
        self.base = self.d - self.c
        self.sib = self.d + 1 - 2 * self.c
        bx = lax.rem(lax.div(self.d, 2), 2)
        by = lax.rem(lax.div(self.d, 4), 2)
        self.xp = self.d + 2 - 4 * bx
        self.yp = self.d + 4 - 8 * by
        self.bx = self.xp - self.c
        self.by = self.yp - self.c
        self.bd = self.bx + 4 - 8 * by
        self.h = lax.div(self.m, 2)
        self.a = lax.rem(self.m, 2)


def remote(src, dst, ssem, rsem, dev):
    return pltpu.make_async_remote_copy(
        src_ref=src, dst_ref=dst, send_sem=ssem, recv_sem=rsem, device_id=dev, device_id_type=MESH
    )


def push(src, dst, ssem, rsem, dev, same):
    @pl.when(same)
    def _():
        pltpu.make_async_copy(src, dst, rsem).start()

    @pl.when(jnp.logical_not(same))
    def _():
        remote(src, dst, ssem, rsem, dev).start()


def pushed(src, dst, ssem, rsem, dev, same):
    @pl.when(jnp.logical_not(same))
    def _():
        remote(src, dst, ssem, rsem, dev).wait_send()


def got(dst, ssem, rsem, dev):
    remote(dst, dst, ssem, rsem, dev).wait_recv()


def greet(peers):
    barrier = pltpu.get_barrier_semaphore()
    for dev in peers:
        pl.semaphore_signal(barrier, inc=1, device_id=dev, device_id_type=MESH)
    pl.semaphore_wait(barrier, len(peers))


def column_peers(p, mp):
    peers = []
    for k in range(1, mp):
        z = lax.rem(p.m + k, mp)
        peers += [(p.base, z), (p.base + 1, z)]
    return peers


class Gather:
    def __init__(self, p, src, dst, sems, mp):
        self.p, self.src, self.dst, self.mp = p, src, dst, mp
        self.zs, self.zr, self.xs, self.xr, self.ys, self.yr = sems
        self.n = src.shape[0]

    def rows(self, a, first, count):
        return self.dst.at[a, pl.ds(first * self.n, count * self.n), :]

    def z_args(self, k):
        p = self.p
        z = lax.rem(p.m + k, self.mp)
        same = (p.h == p.c) if k == 0 else None
        return (self.src, self.rows(p.a, p.d, 1), self.zs.at[k], self.zr.at[2 * p.c + p.a], (p.base + p.h, z)), same

    def z_send(self):
        for k in (2, 1, 3, 0):
            args, same = self.z_args(k)
            if same is None:
                remote(*args).start()
            else:
                push(*args, same)

    def z_recv(self):
        p = self.p
        for core in range(2):
            for a in range(2):
                got(self.rows(a, p.base + core, 1), self.zs.at[0], self.zr.at[2 * core + a], (p.d, p.m))

    def hop(self, axis, step, a):
        p = self.p
        peer = p.xp if axis == 0 else p.yp
        first = p.base if step == 0 else (p.by if axis == 0 else p.bx)
        part = self.rows(a, first, 2)
        s, r = (self.xs, self.xr) if axis == 0 else (self.ys, self.yr)
        i = 2 if step else a
        return remote(part, part, s.at[i], r.at[i], (peer, p.m))

    def xy_send(self):
        for a in range(2):
            self.hop(0, 0, a).start()
            self.hop(1, 0, 1 - a).start()

    def arrived(self, axis, step, a):
        p = self.p
        first = (p.bx if axis == 0 else p.by) if step == 0 else p.bd
        s, r = (self.xs, self.xr) if axis == 0 else (self.ys, self.yr)
        i = 2 if step else a
        got(self.rows(a, first, 2), s.at[i], r.at[i], (p.d, p.m))

    def forward(self):
        self.arrived(0, 0, 0)
        self.hop(1, 1, 0).start()
        self.arrived(1, 0, 1)
        self.hop(0, 1, 1).start()

    def finish(self):
        self.arrived(0, 0, 1)
        self.arrived(1, 0, 0)
        self.arrived(1, 1, 0)
        self.arrived(0, 1, 1)
        for k in range(self.mp):
            args, same = self.z_args(k)
            if same is None:
                remote(*args).wait_send()
            else:
                pushed(*args, same)
        for a in range(2):
            self.hop(0, 0, a).wait_send()
            self.hop(1, 0, a).wait_send()
        self.hop(1, 1, 0).wait_send()
        self.hop(0, 1, 1).wait_send()


def gather_sems(mp):
    return [DMA((mp,)), DMA((4,)), DMA((3,)), DMA((3,)), DMA((3,)), DMA((3,))]


class Tokens:
    def __init__(self, p, tok, x, sems):
        self.p, self.tok, self.x = p, tok, x
        self.s, self.r, self.fs, self.fr = sems
        self.piece = tok.shape[1] // 2

    def args(self, i, half):
        p, n = self.p, self.piece
        z = 2 * p.c + i
        dev = (p.base + half, z)
        dst = self.x.at[pl.ds((2 * p.m + half) * n, n), :]
        src = self.tok.at[i, pl.ds(half * n, n), :]
        return (src, dst, self.s.at[2 * i + half], self.r.at[p.m], dev), jnp.logical_and(p.c == half, p.m == z)

    def send(self):
        for i in range(2):
            for half in range(2):
                args, same = self.args(i, half)
                push(*args, same)

    def part(self, q, core):
        return self.x.at[pl.ds((2 * q + core) * self.piece, self.piece), :]

    def forward(self, mp):
        p = self.p
        for q in range(mp):
            got(self.part(q, p.c), self.s.at[0], self.r.at[q], (p.d, p.m))
            remote(self.part(q, p.c), self.part(q, p.c), self.fs.at[q], self.fr.at[q], (p.sib, p.m)).start()

    def finish(self, mp):
        p = self.p
        for q in range(mp):
            got(self.part(q, 1 - p.c), self.fs.at[q], self.fr.at[q], (p.d, p.m))
            remote(self.part(q, p.c), self.part(q, p.c), self.fs.at[q], self.fr.at[q], (p.sib, p.m)).wait_send()
        for i in range(2):
            for half in range(2):
                args, same = self.args(i, half)
                pushed(*args, same)


class Quarters:
    def __init__(self, p, src, dst, sems):
        self.p, self.src, self.dst = p, src, dst
        self.s, self.r = sems
        self.n = src.shape[1]

    def args(self, i):
        p = self.p
        z = 2 * p.c + i
        dst = self.dst.at[pl.ds(p.a * self.n, self.n), :]
        same = jnp.logical_and(p.h == p.c, p.m == z)
        return (self.src.at[i], dst, self.s.at[i], self.r.at[p.a], (p.base + p.h, z)), same

    def send(self):
        for i in range(2):
            args, same = self.args(i)
            push(*args, same)

    def finish(self):
        p = self.p
        for a in range(2):
            got(self.dst.at[pl.ds(a * self.n, self.n), :], self.s.at[a], self.r.at[a], (p.d, p.m))
        for i in range(2):
            args, same = self.args(i)
            pushed(*args, same)


class Homewards:
    def __init__(self, p, src, dst, sems):
        self.p, self.src, self.dst = p, src, dst
        self.s, self.r = sems
        self.n = dst.shape[1]

    def args(self, q):
        p = self.p
        src = self.src.at[pl.ds(q * self.n, self.n), :]
        owner = p.base + p.h
        same = jnp.logical_and(owner == p.d, p.m == 2 * p.c + q)
        return (src, self.dst.at[p.a], self.s.at[q], self.r.at[p.a], (owner, 2 * p.c + q)), same

    def send(self):
        for q in range(2):
            args, same = self.args(q)
            push(*args, same)

    def finish(self):
        p = self.p
        for i in range(2):
            got(self.dst.at[i], self.s.at[i], self.r.at[i], (p.d, p.m))
        for q in range(2):
            args, same = self.args(q)
            pushed(*args, same)


class Scatter:
    def __init__(self, p, src, out, bufs, sems, mp):
        self.p, self.src, self.out, self.mp = p, src, out, mp
        self.r1, self.r2, self.r3, self.total = bufs
        self.xs, self.xr, self.ys, self.yr, self.zs, self.zr = sems
        self.n = out.shape[1]

    def rows(self, a, first):
        return self.src.at[a, pl.ds(first * self.n, 2 * self.n), :]

    def hop(self, kind, axis):
        p = self.p
        peer = p.xp if axis == 0 else p.yp
        s, r = (self.xs, self.xr) if axis == 0 else (self.ys, self.yr)
        if kind == 0:
            a = 1 if axis == 0 else 0
            src, dst = self.rows(a, p.bd), self.r1.at[axis]
        elif kind == 1:
            a = 1 if axis == 0 else 0
            src, dst = self.rows(a, p.bx if axis == 0 else p.by), self.r2.at[axis]
        else:
            src, dst = self.r1.at[1 - axis], self.r3.at[axis]
        return remote(src, dst, s.at[kind], r.at[kind], (peer, p.m))

    def first(self):
        for axis in range(2):
            self.hop(0, axis).start()
        for axis in range(2):
            self.hop(1, axis).start()

    def second(self):
        p = self.p
        for axis in range(2):
            other = 1 - axis
            self.hop(0, axis).wait_recv()
            a = 1 if axis == 0 else 0
            rows = pl.ds((p.by if axis == 0 else p.bx) * self.n, 2 * self.n)
            self.r1[axis] = (self.src[a, rows, :].astype(F32) + self.r1[axis].astype(F32)).astype(BF16)
            self.hop(2, other).start()

    def third(self):
        p = self.p
        rows = pl.ds(p.base * self.n, 2 * self.n)
        for axis in range(2):
            self.hop(1, axis).wait_recv()
            self.hop(2, axis).wait_recv()
        for a in range(2):
            self.total[a] = (
                self.src[a, rows, :].astype(F32)
                + self.r2[1 - a].astype(F32)
                + self.r3[a].astype(F32)
            ).astype(BF16)
        for a in range(2):
            for core in range(2):
                args, same = self.z_args(a, core)
                push(*args, same)

    def z_args(self, a, core):
        p = self.p
        i = 2 * a + core
        owner = (p.base + core, 2 * p.c + a)
        same = jnp.logical_and(p.c == core, p.m == 2 * p.c + a)
        src = self.total.at[a, pl.ds(core * self.n, self.n), :]
        return (src, self.out.at[p.m], self.zs.at[i], self.zr.at[p.m], owner), same

    def finish(self):
        p = self.p
        for z in range(self.mp):
            got(self.out.at[z], self.zs.at[0], self.zr.at[z], (p.d, p.m))
        for axis in range(2):
            for kind in range(3):
                self.hop(kind, axis).wait_send()
        for a in range(2):
            for core in range(2):
                args, same = self.z_args(a, core)
                pushed(*args, same)


def scatter_bufs(n, width):
    return [pltpu.VMEM((2, 2 * n, width), BF16)] * 4


def scatter_sems(mp):
    return [DMA((3,)), DMA((3,)), DMA((3,)), DMA((3,)), DMA((4,)), DMA((mp,))]


def fetch_kernel(mp, tok, pa, vec, x, ga, gvd, gvz, *sems):
    p = Place()
    vs, vr, us, ur = sems[:4]
    tokens = Tokens(p, tok, x, sems[4:8])
    weight = Gather(p, pa, ga, sems[8:14], mp)
    plane = [lax.rem(p.d + k, 8) for k in range(1, 8)]
    greet(column_peers(p, mp) + [(d, p.m) for d in plane])
    weight.z_send()
    tokens.send()
    vcopies = [remote(vec, gvd.at[p.d], vs.at[k], vr.at[p.d], (d, p.m)) for k, d in enumerate(plane)]
    ucopies = [remote(vec, gvz.at[p.m], us.at[k - 1], ur.at[p.m], (p.d, lax.rem(p.m + k, mp))) for k in range(1, mp)]
    own = [pltpu.make_async_copy(vec, gvd.at[p.d], vr.at[p.d]), pltpu.make_async_copy(vec, gvz.at[p.m], ur.at[p.m])]
    for copy in vcopies + ucopies + own:
        copy.start()
    weight.z_recv()
    weight.xy_send()
    tokens.forward(mp)
    weight.forward()
    tokens.finish(mp)
    weight.finish()
    for d in range(8):
        got(gvd.at[d], vs.at[0], vr.at[d], (p.d, p.m))
    for z in range(mp):
        got(gvz.at[z], us.at[0], ur.at[z], (p.d, p.m))
    for copy in vcopies + ucopies:
        copy.wait_send()


def fetch(mp, tok, pa, vec):
    rows, width = pa.shape
    shape = jax.ShapeDtypeStruct
    return pl.pallas_call(
        lambda *refs: fetch_kernel(mp, *refs),
        name="fetch",
        out_shape=[
            shape((tok.shape[1] * mp, tok.shape[2]), BF16),
            shape((2, 8 * rows, width), BF16),
            shape((8,) + vec.shape, F32),
            shape((mp,) + vec.shape, F32),
        ],
        in_specs=[ANY] * 3,
        out_specs=[ANY] * 4,
        scratch_shapes=[
            DMA((7,)), DMA((8,)), DMA((mp - 1,)), DMA((mp,)),
            DMA((4,)), DMA((mp,)), DMA((mp,)), DMA((mp,)),
            *gather_sems(mp),
        ],
        compiler_params=pltpu.CompilerParams(collective_id=0, has_side_effects=True),
    )(tok, pa, vec)


def deliver_kernel(mp, da, gtok, ra, hgtok, *scr):
    p = Place()
    weight = Scatter(p, da, ra, scr[0:4], scr[4:10], mp)
    home = Homewards(p, gtok, hgtok, scr[10:12])
    greet(column_peers(p, mp) + [(p.sib, p.m), (p.xp, p.m), (p.yp, p.m)])
    home.send()
    weight.first()
    weight.second()
    weight.third()
    weight.finish()
    home.finish()


def deliver(mp, da, gtok, rows, quarter):
    width = da.shape[2]
    shape = jax.ShapeDtypeStruct
    return pl.pallas_call(
        lambda *refs: deliver_kernel(mp, *refs),
        name="deliver",
        out_shape=[shape((mp, rows, width), BF16), shape((2, quarter, gtok.shape[1]), BF16)],
        in_specs=[VMEM, ANY],
        out_specs=[ANY] * 2,
        scratch_shapes=[*scatter_bufs(rows, width), *scatter_sems(mp), DMA((2,)), DMA((2,))],
        compiler_params=pltpu.CompilerParams(collective_id=1, has_side_effects=True, vmem_limit_bytes=48 << 20),
    )(da, gtok)


class Sums:
    def __init__(self, p, src, out, bufs, sems, mp):
        self.p, self.src, self.out, self.mp = p, src, out, mp
        self.mine, self.came, self.parts = bufs
        self.s, self.r, self.zs, self.zr = sems

    def hop(self, i):
        p = self.p
        dev = (p.sib, p.xp, p.yp)[i]
        return remote(self.mine.at[i], self.came.at[i], self.s.at[i], self.r.at[i], (dev, p.m))

    def start(self):
        self.mine[0] = self.src[...]
        self.hop(0).start()

    def step(self, i):
        self.hop(i).wait_recv()
        total = self.mine[i] + self.came[i]
        if i < 2:
            self.mine[i + 1] = total
            self.hop(i + 1).start()
        else:
            self.parts[self.p.m] = total
            for k in range(1, self.mp):
                self.column(k).start()

    def column(self, k):
        p = self.p
        part = self.parts.at[p.m]
        return remote(part, part, self.zs.at[k - 1], self.zr.at[p.m], (p.d, lax.rem(p.m + k, self.mp)))

    def finish(self):
        p = self.p
        for k in range(1, self.mp):
            z = lax.rem(p.m + k, self.mp)
            got(self.parts.at[z], self.zs.at[0], self.zr.at[z], (p.d, p.m))
        total = self.parts[0]
        for z in range(1, self.mp):
            total = total + self.parts[z]
        self.out[...] = total
        for i in range(3):
            self.hop(i).wait_send()
        for k in range(1, self.mp):
            self.column(k).wait_send()


def attend_kernel(q_ref, k_ref, v_ref, bias_ref, hot_ref, ctx_ref, lse_ref, qa, ka):
    seq = q_ref.shape[2]
    head = q_ref.shape[1]
    scale = 1.0 / math.sqrt(head)
    blocks = bias_ref.shape[2]
    step = min(256, seq)
    qa[0:head, :] = (q_ref[0].astype(F32) * scale).astype(BF16)
    qa[head : head + blocks, :] = bias_ref[0, 0]
    low = lax.broadcasted_iota(jnp.int32, (qa.shape[0] - head - blocks, seq), 0)
    qa[head + blocks :, :] = jnp.where(low == 0, NEG, 0.0).astype(BF16)
    ka[0:head, :] = k_ref[0]
    ka[head:, :] = hot_ref[...]
    for i in range(seq // step):
        cols = slice(i * step, (i + 1) * step)
        scores = lax.dot_general(ka[...], qa[:, cols], (((0,), (0,)), ((), ())), preferred_element_type=F32)
        peak = jnp.max(scores, 0, keepdims=True)
        weights = jnp.exp(scores - peak)
        total = jnp.sum(weights, 0, keepdims=True)
        mixed = jnp.dot(v_ref[0], weights.astype(BF16), preferred_element_type=F32)
        ctx_ref[0, :, cols] = (mixed / total).astype(BF16)
        lse_ref[0, 0, :, cols] = peak + jnp.log(total)


def head_specs(head, seq, per, blocks, hot_rows):
    row = lambda part: pl.BlockSpec((1, head, seq), lambda m, h: (m, part * per + h, 0))
    return (
        [row(0), row(1), row(2)],
        pl.BlockSpec((1, 1, blocks, seq), lambda m, h: (m, h, 0, 0)),
        pl.BlockSpec((hot_rows, seq), lambda m, h: (0, 0)),
        pl.BlockSpec((1, 1, 1, seq), lambda m, h: (m, h, 0, 0)),
        row(0),
    )


def attend_fetch_kernel(mp, q, k, v, bias, hot, pb, pc, cot, ctx, lse, gb, gc, ct, qa, ka, *sems):
    p = Place()
    step = pl.program_id(0) * pl.num_programs(1) + pl.program_id(1)
    last = pl.num_programs(0) * pl.num_programs(1) - 1
    first, second = (Gather(p, s, g, sems[6 * i : 6 * i + 6], mp) for i, (s, g) in enumerate(((pb, gb), (pc, gc))))
    cots = Quarters(p, cot, ct, sems[12:14])

    @pl.when(step == 0)
    def _():
        greet(column_peers(p, mp) + [(p.sib, p.m), (p.xp, p.m), (p.yp, p.m)])
        first.z_send()

    @pl.when(step == last - 1)
    def _():
        first.z_recv()
        first.xy_send()
        second.z_send()

    attend_kernel(q, k, v, bias, hot, ctx, lse, qa, ka)

    @pl.when(step == last)
    def _():
        first.forward()
        second.z_recv()
        second.xy_send()
        cots.send()
        second.forward()
        first.finish()
        second.finish()
        cots.finish()


def attend_fetch(mp, qkv, bias, hot, head, pb, pc, cot):
    groups, width, seq = qkv.shape
    per = width // (3 * head)
    rows, bias_spec, hot_spec, line, out = head_specs(head, seq, per, bias.shape[2], hot.shape[0])
    deep = head + hot.shape[0]
    shape = jax.ShapeDtypeStruct
    gathered = shape((2, 8 * pb.shape[0], pb.shape[1]), BF16)
    return pl.pallas_call(
        lambda *refs: attend_fetch_kernel(mp, *refs),
        name="attend_fetch",
        grid=(groups, per),
        out_shape=[
            shape((groups, per * head, seq), BF16),
            shape((groups, per, 1, seq), F32),
            gathered,
            gathered,
            shape((seq // 2, cot.shape[2]), BF16),
        ],
        in_specs=rows + [bias_spec, hot_spec] + [ANY] * 3,
        out_specs=[out, line] + [ANY] * 3,
        scratch_shapes=[
            pltpu.VMEM((deep, seq), BF16), pltpu.VMEM((deep, seq), BF16),
            *gather_sems(mp), *gather_sems(mp), DMA((2,)), DMA((2,)),
        ],
        compiler_params=pltpu.CompilerParams(collective_id=2, has_side_effects=True, vmem_limit_bytes=48 << 20),
    )(qkv, qkv, qkv, bias, hot, pb, pc, cot)


def attend(qkv, bias, hot, head):
    groups, width, seq = qkv.shape
    per = width // (3 * head)
    rows, bias_spec, hot_spec, line, out = head_specs(head, seq, per, bias.shape[2], hot.shape[0])
    deep = head + hot.shape[0]
    return pl.pallas_call(
        attend_kernel,
        name="attend",
        grid=(groups, per),
        out_shape=[
            jax.ShapeDtypeStruct((groups, per * head, seq), BF16),
            jax.ShapeDtypeStruct((groups, per, 1, seq), F32),
        ],
        in_specs=rows + [bias_spec, hot_spec],
        out_specs=[out, line],
        scratch_shapes=[pltpu.VMEM((deep, seq), BF16), pltpu.VMEM((deep, seq), BF16)],
        compiler_params=pltpu.CompilerParams(vmem_limit_bytes=48 << 20),
    )(qkv, qkv, qkv, bias, hot)


def attend_back_kernel(q_ref, k_ref, v_ref, bias_ref, hot_ref, lse_ref, g_ref, dq_ref, dk_ref, dv_ref, qa, ka, ak, av):
    seq = q_ref.shape[2]
    head = q_ref.shape[1]
    scale = 1.0 / math.sqrt(head)
    blocks = bias_ref.shape[2]
    step = min(256, seq)
    qa[0:head, :] = (q_ref[0].astype(F32) * scale).astype(BF16)
    qa[head : head + blocks, :] = bias_ref[0, 0]
    low = lax.broadcasted_iota(jnp.int32, (qa.shape[0] - head - blocks, seq), 0)
    qa[head + blocks :, :] = jnp.where(low == 0, NEG, 0.0).astype(BF16)
    ka[0:head, :] = k_ref[0]
    ka[head:, :] = hot_ref[...]
    for i in range(seq // step):
        cols = slice(i * step, (i + 1) * step)
        scores = lax.dot_general(ka[...], qa[:, cols], (((0,), (0,)), ((), ())), preferred_element_type=F32)
        probs = jnp.exp(scores - lse_ref[0, 0, :, cols])
        grad = g_ref[0, :, cols]
        grad_probs = lax.dot_general(v_ref[0], grad, (((0,), (0,)), ((), ())), preferred_element_type=F32)
        inner = jnp.sum(probs * grad_probs, 0, keepdims=True)
        grad_scores = (probs * (grad_probs - inner)).astype(BF16)
        dq_ref[0, :, cols] = (jnp.dot(k_ref[0], grad_scores, preferred_element_type=F32) * scale).astype(BF16)
        gk = lax.dot_general(qa[0:head, cols], grad_scores, (((1,), (1,)), ((), ())), preferred_element_type=F32)
        gv = lax.dot_general(grad, probs.astype(BF16), (((1,), (1,)), ((), ())), preferred_element_type=F32)
        if i == 0:
            ak[...] = gk
            av[...] = gv
        else:
            ak[...] += gk
            av[...] += gv
    dk_ref[0] = ak[...].astype(BF16)
    dv_ref[0] = av[...].astype(BF16)


def attend_deliver_kernel(
    mp, q, k, v, bias, hot, lse, g, db, dc, out, norm, dq, dk, dv, rb, rc, hout, sums, qa, ka, ak, av, *scr
):
    p = Place()
    step = pl.program_id(0) * pl.num_programs(1) + pl.program_id(1)
    last = pl.num_programs(0) * pl.num_programs(1) - 1
    early = Scatter(p, dc, rc, scr[0:4], scr[8:14], mp)
    late = Scatter(p, db, rb, scr[4:8], scr[14:20], mp)
    home = Homewards(p, out, hout, scr[20:22])
    small = Sums(p, norm, sums, scr[22:25], scr[25:29], mp)

    @pl.when(step == 0)
    def _():
        greet(column_peers(p, mp) + [(p.sib, p.m), (p.xp, p.m), (p.yp, p.m)])
        small.start()
        early.first()
        home.send()

    for i in range(3):

        @pl.when(step == i + 1)
        def _():
            small.step(i)

    @pl.when(step == last - 2)
    def _():
        early.second()
        late.first()

    @pl.when(step == last)
    def _():
        early.third()

    attend_back_kernel(q, k, v, bias, hot, lse, g, dq, dk, dv, qa, ka, ak, av)

    @pl.when(step == last)
    def _():
        late.second()
        late.third()
        small.finish()
        early.finish()
        late.finish()
        home.finish()


def attend_deliver(mp, qkv, bias, hot, lse, grad, head, db, dc, out_rows, norm, n, quarter):
    groups, width, seq = qkv.shape
    per = width // (3 * head)
    rows, bias_spec, hot_spec, line, out = head_specs(head, seq, per, bias.shape[2], hot.shape[0])
    deep = head + hot.shape[0]
    shape = jax.ShapeDtypeStruct
    part = shape((mp, n, db.shape[2]), BF16)
    return pl.pallas_call(
        lambda *refs: attend_deliver_kernel(mp, *refs),
        name="attend_deliver",
        grid=(groups, per),
        out_shape=[
            *[shape((groups, per * head, seq), BF16)] * 3,
            part,
            part,
            shape((2, quarter, out_rows.shape[1]), BF16),
            shape(norm.shape, F32),
        ],
        in_specs=rows + [bias_spec, hot_spec, line, out, VMEM, VMEM, ANY, VMEM],
        out_specs=[out] * 3 + [ANY] * 3 + [VMEM],
        scratch_shapes=[
            pltpu.VMEM((deep, seq), BF16), pltpu.VMEM((deep, seq), BF16),
            pltpu.VMEM((head, seq), F32), pltpu.VMEM((head, seq), F32),
            *scatter_bufs(n, db.shape[2]), *scatter_bufs(n, db.shape[2]),
            *scatter_sems(mp), *scatter_sems(mp), DMA((2,)), DMA((2,)),
            pltpu.VMEM((3,) + norm.shape, F32), pltpu.VMEM((3,) + norm.shape, F32), pltpu.VMEM((mp,) + norm.shape, F32),
            DMA((3,)), DMA((3,)), DMA((mp - 1,)), DMA((mp,)),
        ],
        compiler_params=pltpu.CompilerParams(collective_id=3, has_side_effects=True, vmem_limit_bytes=56 << 20),
    )(qkv, qkv, qkv, bias, hot, lse, grad, db, dc, out_rows, norm)


def attend_back(qkv, bias, hot, lse, grad, head):
    groups, width, seq = qkv.shape
    per = width // (3 * head)
    rows, bias_spec, hot_spec, line, out = head_specs(head, seq, per, bias.shape[2], hot.shape[0])
    deep = head + hot.shape[0]
    return pl.pallas_call(
        attend_back_kernel,
        name="attend_back",
        grid=(groups, per),
        out_shape=[jax.ShapeDtypeStruct((groups, per * head, seq), BF16)] * 3,
        in_specs=rows + [bias_spec, hot_spec, line, out],
        out_specs=[out] * 3,
        scratch_shapes=[
            pltpu.VMEM((deep, seq), BF16),
            pltpu.VMEM((deep, seq), BF16),
            pltpu.VMEM((head, seq), F32),
            pltpu.VMEM((head, seq), F32),
        ],
        compiler_params=pltpu.CompilerParams(vmem_limit_bytes=48 << 20),
    )(qkv, qkv, qkv, bias, hot, lse, grad)


def fetch_plain(dp, mp, tok, cot, pa, pb, pc, vec):
    d, m = lax.axis_index("dp"), lax.axis_index("mp")
    core = d % 2
    swap = [(i, i ^ 1) for i in range(dp)]

    def sequence(rows):
        whole = lax.all_gather(rows, "mp", axis=1, tiled=True)
        other = lax.ppermute(whole, "dp", swap)
        return jnp.where(m // 2 == core, whole, other)[m % 2]

    def weight(part):
        plane = lax.all_gather(part, "dp", axis=0, tiled=True)
        return lax.dynamic_slice_in_dim(lax.all_gather(plane, "mp"), 2 * core, 2, 0)

    half = tok.shape[1] * mp // 2
    ct = lax.dynamic_slice_in_dim(sequence(cot), core * half, half, 0)
    return (
        sequence(tok), ct, weight(pa), weight(pb), weight(pc), lax.all_gather(vec, "dp"), lax.all_gather(vec, "mp"),
    )


def deliver_plain(dp, mp, da, db, dc, out, gtok, rows, quarter):
    d, m = lax.axis_index("dp"), lax.axis_index("mp")
    core = d % 2
    swap = [(i, i ^ 1) for i in range(dp)]

    def grad(part):
        wide = jnp.zeros((mp,) + part.shape[1:], F32)
        wide = lax.dynamic_update_slice_in_dim(wide, part.astype(F32), 2 * core, 0)
        mine = lax.psum_scatter(wide, "mp", scatter_dimension=0, tiled=True)[0]
        return lax.psum_scatter(mine, "dp", scatter_dimension=0, tiled=True)[None]

    def home(half):
        both = jnp.zeros((2,) + half.shape, half.dtype)
        both = lax.dynamic_update_slice_in_dim(both, half[None], core, 0)
        both = lax.dynamic_update_slice_in_dim(both, lax.ppermute(half, "dp", swap)[None], 1 - core, 0)
        all_rows = lax.all_gather(both.reshape(mp, quarter, -1), "mp")
        mine = lax.dynamic_slice_in_dim(all_rows, 2 * core, 2, 0)
        return lax.dynamic_slice_in_dim(mine, m, 1, 1)[:, 0]

    return grad(da), grad(db), grad(dc), home(out), home(gtok)


def layer(
    dp, mp, tokens, cotangent, w_query, w_key, w_value, w_out, w_inner, w_outer,
    gain_attn, shift_attn, gain_ffn, shift_ffn, seq_lengths, rand_blocks,
):
    d, m = lax.axis_index("dp"), lax.axis_index("mp")
    core = d % 2
    swap = [(i, i ^ 1) for i in range(dp)]
    quarter, width = tokens.shape[1:]
    seq = quarter * mp
    half = seq // 2
    per, nblocks, picks = rand_blocks.shape
    cols = w_query.shape[1]
    head = cols // per
    block = seq // nblocks
    rows = w_query.shape[0]
    vec_rows = [v.astype(F32) for v in (gain_attn, shift_attn, gain_ffn, shift_ffn)]
    vec_rows += [seq_lengths.astype(F32)]
    flat = rand_blocks.astype(F32).reshape(-1)
    vec_rows += [flat[:128], flat[128:]]
    vec = jnp.stack([jnp.pad(v, (0, 128 - v.shape[0])) for v in vec_rows] + [jnp.zeros(128, F32)])
    pa = jnp.concatenate([w_query, w_key, w_value, w_out.T], 1)
    kernels = dp == 8 and mp == 4 and rows % 16 == 0 and pa.shape[1] % 128 == 0
    pb, pc = w_inner, w_outer.T
    if kernels:
        x, ga, gvd, gvz = fetch(mp, tokens, pa, vec)
    else:
        x, ct, ga, gb, gc, gvd, gvz = fetch_plain(dp, mp, tokens, cotangent, pa, pb, pc, vec)
    norms = jnp.swapaxes(gvd[:, :4, :rows], 0, 1).reshape(4, width)
    g1, b1, g2, b2 = (norms[i][None] for i in range(4))
    owner = d - core + m // 2
    lens = lax.dynamic_slice_in_dim(gvd[:, 4, :2], owner, 1, 0)[0]
    length = jnp.where(m % 2 == 0, lens[0], lens[1]).astype(jnp.int32)
    picked = lax.dynamic_slice_in_dim(gvz, 2 * core, 2, 0)
    picked = picked[:, 5:7].reshape(2, 256)[:, : per * nblocks * picks].astype(jnp.int32)
    picked = picked.reshape(2, per, nblocks, picks)

    r = jnp.arange(nblocks)
    near = (r[:, None] == 0) | (r[:, None] == nblocks - 1) | (r[None] == 0) | (r[None] == nblocks - 1)
    near = near | (jnp.abs(r[:, None] - r[None]) <= 1)
    hits = jnp.any(picked[:, :, :, :, None] == r, axis=3) | near
    bias = jnp.where(jnp.swapaxes(hits, 2, 3), 0.0, NEG).astype(BF16)
    bias = jnp.repeat(bias, block, axis=3)
    pos = jnp.arange(seq)
    hot = jnp.concatenate([pos[None] // block == r[:, None], pos[None] >= length, jnp.zeros((15, seq), bool)], 0)
    hot = hot.astype(BF16)

    def mine(values):
        return lax.dynamic_slice_in_dim(values, core * half, half, 0)

    def theirs(values):
        return lax.dynamic_slice_in_dim(values, (1 - core) * half, half, 0)

    def pair_sum(partial):
        return mine(partial) + lax.ppermute(theirs(partial).astype(BF16), "dp", swap).astype(F32)

    def pair_join(values):
        other = lax.ppermute(values, "dp", swap)
        lo = jnp.where(core == 0, values, other)
        hi = jnp.where(core == 0, other, values)
        return jnp.concatenate([lo, hi], 0)

    def dot(spec, a, b):
        return jnp.einsum(spec, a, b, preferred_element_type=F32)

    a_qkv, a_out = ga[:, :, : 3 * cols], ga[:, :, 3 * cols :]
    qkv = dot("mrc,tr->mct", a_qkv, x).astype(BF16)
    if kernels:
        ctx, lse, gb, gc, ct = attend_fetch(mp, qkv, bias, hot, head, pb, pc, cotangent)
    else:
        ctx, lse = attend(qkv, bias, hot, head)
    attn = pair_sum(dot("mct,mdc->td", ctx, a_out))
    x_mine = mine(x).astype(F32)

    def norm(z):
        centre = z - jnp.mean(z, -1, keepdims=True)
        inv = lax.rsqrt(jnp.mean(centre * centre, -1, keepdims=True) + EPS)
        return centre * inv, inv

    n1, inv1 = norm(x_mine + attn)
    hidden = n1 * g1 + b1
    hidden_b = pair_join(hidden.astype(BF16))
    inner = dot("td,mdk->tmk", hidden_b, gb)
    cumul = 0.5 * (1.0 + lax.erf(inner * (1.0 / math.sqrt(2.0))))
    active = (inner * cumul).astype(BF16)
    slope = cumul + inner * jnp.exp(-0.5 * inner * inner) * (1.0 / math.sqrt(2.0 * math.pi))
    n2, inv2 = norm(hidden + pair_sum(dot("tmk,mdk->td", active, gc)))
    valid = (core * half + jnp.arange(half) < length).astype(F32)[:, None]
    out = ((n2 * g2 + b2) * valid).astype(BF16)

    def norm_back(e, n, inv):
        return (e - jnp.mean(e, -1, keepdims=True) - n * jnp.mean(e * n, -1, keepdims=True)) * inv

    gy = ct.astype(F32) * valid
    g_mid = norm_back(gy * g2, n2, inv2)
    d_gain2, d_shift2 = jnp.sum(gy * n2, 0), jnp.sum(gy, 0)
    g_ffn = pair_join(g_mid.astype(BF16))
    d_c = dot("td,tmk->mdk", g_ffn, active).astype(BF16)
    g_inner = (dot("td,mdk->tmk", g_ffn, gc) * slope).astype(BF16)
    d_b = dot("td,tmk->mdk", hidden_b, g_inner).astype(BF16)
    g_hidden = g_mid + pair_sum(dot("tmk,mdk->td", g_inner, gb))
    d_gain1, d_shift1 = jnp.sum(g_hidden * n1, 0), jnp.sum(g_hidden, 0)
    g_res = norm_back(g_hidden * g1, n1, inv1)
    g_attn = pair_join(g_res.astype(BF16))
    d_out = dot("td,mct->mdc", g_attn, ctx).astype(BF16)
    g_ctx = dot("td,mdc->mct", g_attn, a_out).astype(BF16)
    sums = jnp.stack([d_gain1, d_shift1, d_gain2, d_shift2] + [jnp.zeros_like(d_gain1)] * 4)
    if kernels:
        dq, dk, dv, rb, rc, out, sums = attend_deliver(
            mp, qkv, bias, hot, lse, g_ctx, head, d_b, d_c, out, sums, rows, quarter
        )
    else:
        dq, dk, dv = attend_back(qkv, bias, hot, lse, g_ctx, head)
    dqkv = jnp.concatenate([dq, dk, dv], 1)
    d_qkv = dot("tr,mct->mrc", x, dqkv).astype(BF16)
    d_a = jnp.concatenate([d_qkv, d_out], 2)
    gtok = (g_res + pair_sum(dot("mct,mrc->tr", dqkv, a_qkv))).astype(BF16)
    if kernels:
        ra, gtok = deliver(mp, d_a, gtok, rows, quarter)
    else:
        ra, rb, rc, out, gtok = deliver_plain(dp, mp, d_a, d_b, d_c, out, gtok, rows, quarter)
        sums = lax.psum(sums, ("dp", "mp"))
    ra, rb, rc = (jnp.sum(v.astype(F32), 0) for v in (ra, rb, rc))
    sums = lax.dynamic_slice_in_dim(sums, d * rows, rows, 1)
    return (
        out, gtok, ra[:, :cols], ra[:, cols : 2 * cols], ra[:, 2 * cols : 3 * cols], ra[:, 3 * cols :].T, rb, rc.T,
        sums[0], sums[1], sums[2], sums[3],
    )


def solution(mesh):
    dp, mp = mesh.shape["dp"], mesh.shape["mp"]
    act, vec = P("dp", "mp", None), P("dp")
    w_in, w_back = P("dp", "mp"), P("mp", "dp")

    def step(*args):
        return layer(dp, mp, *args)

    return jax.shard_map(
        step,
        mesh=mesh,
        in_specs=(act, act, w_in, w_in, w_in, w_back, w_in, w_back, vec, vec, vec, vec, vec, P("mp", None, None)),
        out_specs=(act, act, w_in, w_in, w_in, w_back, w_in, w_back, vec, vec, vec, vec),
        check_vma=False,
    )
```

```python
import math

import jax
import jax.numpy as jnp
from jax import lax
from jax.experimental import pallas as pl
from jax.experimental.pallas import tpu as pltpu
from jax.sharding import PartitionSpec as P

EPS = 1e-06
NEG = -1000000000.0
MESH = pl.DeviceIdType.MESH
F32 = jnp.float32
BF16 = jnp.bfloat16
ANY = pl.BlockSpec(memory_space=pl.ANY)
VMEM = pl.BlockSpec(memory_space=pltpu.VMEM)
DMA = pltpu.SemaphoreType.DMA


class Place:
    def __init__(self):
        self.d = lax.axis_index("dp")
        self.m = lax.axis_index("mp")
        self.c = lax.rem(self.d, 2)
        self.base = self.d - self.c
        self.sib = self.d + 1 - 2 * self.c
        bx = lax.rem(lax.div(self.d, 2), 2)
        by = lax.rem(lax.div(self.d, 4), 2)
        self.xp = self.d + 2 - 4 * bx
        self.yp = self.d + 4 - 8 * by
        self.bx = self.xp - self.c
        self.by = self.yp - self.c
        self.bd = self.bx + 4 - 8 * by
        self.h = lax.div(self.m, 2)
        self.a = lax.rem(self.m, 2)


def remote(src, dst, ssem, rsem, dev):
    return pltpu.make_async_remote_copy(
        src_ref=src, dst_ref=dst, send_sem=ssem, recv_sem=rsem, device_id=dev, device_id_type=MESH
    )


def push(src, dst, ssem, rsem, dev, same):
    @pl.when(same)
    def _():
        pltpu.make_async_copy(src, dst, rsem).start()

    @pl.when(jnp.logical_not(same))
    def _():
        remote(src, dst, ssem, rsem, dev).start()


def pushed(src, dst, ssem, rsem, dev, same):
    @pl.when(jnp.logical_not(same))
    def _():
        remote(src, dst, ssem, rsem, dev).wait_send()


def got(dst, ssem, rsem, dev):
    remote(dst, dst, ssem, rsem, dev).wait_recv()


def greet(peers):
    barrier = pltpu.get_barrier_semaphore()
    for dev in peers:
        pl.semaphore_signal(barrier, inc=1, device_id=dev, device_id_type=MESH)
    pl.semaphore_wait(barrier, len(peers))


def dots(a, b, ca, cb):
    return lax.dot_general(a, b, (((ca,), (cb,)), ((), ())), preferred_element_type=F32)


def column_peers(p, mp):
    peers = []
    for k in range(1, mp):
        z = lax.rem(p.m + k, mp)
        peers += [(p.base, z), (p.base + 1, z)]
    return peers


class Gather:
    def __init__(self, p, src, dst, first, count, sems, mp):
        self.p, self.src, self.dst, self.mp = p, src, dst, mp
        self.zs, self.zr, self.xs, self.xr, self.ys, self.yr = sems
        self.n = src.shape[0]
        self.cols = pl.ds(first, count)

    def rows(self, a, first, count):
        return self.dst.at[a, pl.ds(first * self.n, count * self.n), self.cols]

    def z_args(self, k):
        p = self.p
        z = lax.rem(p.m + k, self.mp)
        same = (p.h == p.c) if k == 0 else None
        src = self.src.at[:, self.cols]
        return (src, self.rows(p.a, p.d, 1), self.zs.at[k], self.zr.at[2 * p.c + p.a], (p.base + p.h, z)), same

    def z_send(self):
        for k in (2, 1, 3, 0):
            args, same = self.z_args(k)
            if same is None:
                remote(*args).start()
            else:
                push(*args, same)

    def z_recv(self):
        p = self.p
        for core in range(2):
            for a in range(2):
                got(self.rows(a, p.base + core, 1), self.zs.at[0], self.zr.at[2 * core + a], (p.d, p.m))

    def hop(self, axis, step, a):
        p = self.p
        peer = p.xp if axis == 0 else p.yp
        first = p.base if step == 0 else (p.by if axis == 0 else p.bx)
        part = self.rows(a, first, 2)
        s, r = (self.xs, self.xr) if axis == 0 else (self.ys, self.yr)
        i = 2 if step else a
        return remote(part, part, s.at[i], r.at[i], (peer, p.m))

    def xy_send(self):
        for a in range(2):
            self.hop(0, 0, a).start()
            self.hop(1, 0, 1 - a).start()

    def arrived(self, axis, step, a):
        p = self.p
        first = (p.bx if axis == 0 else p.by) if step == 0 else p.bd
        s, r = (self.xs, self.xr) if axis == 0 else (self.ys, self.yr)
        i = 2 if step else a
        got(self.rows(a, first, 2), s.at[i], r.at[i], (p.d, p.m))

    def forward(self):
        self.arrived(0, 0, 0)
        self.hop(1, 1, 0).start()
        self.arrived(1, 0, 1)
        self.hop(0, 1, 1).start()

    def land(self):
        self.arrived(0, 0, 1)
        self.arrived(1, 0, 0)
        self.arrived(1, 1, 0)
        self.arrived(0, 1, 1)

    def finish(self):
        for k in range(self.mp):
            args, same = self.z_args(k)
            if same is None:
                remote(*args).wait_send()
            else:
                pushed(*args, same)
        for a in range(2):
            self.hop(0, 0, a).wait_send()
            self.hop(1, 0, a).wait_send()
        self.hop(1, 1, 0).wait_send()
        self.hop(0, 1, 1).wait_send()


def gather_sems(mp):
    return [DMA((mp,)), DMA((4,)), DMA((3,)), DMA((3,)), DMA((3,)), DMA((3,))]


class Tokens:
    def __init__(self, p, tok, x, sems):
        self.p, self.tok, self.x = p, tok, x
        self.s, self.r, self.fs, self.fr = sems
        self.piece = tok.shape[1] // 2

    def args(self, i, half):
        p, n = self.p, self.piece
        z = 2 * p.c + i
        dev = (p.base + half, z)
        dst = self.x.at[pl.ds((2 * p.m + half) * n, n), :]
        src = self.tok.at[i, pl.ds(half * n, n), :]
        return (src, dst, self.s.at[2 * i + half], self.r.at[p.m], dev), jnp.logical_and(p.c == half, p.m == z)

    def send(self):
        for i in range(2):
            for half in range(2):
                args, same = self.args(i, half)
                push(*args, same)

    def part(self, q, core):
        return self.x.at[pl.ds((2 * q + core) * self.piece, self.piece), :]

    def forward(self, mp):
        p = self.p
        for q in range(mp):
            got(self.part(q, p.c), self.s.at[0], self.r.at[q], (p.d, p.m))
            remote(self.part(q, p.c), self.part(q, p.c), self.fs.at[q], self.fr.at[q], (p.sib, p.m)).start()

    def land(self, mp):
        p = self.p
        for q in range(mp):
            got(self.part(q, 1 - p.c), self.fs.at[q], self.fr.at[q], (p.d, p.m))

    def finish(self, mp):
        p = self.p
        for q in range(mp):
            remote(self.part(q, p.c), self.part(q, p.c), self.fs.at[q], self.fr.at[q], (p.sib, p.m)).wait_send()
        for i in range(2):
            for half in range(2):
                args, same = self.args(i, half)
                pushed(*args, same)


class Quarters:
    def __init__(self, p, src, dst, sems):
        self.p, self.src, self.dst = p, src, dst
        self.s, self.r = sems
        self.n = src.shape[1]

    def args(self, i):
        p = self.p
        z = 2 * p.c + i
        dst = self.dst.at[pl.ds(p.a * self.n, self.n), :]
        same = jnp.logical_and(p.h == p.c, p.m == z)
        return (self.src.at[i], dst, self.s.at[i], self.r.at[p.a], (p.base + p.h, z)), same

    def send(self):
        for i in range(2):
            args, same = self.args(i)
            push(*args, same)

    def finish(self):
        p = self.p
        for a in range(2):
            got(self.dst.at[pl.ds(a * self.n, self.n), :], self.s.at[a], self.r.at[a], (p.d, p.m))
        for i in range(2):
            args, same = self.args(i)
            pushed(*args, same)


class Homewards:
    def __init__(self, p, src, dst, sems):
        self.p, self.src, self.dst = p, src, dst
        self.s, self.r = sems
        self.n = dst.shape[1]

    def args(self, q):
        p = self.p
        src = self.src.at[pl.ds(q * self.n, self.n), :]
        owner = p.base + p.h
        same = jnp.logical_and(owner == p.d, p.m == 2 * p.c + q)
        return (src, self.dst.at[p.a], self.s.at[q], self.r.at[p.a], (owner, 2 * p.c + q)), same

    def send(self):
        for q in range(2):
            args, same = self.args(q)
            push(*args, same)

    def finish(self):
        p = self.p
        for i in range(2):
            got(self.dst.at[i], self.s.at[i], self.r.at[i], (p.d, p.m))
        for q in range(2):
            args, same = self.args(q)
            pushed(*args, same)


class Scatter:
    def __init__(self, p, src, out, a, first, count, axis, bufs, sems, mp):
        self.p, self.src, self.out, self.a, self.axis, self.mp = p, src, out, a, axis, mp
        self.r1, self.r2, self.r3, self.total = bufs
        self.s, self.r, self.zs, self.zr = sems
        self.n = out.shape[1]
        self.cols = pl.ds(first, count)
        self.near, self.far = ((p.xp, p.bx), (p.yp, p.by)) if axis == 0 else ((p.yp, p.by), (p.xp, p.bx))

    def rows(self, first):
        return self.src.at[self.a, pl.ds(first * self.n, 2 * self.n), self.cols]

    def hop(self, kind):
        p = self.p
        if kind == 0:
            src, dst, peer = self.rows(p.bd), self.r1, self.near[0]
        elif kind == 1:
            src, dst, peer = self.rows(self.near[1]), self.r2, self.near[0]
        else:
            src, dst, peer = self.r1, self.r3, self.far[0]
        return remote(src, dst, self.s.at[kind], self.r.at[kind], (peer, p.m))

    def start(self):
        self.hop(0).start()
        self.hop(1).start()

    def second(self):
        self.hop(0).wait_recv()
        self.r1[...] = (self.rows(self.far[1])[...].astype(F32) + self.r1[...].astype(F32)).astype(BF16)
        self.hop(2).start()

    def third(self):
        self.hop(1).wait_recv()
        self.hop(2).wait_recv()
        self.total[...] = (
            self.rows(self.p.base)[...].astype(F32) + self.r2[...].astype(F32) + self.r3[...].astype(F32)
        ).astype(BF16)
        for core in range(2):
            args, same = self.z_args(core)
            push(*args, same)

    def z_args(self, core):
        p = self.p
        owner = (p.base + core, 2 * p.c + self.a)
        same = jnp.logical_and(p.c == core, p.m == 2 * p.c + self.a)
        src = self.total.at[pl.ds(core * self.n, self.n), :]
        return (src, self.out.at[p.m, :, self.cols], self.zs.at[core], self.zr.at[p.m], owner), same

    def finish(self):
        for kind in range(3):
            self.hop(kind).wait_send()
        for core in range(2):
            args, same = self.z_args(core)
            pushed(*args, same)


def owned(p, out, first, count, zs, zr, mp):
    for z in range(mp):
        got(out.at[z, :, pl.ds(first, count)], zs.at[0], zr.at[z], (p.d, p.m))


class Sums:
    def __init__(self, p, out, bufs, sems, mp):
        self.p, self.out, self.mp = p, out, mp
        self.mine, self.came, self.parts = bufs
        self.s, self.r, self.zs, self.zr = sems

    def hop(self, i):
        p = self.p
        dev = (p.sib, p.xp, p.yp)[i]
        return remote(self.mine.at[i], self.came.at[i], self.s.at[i], self.r.at[i], (dev, p.m))

    def start(self, values):
        self.mine[0] = values
        self.hop(0).start()

    def step(self, i):
        self.hop(i).wait_recv()
        total = self.mine[i] + self.came[i]
        if i < 2:
            self.mine[i + 1] = total
            self.hop(i + 1).start()
        else:
            self.parts[self.p.m] = total
            for k in range(1, self.mp):
                self.column(k).start()

    def column(self, k):
        p = self.p
        part = self.parts.at[p.m]
        return remote(part, part, self.zs.at[k - 1], self.zr.at[p.m], (p.d, lax.rem(p.m + k, self.mp)))

    def finish(self):
        p = self.p
        for k in range(1, self.mp):
            z = lax.rem(p.m + k, self.mp)
            got(self.parts.at[z], self.zs.at[0], self.zr.at[z], (p.d, p.m))
        total = self.parts[0]
        for z in range(1, self.mp):
            total = total + self.parts[z]
        self.out[...] = total
        for i in range(3):
            self.hop(i).wait_send()
        for k in range(1, self.mp):
            self.column(k).wait_send()


class Swap:
    def __init__(self, p, src, dst, sems, src_first=0, dst_first=0, came_first=0, count=256):
        self.p, self.src, self.dst = p, src, dst
        self.s, self.r = sems
        self.firsts = (src_first, dst_first, came_first)
        self.n = count

    def copy(self, i, side):
        p, n = self.p, self.n
        src_first, dst_first, came_first = self.firsts
        if side == 0:
            src = self.src.at[pl.ds(src_first + i * n, n), :]
            dst = self.dst.at[pl.ds(dst_first + i * n, n), :]
        else:
            src = dst = self.dst.at[pl.ds(came_first + i * n, n), :]
        return remote(src, dst, self.s.at[i], self.r.at[i], (p.sib, p.m))

    def send(self, i):
        self.copy(i, 0).start()

    def recv(self, i):
        self.copy(i, 1).wait_recv()

    def finish(self):
        for i in range(2):
            self.copy(i, 0).wait_send()


def gelu_pair(inner):
    cumul = 0.5 * (1.0 + lax.erf(inner * (1.0 / math.sqrt(2.0))))
    slope = cumul + inner * jnp.exp(-0.5 * inner * inner) * (1.0 / math.sqrt(2.0 * math.pi))
    return inner * cumul, slope


def norm_back(e, n, inv):
    return (e - jnp.mean(e, -1, keepdims=True) - n * jnp.mean(e * n, -1, keepdims=True)) * inv


def norm_rows(z):
    centre = z - jnp.mean(z, -1, keepdims=True)
    inv = lax.rsqrt(jnp.mean(centre * centre, -1, keepdims=True) + EPS)
    return centre * inv, inv


def scatter_sems(mp):
    return [DMA((3,)), DMA((3,)), DMA((2,)), DMA((mp,))]


def layer_kernel(mp, head, nblocks, picks, names, *refs):
    r = dict(zip(names, refs, strict=True))
    p = Place()
    x, ga, gb, gc, at, qkv, ctx, gctx = (r[k] for k in ("x", "ga", "gb", "gc", "at", "qkv", "ctx", "gctx"))
    seq, width = x.shape
    half = seq // 2
    rc = half // 2
    group = qkv.shape[0] // 2
    cols = group // 3
    per = cols // head
    heads = 2 * per
    n = r["pa"].shape[0]
    scale = 1.0 / math.sqrt(head)
    mine = pl.multiple_of(p.c * half, half)
    theirs = pl.multiple_of(half - p.c * half, half)
    hw = width // 2

    def sems(key):
        return [v for k, v in r.items() if k.startswith(key + ".")]

    tokens = Tokens(p, r["tok"], x, sems("tok"))
    cots = Quarters(p, r["cot"], r["ct"], sems("cot"))
    gathers = [
        Gather(p, r["p" + w], r["g" + w], i * hw, hw, sems(f"g{w}{i}"), mp) for w in "abc" for i in range(2)
    ]
    a0, a1, b0, b1, c0, c1 = gathers
    plane = [lax.rem(p.d + k, 8) for k in range(1, 8)]
    vec, pick, gvec, gpick = r["vec"], r["pick"], r["gvec"], r["gpick"]
    vs, vr, us, ur = sems("vec")
    sums = Sums(p, r["sums"], sems("sumbuf"), sems("sum"), mp)
    home = Homewards(p, r["outb"], r["hout"], sems("home"))
    home_g = Homewards(p, r["gtokb"], r["hgtok"], sems("homeg"))
    pair_attn = Swap(p, r["send"], r["recv"], sems("sw0"), count=rc)
    pair_hid = Swap(p, r["hb"], r["hb"], sems("sw1"), mine, mine, theirs, rc)
    pair_ffn = Swap(p, r["send1"], r["recv1"], sems("sw2"), count=rc)
    pair_gf = Swap(p, r["gf"], r["gf"], sems("sw3"), mine, mine, theirs, rc)
    pair_gh = Swap(p, r["send2"], r["recv2"], sems("sw4"), count=rc)
    pair_ga = Swap(p, r["gat"], r["gat"], sems("sw5"), mine, mine, theirs, rc)
    pair_gt = Swap(p, r["send3"], r["recv3"], sems("sw6"), count=rc)

    def units(name, src, out):
        made = []
        for a in range(2):
            for i in range(2):
                made.append(Scatter(p, src, out, a, i * hw, hw, i, sems(f"s{name}{a}{i}b"), sems(f"s{name}{a}{i}s"), mp))
        return made

    ua, ub, uc = units("a", ga, r["la"]), units("b", r["db"], r["lb"]), units("c", r["dc"], r["lc"])

    greet(column_peers(p, mp) + [(d, p.m) for d in plane])
    a0.z_send()
    a1.z_send()
    tokens.send()
    vcopies = [remote(vec, gvec.at[p.d], vs.at[k], vr.at[p.d], (d, p.m)) for k, d in enumerate(plane)]
    ucopies = [remote(pick, gpick.at[p.m], us.at[k - 1], ur.at[p.m], (p.d, lax.rem(p.m + k, mp))) for k in range(1, mp)]
    own = [pltpu.make_async_copy(vec, gvec.at[p.d], vr.at[p.d]), pltpu.make_async_copy(pick, gpick.at[p.m], ur.at[p.m])]
    for copy in vcopies + ucopies + own:
        copy.start()
    a0.z_recv()
    a0.xy_send()
    a1.z_recv()
    a1.xy_send()

    for d in range(8):
        got(gvec.at[d], vs.at[0], vr.at[d], (p.d, p.m))
    for z in range(mp):
        got(gpick.at[z], us.at[0], ur.at[z], (p.d, p.m))
    vecs = gvec[0].astype(F32)
    for d in range(1, 8):
        vecs = vecs + gvec[d].astype(F32)
    r["norms"][...] = vecs
    lane = lax.broadcasted_iota(jnp.int32, (1, width), 1)
    spot = (p.base + p.h) * n + 2 * p.a
    row = vecs[4:5]
    length = jnp.sum(jnp.where(lane == spot, row * 32.0, 0.0) + jnp.where(lane == spot + 1, row, 0.0), 1, keepdims=True)
    block = seq // nblocks
    sub = lax.broadcasted_iota(jnp.int32, (nblocks, seq), 0)
    place = lax.broadcasted_iota(jnp.int32, (nblocks, seq), 1)
    rb = lax.div(place, block)
    near = (rb == 0) | (rb == nblocks - 1) | (sub == 0) | (sub == nblocks - 1) | (jnp.abs(rb - sub) <= 1)
    spread = lax.broadcasted_iota(jnp.int32, (128, seq), 0) == lax.div(lax.broadcasted_iota(jnp.int32, (128, seq), 1), block)
    spread = jnp.where(spread, 1.0, 0.0).astype(BF16)
    subf = sub.astype(F32)
    for a in range(2):
        wide = dots(gpick[2 * p.c + a], spread, 1, 0)
        for h in range(per):
            hit = near
            for j in range(picks):
                at_row = h * picks + j
                hit = hit | (wide[at_row : at_row + 1] == subf)
            r["bias"][a * per + h] = jnp.where(hit, 0.0, NEG).astype(BF16)
    qa, ka = r["qa"], r["ka"]
    low = lax.broadcasted_iota(jnp.int32, (16, seq), 0)
    ka[head : head + nblocks, :] = jnp.where(rb == sub, 1.0, 0.0).astype(BF16)
    beyond = lax.broadcasted_iota(jnp.int32, (16, seq), 1).astype(F32) >= length
    ka[head + nblocks :, :] = jnp.where((low == 0) & beyond, 1.0, 0.0).astype(BF16)
    qa[head + nblocks :, :] = jnp.where(low == 0, NEG, 0.0).astype(BF16)

    a0.forward()
    a1.forward()
    tokens.forward(mp)
    b0.z_send()
    b1.z_send()
    a0.land()
    a1.land()
    for a in range(2):
        at[a] = ga[a].T
    tokens.land(mp)

    def project(i, _):
        rows = pl.ds(pl.multiple_of(i * rc, rc), rc)
        for a in range(2):
            qkv[a * group : (a + 1) * group, rows] = dots(at[a, :group, :], x[rows, :], 1, 1).astype(BF16)
        return 0

    lax.fori_loop(0, seq // rc, project, 0)

    def parts(i):
        a = lax.div(i, per)
        first = a * group + (i - a * per) * head
        return [pl.ds(pl.multiple_of(first + part * cols, head), head) for part in range(3)]

    def set_head(i):
        q, k, v = parts(i)
        qa[0:head, :] = (qkv[q, :].astype(F32) * scale).astype(BF16)
        qa[head : head + nblocks, :] = r["bias"][i]
        ka[0:head, :] = qkv[k, :]
        return q, k, v

    def attend_head(i, _):
        q, k, v = set_head(i)
        own_rows = pl.ds(pl.multiple_of(i * head, head), head)
        for j in range(2):
            span = slice(j * half, (j + 1) * half)
            scores = dots(ka[...], qa[:, span], 0, 0)
            peak = jnp.max(scores, 0, keepdims=True)
            weights = jnp.exp(scores - peak)
            total = jnp.sum(weights, 0, keepdims=True)
            mixed = jnp.dot(qkv[v, :], weights.astype(BF16), preferred_element_type=F32)
            ctx[own_rows, span] = (mixed / total).astype(BF16)
            r["lse"][i, :, span] = peak + jnp.log(total)

        @pl.when(i == 2)
        def _():
            b0.z_recv()
            b0.xy_send()
            b1.z_recv()
            b1.xy_send()
            c0.z_send()
            c1.z_send()

        return 0

    lax.fori_loop(0, heads, attend_head, 0)
    b0.forward()

    wo = r["wo"]
    for a in range(2):
        wo[a * cols : (a + 1) * cols, :] = at[a, group:, :]
    norms = r["norms"]
    g1, s1, g2, s2 = (norms[i : i + 1] for i in range(4))

    def attn_part(first):
        return dots(ctx[:, pl.ds(first, rc)], wo[...], 0, 0)

    for i in range(2):
        r["send"][i * rc : (i + 1) * rc, :] = attn_part(pl.multiple_of(theirs + i * rc, rc)).astype(BF16)
        pair_attn.send(i)
    b1.forward()
    for i in range(2):
        rows = pl.ds(pl.multiple_of(mine + i * rc, rc), rc)
        here = slice(i * rc, (i + 1) * rc)
        part = attn_part(pl.multiple_of(mine + i * rc, rc))
        pair_attn.recv(i)
        n1, inv = norm_rows(x[rows, :].astype(F32) + part + r["recv"][here, :].astype(F32))
        hidden = n1 * g1 + s1
        r["n1"][here, :] = n1
        r["inv1"][here, :] = jnp.broadcast_to(inv, (rc, 128))
        r["res"][here, :] = hidden
        r["hb"][rows, :] = hidden.astype(BF16)
        pair_hid.send(i)

    c0.z_recv()
    c0.xy_send()
    c1.z_recv()
    c1.xy_send()
    cots.send()
    b0.land()
    b1.land()

    def up(i, _):
        for k in range(2):

            @pl.when(i == 2 + k)
            def _():
                pair_hid.recv(k)

        rows = pl.ds(pl.multiple_of(lax.rem(2 * p.c + i, 4) * rc, rc), rc)
        for a in range(2):
            active, slope = gelu_pair(dots(r["hb"][rows, :], gb[a], 1, 0))
            r["act"][rows, a * width : (a + 1) * width] = active.astype(BF16)
            r["slope"][rows, a * width : (a + 1) * width] = slope.astype(BF16)
        return 0

    lax.fori_loop(0, 4, up, 0)
    c0.forward()
    c1.forward()
    c0.land()
    c1.land()

    def ffn_part(rows):
        return dots(r["act"][rows, :width], gc[0], 1, 1) + dots(r["act"][rows, width:], gc[1], 1, 1)

    for i in range(2):
        r["send1"][i * rc : (i + 1) * rc, :] = ffn_part(pl.ds(pl.multiple_of(theirs + i * rc, rc), rc)).astype(BF16)
        pair_ffn.send(i)
    cots.finish()
    small = r["small"]
    small[...] = jnp.zeros_like(small)
    for i in range(2):
        rows = pl.ds(pl.multiple_of(mine + i * rc, rc), rc)
        here = slice(i * rc, (i + 1) * rc)
        part = ffn_part(rows)
        pair_ffn.recv(i)
        n2, inv = norm_rows(r["res"][here, :] + part + r["recv1"][here, :].astype(F32))
        pos = (lax.broadcasted_iota(jnp.int32, (rc, 1), 0) + (mine + i * rc)).astype(F32)
        valid = jnp.where(pos < length, 1.0, 0.0)
        r["outb"][here, :] = ((n2 * g2 + s2) * valid).astype(BF16)
        gy = r["ct"][here, :].astype(F32) * valid
        small[2:3, :] += jnp.sum(gy * n2, 0, keepdims=True)
        small[3:4, :] += jnp.sum(gy, 0, keepdims=True)
        g_mid = norm_back(gy * g2, n2, inv)
        r["res"][here, :] = g_mid
        r["gf"][rows, :] = g_mid.astype(BF16)
        pair_gf.send(i)
    home.send()

    for g in gathers:
        g.finish()
    for i in range(2):
        pair_gf.recv(i)

    def grad_c(j, _):
        span = pl.ds(pl.multiple_of(j * rc, rc), rc)
        for a in range(2):
            r["dc"][a, span, :] = dots(r["gf"][:, span], r["act"][:, a * width : (a + 1) * width], 0, 0).astype(BF16)
        return 0

    lax.fori_loop(0, width // rc, grad_c, 0)
    for u in uc:
        u.start()

    def back(i, _):
        rows = pl.ds(pl.multiple_of(i * rc, rc), rc)
        for a in range(2):
            part = (rows, slice(a * width, (a + 1) * width))
            r["slope"][part] = (dots(r["gf"][rows, :], gc[a], 1, 0) * r["slope"][part].astype(F32)).astype(BF16)
        return 0

    lax.fori_loop(0, 4, back, 0)

    def hid_part(rows):
        return dots(r["slope"][rows, :width], gb[0], 1, 1) + dots(r["slope"][rows, width:], gb[1], 1, 1)

    for i in range(2):
        r["send2"][i * rc : (i + 1) * rc, :] = hid_part(pl.ds(pl.multiple_of(theirs + i * rc, rc), rc)).astype(BF16)
        pair_gh.send(i)
    for u in uc:
        u.second()

    def grad_b(j, _):
        span = pl.ds(pl.multiple_of(j * rc, rc), rc)
        for a in range(2):
            r["db"][a, span, :] = dots(r["hb"][:, span], r["slope"][:, a * width : (a + 1) * width], 0, 0).astype(BF16)
        return 0

    lax.fori_loop(0, width // rc, grad_b, 0)
    for u in ub:
        u.start()
    for i in range(2):
        rows = pl.ds(pl.multiple_of(mine + i * rc, rc), rc)
        here = slice(i * rc, (i + 1) * rc)
        part = hid_part(rows)
        pair_gh.recv(i)
        gh = r["res"][here, :] + part + r["recv2"][here, :].astype(F32)
        n1 = r["n1"][here, :]
        small[0:1, :] += jnp.sum(gh * n1, 0, keepdims=True)
        small[1:2, :] += jnp.sum(gh, 0, keepdims=True)
        g_res = norm_back(gh * g1, n1, r["inv1"][here, 0:1])
        r["res"][here, :] = g_res
        r["gat"][rows, :] = g_res.astype(BF16)
        pair_ga.send(i)
    sums.start(small[...])
    for k in range(4):
        rows = pl.ds(pl.multiple_of(lax.rem(2 * p.c + k, 4) * rc, rc), rc)
        if k >= 2:
            pair_ga.recv(k - 2)
        gctx[:, rows] = dots(wo[...], r["gat"][rows, :], 1, 1).astype(BF16)

    def grad_a(a):
        turn = r["turn"]
        turn[:group, :] = jnp.dot(qkv[a * group : (a + 1) * group, :], x[...], preferred_element_type=F32).astype(BF16)
        turn[group:, :] = jnp.dot(ctx[a * cols : (a + 1) * cols, :], r["gat"][...], preferred_element_type=F32).astype(BF16)
        ga[a] = turn[...].T

    def attend_head_back(i, _):
        q, k, v = set_head(i)
        own_rows = pl.ds(pl.multiple_of(i * head, head), head)
        gk = gv = None
        for j in range(2):
            span = slice(j * half, (j + 1) * half)
            scores = dots(ka[...], qa[:, span], 0, 0)
            probs = jnp.exp(scores - r["lse"][i, :, span])
            grad = gctx[own_rows, span]
            grad_probs = dots(qkv[v, :], grad, 0, 0)
            inner = jnp.sum(probs * grad_probs, 0, keepdims=True)
            grad_scores = (probs * (grad_probs - inner)).astype(BF16)
            qkv[q, span] = (jnp.dot(ka[0:head, :], grad_scores, preferred_element_type=F32) * scale).astype(BF16)
            dk = dots(qa[0:head, span], grad_scores, 1, 1)
            dv = dots(grad, probs.astype(BF16), 1, 1)
            gk, gv = (dk, dv) if gk is None else (gk + dk, gv + dv)
        qkv[k, :] = gk.astype(BF16)
        qkv[v, :] = gv.astype(BF16)

        for k in range(3):

            @pl.when(i == k)
            def _():
                sums.step(k)

        @pl.when(i == 1)
        def _():
            for u in uc:
                u.third()

        @pl.when(i == 2)
        def _():
            grad_a(0)
            for u in ua[:2]:
                u.start()

        @pl.when(i == 3)
        def _():
            for u in ub:
                u.second()

        return 0

    lax.fori_loop(0, heads, attend_head_back, 0)

    def tok_part(rows):
        return dots(qkv[:group, rows], at[0, :group, :], 0, 0) + dots(qkv[group:, rows], at[1, :group, :], 0, 0)

    for i in range(2):
        r["send3"][i * rc : (i + 1) * rc, :] = tok_part(pl.ds(pl.multiple_of(theirs + i * rc, rc), rc)).astype(BF16)
        pair_gt.send(i)
    grad_a(1)
    for u in ua[2:]:
        u.start()
    for i in range(2):
        rows = pl.ds(pl.multiple_of(mine + i * rc, rc), rc)
        here = slice(i * rc, (i + 1) * rc)
        part = tok_part(rows)
        pair_gt.recv(i)
        r["gtokb"][here, :] = (r["res"][here, :] + part + r["recv3"][here, :].astype(F32)).astype(BF16)
    home_g.send()
    for u in ub:
        u.third()
    for u in ua[:2]:
        u.second()
    for u in ua[2:]:
        u.second()
    for u in ua[:2]:
        u.third()
    for u in ua[2:]:
        u.third()
    sums.finish()

    def settle(made, land, out):
        for i in range(2):
            for a in range(2):
                u = made[2 * a + i]

                @pl.when(p.a == a)
                def _():
                    owned(p, land, i * hw, hw, u.zs, u.zr, mp)

        total = land[0].astype(F32)
        for z in range(1, mp):
            total = total + land[z].astype(F32)
        out[...] = total

    settle(uc, r["lc"], r["rc"])
    settle(ub, r["lb"], r["rb"])
    settle(ua, r["la"], r["ra"])
    home.finish()
    home_g.finish()
    cots_done = [tokens.finish(mp)]
    for swap in (pair_attn, pair_hid, pair_ffn, pair_gf, pair_gh, pair_ga, pair_gt):
        swap.finish()
    for u in ua + ub + uc:
        u.finish()
    for copy in vcopies + ucopies:
        copy.wait_send()


def fused_layer(mp, tok, cot, pa, pb, pc, vec, pick, head, nblocks, picks):
    n, width = pa.shape
    quarter = tok.shape[1]
    seq = quarter * mp
    half = seq // 2
    per = width // 4 // head
    group = 3 * per * head
    shape = jax.ShapeDtypeStruct
    names = ["tok", "cot", "pa", "pb", "pc", "vec", "pick"]
    outs = {
        "hout": (shape((2, quarter, width), BF16), ANY),
        "hgtok": (shape((2, quarter, width), BF16), ANY),
        "ra": (shape((n, width), F32), VMEM),
        "rb": (shape((n, width), F32), VMEM),
        "rc": (shape((n, width), F32), VMEM),
        "sums": (shape((8, width), F32), VMEM),
    }
    weight = ((2, 8 * n, width), BF16)
    rows_b, half_b, half_f = ((seq, width), BF16), ((half, width), BF16), ((half, width), F32)
    bufs = {
        "x": rows_b, "ga": weight, "gb": weight, "gc": weight, "at": weight, "db": weight, "dc": weight,
        "qkv": ((2 * group, seq), BF16), "ctx": ((2 * per * head, seq), BF16), "gctx": ((2 * per * head, seq), BF16),
        "wo": ((2 * per * head, width), BF16), "lse": ((2 * per, 1, seq), F32), "n1": half_f, "inv1": ((half, 128), F32), "res": half_f,
        "hb": rows_b, "act": ((seq, 2 * width), BF16), "slope": ((seq, 2 * width), BF16), "gf": rows_b, "gat": rows_b,
        "send": half_b, "recv": half_b, "send1": half_b, "recv1": half_b, "send2": half_b, "recv2": half_b,
        "send3": half_b, "recv3": half_b, "outb": half_b, "gtokb": half_b, "ct": half_b,
        "gvec": ((8,) + vec.shape, BF16), "gpick": ((mp,) + pick.shape, BF16), "norms": (vec.shape, F32),
        "bias": ((2 * per, nblocks, seq), BF16), "qa": ((head + nblocks + 16, seq), BF16), "ka": ((head + nblocks + 16, seq), BF16),
        "small": ((8, width), F32), "turn": ((width, width), BF16),
        "la": ((mp, n, width), BF16), "lb": ((mp, n, width), BF16), "lc": ((mp, n, width), BF16),
        "sumbuf.0": ((3, 8, width), F32), "sumbuf.1": ((3, 8, width), F32), "sumbuf.2": ((mp, 8, width), F32),
    }
    for w in "abc":
        for a in range(2):
            for i in range(2):
                for k in range(4):
                    bufs[f"s{w}{a}{i}b.{k}"] = ((2 * n, width // 2), BF16)
    scratch = {k: pltpu.VMEM(*v) for k, v in bufs.items()}

    def add(key, specs):
        for i, spec in enumerate(specs):
            scratch[f"{key}.{i}"] = spec

    add("tok", [DMA((4,)), DMA((mp,)), DMA((mp,)), DMA((mp,))])
    for key in ("cot", "home", "homeg", *(f"sw{i}" for i in range(7))):
        add(key, [DMA((2,)), DMA((2,))])
    for w in "abc":
        for i in range(2):
            add(f"g{w}{i}", gather_sems(mp))
        for a in range(2):
            for i in range(2):
                add(f"s{w}{a}{i}s", scatter_sems(mp))
    add("vec", [DMA((7,)), DMA((8,)), DMA((mp - 1,)), DMA((mp,))])
    add("sum", [DMA((3,)), DMA((3,)), DMA((mp - 1,)), DMA((mp,))])
    names = names + list(outs) + list(scratch)
    return pl.pallas_call(
        lambda *refs: layer_kernel(mp, head, nblocks, picks, names, *refs),
        name="layer",
        out_shape=[o[0] for o in outs.values()],
        in_specs=[ANY] * 5 + [VMEM] * 2,
        out_specs=[o[1] for o in outs.values()],
        scratch_shapes=list(scratch.values()),
        compiler_params=pltpu.CompilerParams(collective_id=0, has_side_effects=True, vmem_limit_bytes=64 << 20),
    )(tok, cot, pa, pb, pc, vec, pick)


def attend_kernel(q_ref, k_ref, v_ref, bias_ref, hot_ref, ctx_ref, lse_ref, qa, ka):
    seq = q_ref.shape[2]
    head = q_ref.shape[1]
    scale = 1.0 / math.sqrt(head)
    blocks = bias_ref.shape[2]
    step = min(256, seq)
    qa[0:head, :] = (q_ref[0].astype(F32) * scale).astype(BF16)
    qa[head : head + blocks, :] = bias_ref[0, 0]
    low = lax.broadcasted_iota(jnp.int32, (qa.shape[0] - head - blocks, seq), 0)
    qa[head + blocks :, :] = jnp.where(low == 0, NEG, 0.0).astype(BF16)
    ka[0:head, :] = k_ref[0]
    ka[head:, :] = hot_ref[...]
    for i in range(seq // step):
        cols = slice(i * step, (i + 1) * step)
        scores = lax.dot_general(ka[...], qa[:, cols], (((0,), (0,)), ((), ())), preferred_element_type=F32)
        peak = jnp.max(scores, 0, keepdims=True)
        weights = jnp.exp(scores - peak)
        total = jnp.sum(weights, 0, keepdims=True)
        mixed = jnp.dot(v_ref[0], weights.astype(BF16), preferred_element_type=F32)
        ctx_ref[0, :, cols] = (mixed / total).astype(BF16)
        lse_ref[0, 0, :, cols] = peak + jnp.log(total)


def head_specs(head, seq, per, blocks, hot_rows):
    row = lambda part: pl.BlockSpec((1, head, seq), lambda m, h: (m, part * per + h, 0))
    return (
        [row(0), row(1), row(2)],
        pl.BlockSpec((1, 1, blocks, seq), lambda m, h: (m, h, 0, 0)),
        pl.BlockSpec((hot_rows, seq), lambda m, h: (0, 0)),
        pl.BlockSpec((1, 1, 1, seq), lambda m, h: (m, h, 0, 0)),
        row(0),
    )


def attend(qkv, bias, hot, head):
    groups, width, seq = qkv.shape
    per = width // (3 * head)
    rows, bias_spec, hot_spec, line, out = head_specs(head, seq, per, bias.shape[2], hot.shape[0])
    deep = head + hot.shape[0]
    return pl.pallas_call(
        attend_kernel,
        name="attend",
        grid=(groups, per),
        out_shape=[
            jax.ShapeDtypeStruct((groups, per * head, seq), BF16),
            jax.ShapeDtypeStruct((groups, per, 1, seq), F32),
        ],
        in_specs=rows + [bias_spec, hot_spec],
        out_specs=[out, line],
        scratch_shapes=[pltpu.VMEM((deep, seq), BF16), pltpu.VMEM((deep, seq), BF16)],
        compiler_params=pltpu.CompilerParams(vmem_limit_bytes=48 << 20),
    )(qkv, qkv, qkv, bias, hot)


def attend_back_kernel(q_ref, k_ref, v_ref, bias_ref, hot_ref, lse_ref, g_ref, dq_ref, dk_ref, dv_ref, qa, ka, ak, av):
    seq = q_ref.shape[2]
    head = q_ref.shape[1]
    scale = 1.0 / math.sqrt(head)
    blocks = bias_ref.shape[2]
    step = min(256, seq)
    qa[0:head, :] = (q_ref[0].astype(F32) * scale).astype(BF16)
    qa[head : head + blocks, :] = bias_ref[0, 0]
    low = lax.broadcasted_iota(jnp.int32, (qa.shape[0] - head - blocks, seq), 0)
    qa[head + blocks :, :] = jnp.where(low == 0, NEG, 0.0).astype(BF16)
    ka[0:head, :] = k_ref[0]
    ka[head:, :] = hot_ref[...]
    for i in range(seq // step):
        cols = slice(i * step, (i + 1) * step)
        scores = lax.dot_general(ka[...], qa[:, cols], (((0,), (0,)), ((), ())), preferred_element_type=F32)
        probs = jnp.exp(scores - lse_ref[0, 0, :, cols])
        grad = g_ref[0, :, cols]
        grad_probs = lax.dot_general(v_ref[0], grad, (((0,), (0,)), ((), ())), preferred_element_type=F32)
        inner = jnp.sum(probs * grad_probs, 0, keepdims=True)
        grad_scores = (probs * (grad_probs - inner)).astype(BF16)
        dq_ref[0, :, cols] = (jnp.dot(k_ref[0], grad_scores, preferred_element_type=F32) * scale).astype(BF16)
        gk = lax.dot_general(qa[0:head, cols], grad_scores, (((1,), (1,)), ((), ())), preferred_element_type=F32)
        gv = lax.dot_general(grad, probs.astype(BF16), (((1,), (1,)), ((), ())), preferred_element_type=F32)
        if i == 0:
            ak[...] = gk
            av[...] = gv
        else:
            ak[...] += gk
            av[...] += gv
    dk_ref[0] = ak[...].astype(BF16)
    dv_ref[0] = av[...].astype(BF16)


def attend_back(qkv, bias, hot, lse, grad, head):
    groups, width, seq = qkv.shape
    per = width // (3 * head)
    rows, bias_spec, hot_spec, line, out = head_specs(head, seq, per, bias.shape[2], hot.shape[0])
    deep = head + hot.shape[0]
    return pl.pallas_call(
        attend_back_kernel,
        name="attend_back",
        grid=(groups, per),
        out_shape=[jax.ShapeDtypeStruct((groups, per * head, seq), BF16)] * 3,
        in_specs=rows + [bias_spec, hot_spec, line, out],
        out_specs=[out] * 3,
        scratch_shapes=[
            pltpu.VMEM((deep, seq), BF16),
            pltpu.VMEM((deep, seq), BF16),
            pltpu.VMEM((head, seq), F32),
            pltpu.VMEM((head, seq), F32),
        ],
        compiler_params=pltpu.CompilerParams(vmem_limit_bytes=48 << 20),
    )(qkv, qkv, qkv, bias, hot, lse, grad)


def fetch_plain(dp, mp, tok, cot, pa, pb, pc, vec):
    d, m = lax.axis_index("dp"), lax.axis_index("mp")
    core = d % 2
    swap = [(i, i ^ 1) for i in range(dp)]

    def sequence(rows):
        whole = lax.all_gather(rows, "mp", axis=1, tiled=True)
        other = lax.ppermute(whole, "dp", swap)
        return jnp.where(m // 2 == core, whole, other)[m % 2]

    def weight(part):
        plane = lax.all_gather(part, "dp", axis=0, tiled=True)
        return lax.dynamic_slice_in_dim(lax.all_gather(plane, "mp"), 2 * core, 2, 0)

    half = tok.shape[1] * mp // 2
    ct = lax.dynamic_slice_in_dim(sequence(cot), core * half, half, 0)
    return (
        sequence(tok), ct, weight(pa), weight(pb), weight(pc), lax.all_gather(vec, "dp"), lax.all_gather(vec, "mp"),
    )


def deliver_plain(dp, mp, da, db, dc, out, gtok, rows, quarter):
    d, m = lax.axis_index("dp"), lax.axis_index("mp")
    core = d % 2
    swap = [(i, i ^ 1) for i in range(dp)]

    def grad(part):
        wide = jnp.zeros((mp,) + part.shape[1:], F32)
        wide = lax.dynamic_update_slice_in_dim(wide, part.astype(F32), 2 * core, 0)
        mine = lax.psum_scatter(wide, "mp", scatter_dimension=0, tiled=True)[0]
        return lax.psum_scatter(mine, "dp", scatter_dimension=0, tiled=True)[None]

    def home(half):
        both = jnp.zeros((2,) + half.shape, half.dtype)
        both = lax.dynamic_update_slice_in_dim(both, half[None], core, 0)
        both = lax.dynamic_update_slice_in_dim(both, lax.ppermute(half, "dp", swap)[None], 1 - core, 0)
        all_rows = lax.all_gather(both.reshape(mp, quarter, -1), "mp")
        mine = lax.dynamic_slice_in_dim(all_rows, 2 * core, 2, 0)
        return lax.dynamic_slice_in_dim(mine, m, 1, 1)[:, 0]

    return grad(da), grad(db), grad(dc), home(out), home(gtok)


def layer_plain(
    dp, mp, tokens, cotangent, w_query, w_key, w_value, w_out, w_inner, w_outer,
    gain_attn, shift_attn, gain_ffn, shift_ffn, seq_lengths, rand_blocks,
):
    d, m = lax.axis_index("dp"), lax.axis_index("mp")
    core = d % 2
    swap = [(i, i ^ 1) for i in range(dp)]
    quarter, width = tokens.shape[1:]
    seq = quarter * mp
    half = seq // 2
    per, nblocks, picks = rand_blocks.shape
    cols = w_query.shape[1]
    head = cols // per
    block = seq // nblocks
    rows = w_query.shape[0]
    vec_rows = [v.astype(F32) for v in (gain_attn, shift_attn, gain_ffn, shift_ffn)]
    vec_rows += [seq_lengths.astype(F32)]
    flat = rand_blocks.astype(F32).reshape(-1)
    vec_rows += [flat[:128], flat[128:]]
    vec = jnp.stack([jnp.pad(v, (0, 128 - v.shape[0])) for v in vec_rows] + [jnp.zeros(128, F32)])
    pa = jnp.concatenate([w_query, w_key, w_value, w_out.T], 1)
    pb, pc = w_inner, w_outer.T
    x, ct, ga, gb, gc, gvd, gvz = fetch_plain(dp, mp, tokens, cotangent, pa, pb, pc, vec)
    norms = jnp.swapaxes(gvd[:, :4, :rows], 0, 1).reshape(4, width)
    g1, b1, g2, b2 = (norms[i][None] for i in range(4))
    owner = d - core + m // 2
    lens = lax.dynamic_slice_in_dim(gvd[:, 4, :2], owner, 1, 0)[0]
    length = jnp.where(m % 2 == 0, lens[0], lens[1]).astype(jnp.int32)
    picked = lax.dynamic_slice_in_dim(gvz, 2 * core, 2, 0)
    picked = picked[:, 5:7].reshape(2, 256)[:, : per * nblocks * picks].astype(jnp.int32)
    picked = picked.reshape(2, per, nblocks, picks)

    r = jnp.arange(nblocks)
    near = (r[:, None] == 0) | (r[:, None] == nblocks - 1) | (r[None] == 0) | (r[None] == nblocks - 1)
    near = near | (jnp.abs(r[:, None] - r[None]) <= 1)
    hits = jnp.any(picked[:, :, :, :, None] == r, axis=3) | near
    bias = jnp.where(jnp.swapaxes(hits, 2, 3), 0.0, NEG).astype(BF16)
    bias = jnp.repeat(bias, block, axis=3)
    pos = jnp.arange(seq)
    hot = jnp.concatenate([pos[None] // block == r[:, None], pos[None] >= length, jnp.zeros((15, seq), bool)], 0)
    hot = hot.astype(BF16)

    def mine(values):
        return lax.dynamic_slice_in_dim(values, core * half, half, 0)

    def theirs(values):
        return lax.dynamic_slice_in_dim(values, (1 - core) * half, half, 0)

    def pair_sum(partial):
        return mine(partial) + lax.ppermute(theirs(partial).astype(BF16), "dp", swap).astype(F32)

    def pair_join(values):
        other = lax.ppermute(values, "dp", swap)
        lo = jnp.where(core == 0, values, other)
        hi = jnp.where(core == 0, other, values)
        return jnp.concatenate([lo, hi], 0)

    def dot(spec, a, b):
        return jnp.einsum(spec, a, b, preferred_element_type=F32)

    a_qkv, a_out = ga[:, :, : 3 * cols], ga[:, :, 3 * cols :]
    qkv = dot("mrc,tr->mct", a_qkv, x).astype(BF16)
    ctx, lse = attend(qkv, bias, hot, head)
    attn = pair_sum(dot("mct,mdc->td", ctx, a_out))
    x_mine = mine(x).astype(F32)

    def norm(z):
        centre = z - jnp.mean(z, -1, keepdims=True)
        inv = lax.rsqrt(jnp.mean(centre * centre, -1, keepdims=True) + EPS)
        return centre * inv, inv

    n1, inv1 = norm(x_mine + attn)
    hidden = n1 * g1 + b1
    hidden_b = pair_join(hidden.astype(BF16))
    inner = dot("td,mdk->tmk", hidden_b, gb)
    cumul = 0.5 * (1.0 + lax.erf(inner * (1.0 / math.sqrt(2.0))))
    active = (inner * cumul).astype(BF16)
    slope = cumul + inner * jnp.exp(-0.5 * inner * inner) * (1.0 / math.sqrt(2.0 * math.pi))
    n2, inv2 = norm(hidden + pair_sum(dot("tmk,mdk->td", active, gc)))
    valid = (core * half + jnp.arange(half) < length).astype(F32)[:, None]
    out = ((n2 * g2 + b2) * valid).astype(BF16)

    def norm_back(e, n, inv):
        return (e - jnp.mean(e, -1, keepdims=True) - n * jnp.mean(e * n, -1, keepdims=True)) * inv

    gy = ct.astype(F32) * valid
    g_mid = norm_back(gy * g2, n2, inv2)
    d_gain2, d_shift2 = jnp.sum(gy * n2, 0), jnp.sum(gy, 0)
    g_ffn = pair_join(g_mid.astype(BF16))
    d_c = dot("td,tmk->mdk", g_ffn, active).astype(BF16)
    g_inner = (dot("td,mdk->tmk", g_ffn, gc) * slope).astype(BF16)
    d_b = dot("td,tmk->mdk", hidden_b, g_inner).astype(BF16)
    g_hidden = g_mid + pair_sum(dot("tmk,mdk->td", g_inner, gb))
    d_gain1, d_shift1 = jnp.sum(g_hidden * n1, 0), jnp.sum(g_hidden, 0)
    g_res = norm_back(g_hidden * g1, n1, inv1)
    g_attn = pair_join(g_res.astype(BF16))
    d_out = dot("td,mct->mdc", g_attn, ctx).astype(BF16)
    g_ctx = dot("td,mdc->mct", g_attn, a_out).astype(BF16)
    sums = jnp.stack([d_gain1, d_shift1, d_gain2, d_shift2] + [jnp.zeros_like(d_gain1)] * 4)
    dq, dk, dv = attend_back(qkv, bias, hot, lse, g_ctx, head)
    dqkv = jnp.concatenate([dq, dk, dv], 1)
    d_qkv = dot("tr,mct->mrc", x, dqkv).astype(BF16)
    d_a = jnp.concatenate([d_qkv, d_out], 2)
    gtok = (g_res + pair_sum(dot("mct,mrc->tr", dqkv, a_qkv))).astype(BF16)
    ra, rb, rc, out, gtok = deliver_plain(dp, mp, d_a, d_b, d_c, out, gtok, rows, quarter)
    sums = lax.psum(sums, ("dp", "mp"))
    ra, rb, rc = (jnp.sum(v.astype(F32), 0) for v in (ra, rb, rc))
    sums = lax.dynamic_slice_in_dim(sums, d * rows, rows, 1)
    return (
        out, gtok, ra[:, :cols], ra[:, cols : 2 * cols], ra[:, 2 * cols : 3 * cols], ra[:, 3 * cols :].T, rb, rc.T,
        sums[0], sums[1], sums[2], sums[3],
    )


def layer(
    dp, mp, tokens, cotangent, w_query, w_key, w_value, w_out, w_inner, w_outer,
    gain_attn, shift_attn, gain_ffn, shift_ffn, seq_lengths, rand_blocks,
):
    rows, cols = w_query.shape
    per, nblocks, picks = rand_blocks.shape
    if not (dp == 8 and mp == 4 and rows % 16 == 0 and 4 * cols == 8 * rows and tokens.shape[0] == 2):
        return layer_plain(
            dp, mp, tokens, cotangent, w_query, w_key, w_value, w_out, w_inner, w_outer,
            gain_attn, shift_attn, gain_ffn, shift_ffn, seq_lengths, rand_blocks,
        )
    d = lax.axis_index("dp")
    pa = jnp.concatenate([w_query, w_key, w_value, w_out.T], 1)
    lens = jnp.stack([seq_lengths // 32, seq_lengths % 32], 1).reshape(-1).astype(BF16)
    vec = jnp.stack([gain_attn, shift_attn, gain_ffn, shift_ffn, jnp.pad(lens, (0, rows - 4))])
    vec = lax.dynamic_update_slice(jnp.zeros((16, 4 * cols), BF16), vec, (0, d * rows))
    pick = jnp.swapaxes(rand_blocks, 1, 2).reshape(per * picks, nblocks).astype(BF16)
    pick = jnp.pad(pick, ((0, 16 - per * picks), (0, 128 - nblocks)))
    out, gtok, ra, rb, rc, sums = fused_layer(
        mp, tokens, cotangent, pa, w_inner, w_outer.T, vec, pick, cols // per, nblocks, picks
    )
    sums = lax.dynamic_slice_in_dim(sums, d * rows, rows, 1)
    return (
        out, gtok, ra[:, :cols], ra[:, cols : 2 * cols], ra[:, 2 * cols : 3 * cols], ra[:, 3 * cols :].T, rb, rc.T,
        sums[0], sums[1], sums[2], sums[3],
    )


def solution(mesh):
    dp, mp = mesh.shape["dp"], mesh.shape["mp"]
    act, vec = P("dp", "mp", None), P("dp")
    w_in, w_back = P("dp", "mp"), P("mp", "dp")

    def step(*args):
        return layer(dp, mp, *args)

    return jax.shard_map(
        step,
        mesh=mesh,
        in_specs=(act, act, w_in, w_in, w_in, w_back, w_in, w_back, vec, vec, vec, vec, vec, P("mp", None, None)),
        out_specs=(act, act, w_in, w_in, w_in, w_back, w_in, w_back, vec, vec, vec, vec),
        check_vma=False,
    )
```

```python
import math

import jax
import jax.numpy as jnp
from jax import lax
from jax.experimental import pallas as pl
from jax.experimental.pallas import tpu as pltpu
from jax.sharding import PartitionSpec as P

EPS = 1e-06
NEG = -1000000000.0
MESH = pl.DeviceIdType.MESH
F32 = jnp.float32
BF16 = jnp.bfloat16
ANY = pl.BlockSpec(memory_space=pl.ANY)
VMEM = pl.BlockSpec(memory_space=pltpu.VMEM)
DMA = pltpu.SemaphoreType.DMA


class Place:
    def __init__(self):
        self.d = lax.axis_index("dp")
        self.m = lax.axis_index("mp")
        self.c = lax.rem(self.d, 2)
        self.base = self.d - self.c
        self.sib = self.d + 1 - 2 * self.c
        bx = lax.rem(lax.div(self.d, 2), 2)
        by = lax.rem(lax.div(self.d, 4), 2)
        self.xp = self.d + 2 - 4 * bx
        self.yp = self.d + 4 - 8 * by
        self.bx = self.xp - self.c
        self.by = self.yp - self.c
        self.bd = self.bx + 4 - 8 * by
        self.h = lax.div(self.m, 2)
        self.a = lax.rem(self.m, 2)
        self.close = self.h == self.c
        self.inner = jnp.logical_and(self.h != self.c, self.a + self.h == 1)
        self.outer = jnp.logical_and(self.h != self.c, self.a + self.h != 1)


def remote(src, dst, ssem, rsem, dev):
    return pltpu.make_async_remote_copy(
        src_ref=src, dst_ref=dst, send_sem=ssem, recv_sem=rsem, device_id=dev, device_id_type=MESH
    )


def push(src, dst, ssem, rsem, dev, same):
    @pl.when(same)
    def _():
        pltpu.make_async_copy(src, dst, rsem).start()

    @pl.when(jnp.logical_not(same))
    def _():
        remote(src, dst, ssem, rsem, dev).start()


def pushed(src, dst, ssem, rsem, dev, same):
    @pl.when(jnp.logical_not(same))
    def _():
        remote(src, dst, ssem, rsem, dev).wait_send()


def got(dst, ssem, rsem, dev):
    remote(dst, dst, ssem, rsem, dev).wait_recv()


def greet(peers):
    barrier = pltpu.get_barrier_semaphore()
    for dev in peers:
        pl.semaphore_signal(barrier, inc=1, device_id=dev, device_id_type=MESH)
    pl.semaphore_wait(barrier, len(peers))


def dots(a, b, ca, cb):
    return lax.dot_general(a, b, (((ca,), (cb,)), ((), ())), preferred_element_type=F32)


def column_peers(p, mp):
    peers = []
    for k in range(1, mp):
        z = lax.rem(p.m + k, mp)
        peers += [(p.base, z), (p.base + 1, z)]
    return peers


class Gather:
    def __init__(self, p, src, dst, first, count, sems):
        self.p, self.src, self.dst = p, src, dst
        self.zs, self.zr, self.fs, self.fr, self.xs, self.xr, self.ys, self.yr = sems
        self.n = src.shape[0]
        self.cols = pl.ds(first, count)

    def rows(self, a, first, count):
        return self.dst.at[a, pl.ds(first * self.n, count * self.n), self.cols]

    def both(self, first):
        return self.dst.at[:, pl.ds(first * self.n, 2 * self.n), self.cols]

    def z_args(self, k):
        p = self.p
        z = (p.m, p.m + 1 - 2 * p.a, 2 - p.h)[k]
        src = self.src.at[:, self.cols]
        return src, self.rows(p.a, p.d, 1), self.zs.at[k], self.zr.at[2 * p.c + p.a], (p.base + p.h, z)

    def z_send(self):
        for k in (2, 1):
            remote(*self.z_args(k)).start()
        push(*self.z_args(0), self.p.close)

    def pass_on(self):
        p = self.p
        part = self.both(p.base)
        return remote(part, part, self.fs.at[0], self.fr.at[0], (p.d, 3 * p.h))

    def z_mid(self):
        p = self.p

        @pl.when(jnp.logical_not(p.outer))
        def _():
            for core in range(2):
                for a in range(2):
                    got(self.rows(a, p.base + core, 1), self.zs.at[0], self.zr.at[2 * core + a], (p.d, p.m))

        @pl.when(p.inner)
        def _():
            self.pass_on().start()

        @pl.when(p.outer)
        def _():
            self.pass_on().wait_recv()

        self.hop(0, 0).start()
        self.hop(1, 0).start()

    def hop(self, axis, step):
        p = self.p
        peer = p.xp if axis == 0 else p.yp
        s, r = (self.xs, self.xr) if axis == 0 else (self.ys, self.yr)
        part = self.both(p.base) if step == 0 else self.rows(1 - axis, p.by if axis == 0 else p.bx, 2)
        return remote(part, part, s.at[step], r.at[step], (peer, p.m))

    def arrived(self, axis, step):
        p = self.p
        s, r = (self.xs, self.xr) if axis == 0 else (self.ys, self.yr)
        part = self.both(p.bx if axis == 0 else p.by) if step == 0 else self.rows(1 - axis, p.bd, 2)
        got(part, s.at[step], r.at[step], (p.d, p.m))

    def forward(self):
        for axis in range(2):
            self.arrived(axis, 0)
            self.hop(1 - axis, 1).start()

    def land(self):
        self.arrived(1, 1)
        self.arrived(0, 1)

    def finish(self):
        for k in (1, 2):
            remote(*self.z_args(k)).wait_send()
        pushed(*self.z_args(0), self.p.close)

        @pl.when(self.p.inner)
        def _():
            self.pass_on().wait_send()

        for axis in range(2):
            for step in range(2):
                self.hop(axis, step).wait_send()


def gather_sems():
    return [DMA((3,)), DMA((4,)), DMA((1,)), DMA((1,)), DMA((2,)), DMA((2,)), DMA((2,)), DMA((2,))]


class Tokens:
    def __init__(self, p, tok, x, sems):
        self.p, self.tok, self.x = p, tok, x
        self.s, self.r, self.fs, self.fr = sems
        self.piece = tok.shape[1] // 2

    def args(self, i, half):
        p, n = self.p, self.piece
        z = 2 * p.c + i
        dev = (p.base + half, z)
        dst = self.x.at[pl.ds((2 * p.m + half) * n, n), :]
        src = self.tok.at[i, pl.ds(half * n, n), :]
        return (src, dst, self.s.at[2 * i + half], self.r.at[p.m], dev), jnp.logical_and(p.c == half, p.m == z)

    def send(self):
        for i in range(2):
            for half in range(2):
                args, same = self.args(i, half)
                push(*args, same)

    def part(self, q, core):
        return self.x.at[pl.ds((2 * q + core) * self.piece, self.piece), :]

    def forward(self, mp):
        p = self.p
        for q in range(mp):
            got(self.part(q, p.c), self.s.at[0], self.r.at[q], (p.d, p.m))
            remote(self.part(q, p.c), self.part(q, p.c), self.fs.at[q], self.fr.at[q], (p.sib, p.m)).start()

    def land(self, mp):
        p = self.p
        for q in range(mp):
            got(self.part(q, 1 - p.c), self.fs.at[q], self.fr.at[q], (p.d, p.m))

    def finish(self, mp):
        p = self.p
        for q in range(mp):
            remote(self.part(q, p.c), self.part(q, p.c), self.fs.at[q], self.fr.at[q], (p.sib, p.m)).wait_send()
        for i in range(2):
            for half in range(2):
                args, same = self.args(i, half)
                pushed(*args, same)


class Quarters:
    def __init__(self, p, src, dst, sems):
        self.p, self.src, self.dst = p, src, dst
        self.s, self.r = sems
        self.n = src.shape[1]

    def args(self, i):
        p = self.p
        z = 2 * p.c + i
        dst = self.dst.at[pl.ds(p.a * self.n, self.n), :]
        same = jnp.logical_and(p.h == p.c, p.m == z)
        return (self.src.at[i], dst, self.s.at[i], self.r.at[p.a], (p.base + p.h, z)), same

    def send(self):
        for i in range(2):
            args, same = self.args(i)
            push(*args, same)

    def finish(self):
        p = self.p
        for a in range(2):
            got(self.dst.at[pl.ds(a * self.n, self.n), :], self.s.at[a], self.r.at[a], (p.d, p.m))
        for i in range(2):
            args, same = self.args(i)
            pushed(*args, same)


class Homewards:
    def __init__(self, p, src, dst, sems):
        self.p, self.src, self.dst = p, src, dst
        self.s, self.r = sems
        self.n = dst.shape[1]

    def args(self, q):
        p = self.p
        src = self.src.at[pl.ds(q * self.n, self.n), :]
        owner = p.base + p.h
        same = jnp.logical_and(owner == p.d, p.m == 2 * p.c + q)
        return (src, self.dst.at[p.a], self.s.at[q], self.r.at[p.a], (owner, 2 * p.c + q)), same

    def send(self, q):
        args, same = self.args(q)
        push(*args, same)

    def finish(self):
        p = self.p
        for i in range(2):
            got(self.dst.at[i], self.s.at[i], self.r.at[i], (p.d, p.m))
        for q in range(2):
            args, same = self.args(q)
            pushed(*args, same)


class Scatter:
    def __init__(self, p, src, out, halves, first, count, axis, bufs, sems):
        self.p, self.src, self.out, self.halves = p, src, out, halves
        self.r1, self.r2, self.r3, self.total, self.met = bufs
        self.s, self.r, self.zs, self.zr = sems
        self.n = out.shape[1]
        self.first, self.count = first, count
        self.cols = pl.ds(first, count)
        self.near, self.far = ((p.xp, p.bx), (p.yp, p.by)) if axis == 0 else ((p.yp, p.by), (p.xp, p.bx))

    def rows(self, first):
        return self.src.at[pl.ds(self.halves[0], len(self.halves)), pl.ds(first * self.n, 2 * self.n), self.cols]

    def hop(self, kind):
        p = self.p
        if kind == 0:
            src, dst, peer = self.rows(p.bd), self.r1, self.near[0]
        elif kind == 1:
            src, dst, peer = self.rows(self.near[1]), self.r2, self.near[0]
        else:
            src, dst, peer = self.r1, self.r3, self.far[0]
        return remote(src, dst, self.s.at[kind], self.r.at[kind], (peer, p.m))

    def second(self):
        self.hop(0).wait_recv()
        self.r1[...] = (self.rows(self.far[1])[...].astype(F32) + self.r1[...].astype(F32)).astype(BF16)
        self.hop(2).start()

    def third(self):
        p = self.p
        self.hop(1).wait_recv()
        self.hop(2).wait_recv()
        self.total[...] = (
            self.rows(p.base)[...].astype(F32) + self.r2[...].astype(F32) + self.r3[...].astype(F32)
        ).astype(BF16)

        @pl.when(p.close)
        def _():
            for args in self.z_args():
                push(*args)

        @pl.when(p.outer)
        def _():
            self.meet().start()

    def meet(self):
        p = self.p
        return remote(self.total, self.met, self.zs.at[0], self.zr.at[3], (p.d, 1 + p.h))

    def z_args(self):
        p = self.p
        slot = jnp.where(p.close, p.a, 2)
        made = []
        for i, a in enumerate(self.halves):
            for core in range(2):
                same = jnp.logical_and(p.c == core, p.m == 2 * p.c + a)
                src = self.total.at[i, pl.ds(core * self.n, self.n), :]
                dst = self.out.at[slot, :, self.cols]
                made.append((src, dst, self.zs.at[2 * i + core], self.zr.at[slot], (p.base + core, 2 * p.c + a), same))
        return made

    def line(self):
        @pl.when(self.p.inner)
        def _():
            self.meet().wait_recv()
            self.total[...] = (self.total[...].astype(F32) + self.met[...].astype(F32)).astype(BF16)
            for args in self.z_args():
                remote(*args[:-1]).start()

    def owned(self):
        for slot in range(3):
            got(self.out.at[slot, :, self.cols], self.zs.at[0], self.zr.at[slot], (self.p.d, self.p.m))

    def finish(self):
        p = self.p
        for kind in range(3):
            self.hop(kind).wait_send()

        @pl.when(p.outer)
        def _():
            self.meet().wait_send()

        @pl.when(p.close)
        def _():
            for args in self.z_args():
                pushed(*args)

        @pl.when(p.inner)
        def _():
            for args in self.z_args():
                remote(*args[:-1]).wait_send()


def start_all(units):
    for kind in range(2):
        for u in units:
            u.hop(kind).start()


class Sums:
    def __init__(self, p, out, bufs, sems, mp):
        self.p, self.out, self.mp = p, out, mp
        self.mine, self.came, self.parts = bufs
        self.s, self.r, self.zs, self.zr = sems

    def hop(self, i):
        p = self.p
        dev = (p.sib, p.xp, p.yp)[i]
        return remote(self.mine.at[i], self.came.at[i], self.s.at[i], self.r.at[i], (dev, p.m))

    def start(self, values):
        self.mine[0] = values
        self.hop(0).start()

    def step(self, i):
        self.hop(i).wait_recv()
        total = self.mine[i] + self.came[i]
        if i < 2:
            self.mine[i + 1] = total
            self.hop(i + 1).start()
        else:
            self.parts[self.p.m] = total
            for k in range(1, self.mp):
                self.column(k).start()

    def column(self, k):
        p = self.p
        part = self.parts.at[p.m]
        return remote(part, part, self.zs.at[k - 1], self.zr.at[p.m], (p.d, lax.rem(p.m + k, self.mp)))

    def finish(self):
        p = self.p
        for k in range(1, self.mp):
            z = lax.rem(p.m + k, self.mp)
            got(self.parts.at[z], self.zs.at[0], self.zr.at[z], (p.d, p.m))
        total = self.parts[0]
        for z in range(1, self.mp):
            total = total + self.parts[z]
        self.out[...] = total
        for i in range(3):
            self.hop(i).wait_send()
        for k in range(1, self.mp):
            self.column(k).wait_send()


class Swap:
    def __init__(self, p, src, dst, sems, src_first=0, dst_first=0, came_first=0, count=256):
        self.p, self.src, self.dst = p, src, dst
        self.s, self.r = sems
        self.firsts = (src_first, dst_first, came_first)
        self.n = count

    def copy(self, i, side):
        p, n = self.p, self.n
        src_first, dst_first, came_first = self.firsts
        if side == 0:
            src = self.src.at[pl.ds(src_first + i * n, n), :]
            dst = self.dst.at[pl.ds(dst_first + i * n, n), :]
        else:
            src = dst = self.dst.at[pl.ds(came_first + i * n, n), :]
        return remote(src, dst, self.s.at[i], self.r.at[i], (p.sib, p.m))

    def send(self, i):
        self.copy(i, 0).start()

    def recv(self, i):
        self.copy(i, 1).wait_recv()

    def finish(self):
        for i in range(2):
            self.copy(i, 0).wait_send()


def gelu_pair(inner):
    cumul = 0.5 * (1.0 + lax.erf(inner * (1.0 / math.sqrt(2.0))))
    slope = cumul + inner * jnp.exp(-0.5 * inner * inner) * (1.0 / math.sqrt(2.0 * math.pi))
    return inner * cumul, slope


def norm_back(e, n, inv):
    return (e - jnp.mean(e, -1, keepdims=True) - n * jnp.mean(e * n, -1, keepdims=True)) * inv


def norm_rows(z):
    centre = z - jnp.mean(z, -1, keepdims=True)
    inv = lax.rsqrt(jnp.mean(centre * centre, -1, keepdims=True) + EPS)
    return centre * inv, inv


def layer_kernel(mp, head, nblocks, picks, names, *refs):
    r = dict(zip(names, refs, strict=True))
    p = Place()
    x, ga, gb, gc, at, qkv, ctx, gctx = (r[k] for k in ("x", "ga", "gb", "gc", "at", "qkv", "ctx", "gctx"))
    seq, width = x.shape
    half = seq // 2
    rc = half // 2
    group = qkv.shape[0] // 2
    cols = group // 3
    per = cols // head
    heads = 2 * per
    n = r["pa"].shape[0]
    scale = 1.0 / math.sqrt(head)
    mine = pl.multiple_of(p.c * half, half)
    theirs = pl.multiple_of(half - p.c * half, half)
    hw = width // 2

    def sems(key):
        return [v for k, v in r.items() if k.startswith(key + ".")]

    tokens = Tokens(p, r["tok"], x, sems("tok"))
    cots = Quarters(p, r["cot"], r["ct"], sems("cot"))
    each = 4 * head
    ga_parts = [Gather(p, r["pa"], ga, i * each, each, sems(f"ga{i}")) for i in range(per)]
    b0, b1, c0, c1 = (
        Gather(p, r["p" + w], r["g" + w], i * hw, hw, sems(f"g{w}{i}")) for w in "bc" for i in range(2)
    )
    gathers = ga_parts + [b0, b1, c0, c1]
    plane = [lax.rem(p.d + k, 8) for k in range(1, 8)]
    vec, pick, gvec, gpick = r["vec"], r["pick"], r["gvec"], r["gpick"]
    vs, vr, us, ur = sems("vec")
    sums = Sums(p, r["sums"], sems("sumbuf"), sems("sum"), mp)
    home = Homewards(p, r["outb"], r["hout"], sems("home"))
    home_g = Homewards(p, r["gtokb"], r["hgtok"], sems("homeg"))
    pair_attn = Swap(p, r["send"], r["recv"], sems("sw0"), count=rc)
    pair_hid = Swap(p, r["hb"], r["hb"], sems("sw1"), mine, mine, theirs, rc)
    pair_ffn = Swap(p, r["send1"], r["recv1"], sems("sw2"), count=rc)
    pair_gf = Swap(p, r["gf"], r["gf"], sems("sw3"), mine, mine, theirs, rc)
    pair_gh = Swap(p, r["send"], r["recv"], sems("sw4"), count=rc)
    pair_ga = Swap(p, r["gat"], r["gat"], sems("sw5"), mine, mine, theirs, rc)
    pair_gt = Swap(p, r["send1"], r["recv1"], sems("sw6"), count=rc)

    def unit(name, src, halves, first, count, axis):
        return Scatter(p, src, r["l" + name[0]], halves, first, count, axis, sems(f"s{name}b"), sems(f"s{name}s"))

    ua = [unit(f"a{i}", ga, (i % 2,), (i // 2) * each, each, i % 2) for i in range(heads)]
    ub, uc = ([unit(f"{w}{i}", r["d" + w], (0, 1), i * hw, hw, i) for i in range(2)] for w in "bc")

    greet(column_peers(p, mp) + [(d, p.m) for d in plane])
    pcopies = [remote(pick, gpick.at[p.m], us.at[k - 1], ur.at[p.m], (p.d, lax.rem(p.m + k, mp))) for k in range(1, mp)]
    pcopies.append(remote(pick, gpick.at[mp], us.at[mp - 1], ur.at[mp], (p.sib, p.m)))
    mine_too = pltpu.make_async_copy(pick, gpick.at[p.m], ur.at[p.m])
    for copy in pcopies + [mine_too]:
        copy.start()
    for g in ga_parts:
        g.z_send()
    b0.z_send()
    pl.when(jnp.logical_not(p.inner))(tokens.send)
    vcopies = [remote(vec, gvec.at[p.d], vs.at[k], vr.at[p.d], (d, p.m)) for k, d in enumerate(plane)]
    vcopies.append(pltpu.make_async_copy(vec, gvec.at[p.d], vr.at[p.d]))
    for g in ga_parts:
        g.z_mid()
    b0.z_mid()
    pl.when(p.inner)(tokens.send)
    for copy in vcopies:
        copy.start()

    for z in range(mp + 1):
        got(gpick.at[z], us.at[0], ur.at[z], (p.d, p.m))
    row = jnp.where(p.close, gpick[p.m, 15:16, :].astype(F32), gpick[mp, 15:16, :].astype(F32))
    lane = lax.broadcasted_iota(jnp.int32, (1, 128), 1)
    high, low = (jnp.sum(jnp.where(lane == 2 * p.a + i, row, 0.0), 1, keepdims=True) for i in range(2))
    length = high * 32.0 + low
    block = seq // nblocks
    sub = lax.broadcasted_iota(jnp.int32, (nblocks, seq), 0)
    place = lax.broadcasted_iota(jnp.int32, (nblocks, seq), 1)
    rb = lax.div(place, block)
    near = (rb == 0) | (rb == nblocks - 1) | (sub == 0) | (sub == nblocks - 1) | (jnp.abs(rb - sub) <= 1)
    spread = lax.broadcasted_iota(jnp.int32, (128, seq), 0) == lax.div(lax.broadcasted_iota(jnp.int32, (128, seq), 1), block)
    spread = jnp.where(spread, 1.0, 0.0).astype(BF16)
    subf = sub.astype(F32)
    for a in range(2):
        wide = dots(gpick[2 * p.c + a], spread, 1, 0)
        for h in range(per):
            hit = near
            for j in range(picks):
                at_row = h * picks + j
                hit = hit | (wide[at_row : at_row + 1] == subf)
            r["bias"][2 * h + a] = jnp.where(hit, 0.0, NEG).astype(BF16)
    qa, ka = r["qa"], r["ka"]
    low = lax.broadcasted_iota(jnp.int32, (16, seq), 0)
    ka[head : head + nblocks, :] = jnp.where(rb == sub, 1.0, 0.0).astype(BF16)
    beyond = lax.broadcasted_iota(jnp.int32, (16, seq), 1).astype(F32) >= length
    ka[head + nblocks :, :] = jnp.where((low == 0) & beyond, 1.0, 0.0).astype(BF16)
    qa[head + nblocks :, :] = jnp.where(low == 0, NEG, 0.0).astype(BF16)

    for g in ga_parts:
        g.forward()
    tokens.forward(mp)
    b1.z_send()
    c0.z_send()
    tokens.land(mp)

    def project(h):
        span = pl.ds(pl.multiple_of(h * each, each), each)
        for a in range(2):
            at[a, span, :] = ga[a, :, span].T
        own_rows = pl.ds(pl.multiple_of(h * each, each), 3 * head)

        def some(j, _):
            rows = pl.ds(pl.multiple_of(j * rc, rc), rc)
            for a in range(2):
                to = pl.ds(pl.multiple_of((2 * h + a) * 3 * head, head), 3 * head)
                qkv[to, rows] = dots(at[a, own_rows, :], x[rows, :], 1, 1).astype(BF16)
            return 0

        lax.fori_loop(0, seq // rc, some, 0)

    def parts(i):
        return [pl.ds(pl.multiple_of((3 * i + part) * head, head), head) for part in range(3)]

    def set_head(i):
        q, k, v = parts(i)
        qa[0:head, :] = (qkv[q, :].astype(F32) * scale).astype(BF16)
        qa[head : head + nblocks, :] = r["bias"][i]
        ka[0:head, :] = qkv[k, :]
        return q, k, v

    def attend_head(i, _):
        for h in range(per):

            @pl.when(i == 2 * h)
            def _():
                ga_parts[h].land()

        @pl.when(lax.rem(i, 2) == 0)
        def _():
            project(lax.div(i, 2))

        q, k, v = set_head(i)
        own_rows = pl.ds(pl.multiple_of(i * head, head), head)
        for j in range(2):
            span = slice(j * half, (j + 1) * half)
            scores = dots(ka[...], qa[:, span], 0, 0)
            peak = jnp.max(scores, 0, keepdims=True)
            weights = jnp.exp(scores - peak)
            total = jnp.sum(weights, 0, keepdims=True)
            mixed = jnp.dot(qkv[v, :], weights.astype(BF16), preferred_element_type=F32)
            ctx[own_rows, span] = (mixed / total).astype(BF16)
            r["lse"][i, :, span] = peak + jnp.log(total)

        @pl.when(i == 0)
        def _():
            b1.z_mid()
            c1.z_send()
            b0.forward()

        @pl.when(i == 3)
        def _():
            c0.z_mid()

        @pl.when(i == 5)
        def _():
            b1.forward()
            c1.z_mid()
            cots.send()

        return 0

    lax.fori_loop(0, heads, attend_head, 0)

    wo = r["wo"]
    for i in range(heads):
        wo[i * head : (i + 1) * head, :] = at[i % 2, (i // 2) * each + 3 * head : (i // 2 + 1) * each, :]
    norms = r["norms"]
    for d in range(8):
        got(gvec.at[d], vs.at[0], vr.at[d], (p.d, p.m))
    vecs = gvec[0].astype(F32)
    for d in range(1, 8):
        vecs = vecs + gvec[d].astype(F32)
    norms[...] = vecs
    g1, s1, g2, s2 = (norms[i : i + 1] for i in range(4))

    def attn_part(first):
        return dots(ctx[:, pl.ds(first, rc)], wo[...], 0, 0)

    for i in range(2):
        r["send"][i * rc : (i + 1) * rc, :] = attn_part(pl.multiple_of(theirs + i * rc, rc)).astype(BF16)
        pair_attn.send(i)
    c0.forward()
    for i in range(2):
        rows = pl.ds(pl.multiple_of(mine + i * rc, rc), rc)
        here = slice(i * rc, (i + 1) * rc)
        part = attn_part(pl.multiple_of(mine + i * rc, rc))
        pair_attn.recv(i)
        n1, inv = norm_rows(x[rows, :].astype(F32) + part + r["recv"][here, :].astype(F32))
        hidden = n1 * g1 + s1
        r["n1"][here, :] = n1
        r["inv1"][here, :] = jnp.broadcast_to(inv, (rc, 128))
        r["res"][here, :] = hidden
        r["hb"][rows, :] = hidden.astype(BF16)
        pair_hid.send(i)

    b0.land()
    b1.land()

    def up(i, _):
        for k in range(2):

            @pl.when(i == 2 + k)
            def _():
                pair_hid.recv(k)

        rows = pl.ds(pl.multiple_of(lax.rem(2 * p.c + i, 4) * rc, rc), rc)
        for a in range(2):
            active, slope = gelu_pair(dots(r["hb"][rows, :], gb[a], 1, 0))
            r["act"][rows, a * width : (a + 1) * width] = active.astype(BF16)
            r["slope"][rows, a * width : (a + 1) * width] = slope.astype(BF16)
        return 0

    lax.fori_loop(0, 4, up, 0)
    c1.forward()
    c0.land()
    c1.land()

    def ffn_part(rows):
        return dots(r["act"][rows, :width], gc[0], 1, 1) + dots(r["act"][rows, width:], gc[1], 1, 1)

    for i in range(2):
        r["send1"][i * rc : (i + 1) * rc, :] = ffn_part(pl.ds(pl.multiple_of(theirs + i * rc, rc), rc)).astype(BF16)
        pair_ffn.send(i)
    cots.finish()
    small = r["small"]
    small[...] = jnp.zeros_like(small)
    for i in range(2):
        rows = pl.ds(pl.multiple_of(mine + i * rc, rc), rc)
        here = slice(i * rc, (i + 1) * rc)
        part = ffn_part(rows)
        pair_ffn.recv(i)
        n2, inv = norm_rows(r["res"][here, :] + part + r["recv1"][here, :].astype(F32))
        pos = (lax.broadcasted_iota(jnp.int32, (rc, 1), 0) + (mine + i * rc)).astype(F32)
        valid = jnp.where(pos < length, 1.0, 0.0)
        r["outb"][here, :] = ((n2 * g2 + s2) * valid).astype(BF16)
        gy = r["ct"][here, :].astype(F32) * valid
        small[2:3, :] += jnp.sum(gy * n2, 0, keepdims=True)
        small[3:4, :] += jnp.sum(gy, 0, keepdims=True)
        g_mid = norm_back(gy * g2, n2, inv)
        r["res"][here, :] = g_mid
        r["gf"][rows, :] = g_mid.astype(BF16)
        pair_gf.send(i)
        home.send(i)

    for g in gathers:
        g.finish()
    for swap in (pair_attn, pair_hid, pair_ffn, pair_gf):
        swap.finish()
    for i in range(2):
        pair_gf.recv(i)

    for k in range(2):

        def grad_c(j, _):
            span = pl.ds(pl.multiple_of(j * rc, rc), rc)
            for a in range(2):
                first = a * width + k * hw
                r["dc"][a, span, k * hw : (k + 1) * hw] = dots(
                    r["gf"][:, span], r["act"][:, first : first + hw], 0, 0
                ).astype(BF16)
            return 0

        lax.fori_loop(0, width // rc, grad_c, 0)
        start_all([uc[k]])

    def back(i, _):
        rows = pl.ds(pl.multiple_of(i * rc, rc), rc)
        for a in range(2):
            part = (rows, slice(a * width, (a + 1) * width))
            r["slope"][part] = (dots(r["gf"][rows, :], gc[a], 1, 0) * r["slope"][part].astype(F32)).astype(BF16)
        return 0

    lax.fori_loop(0, 4, back, 0)

    def hid_part(rows):
        return dots(r["slope"][rows, :width], gb[0], 1, 1) + dots(r["slope"][rows, width:], gb[1], 1, 1)

    for i in range(2):
        r["send"][i * rc : (i + 1) * rc, :] = hid_part(pl.ds(pl.multiple_of(theirs + i * rc, rc), rc)).astype(BF16)
        pair_gh.send(i)
    for u in uc:
        u.second()

    def grad_b(j, _):
        span = pl.ds(pl.multiple_of(j * rc, rc), rc)
        for a in range(2):
            r["db"][a, span, :] = dots(r["hb"][:, span], r["slope"][:, a * width : (a + 1) * width], 0, 0).astype(BF16)
        return 0

    lax.fori_loop(0, width // rc, grad_b, 0)
    start_all(ub)
    for i in range(2):
        rows = pl.ds(pl.multiple_of(mine + i * rc, rc), rc)
        here = slice(i * rc, (i + 1) * rc)
        part = hid_part(rows)
        pair_gh.recv(i)
        gh = r["res"][here, :] + part + r["recv"][here, :].astype(F32)
        n1 = r["n1"][here, :]
        small[0:1, :] += jnp.sum(gh * n1, 0, keepdims=True)
        small[1:2, :] += jnp.sum(gh, 0, keepdims=True)
        g_res = norm_back(gh * g1, n1, r["inv1"][here, 0:1])
        r["res"][here, :] = g_res
        r["gat"][rows, :] = g_res.astype(BF16)
        pair_ga.send(i)
    sums.start(small[...])
    for k in range(4):
        rows = pl.ds(pl.multiple_of(lax.rem(2 * p.c + k, 4) * rc, rc), rc)
        if k >= 2:
            pair_ga.recv(k - 2)
        gctx[:, rows] = dots(wo[...], r["gat"][rows, :], 1, 1).astype(BF16)

    def grad_a(i):
        turn = r["turn"]
        rows = pl.ds(pl.multiple_of(i * 3 * head, head), 3 * head)
        turn[: 3 * head, :] = jnp.dot(qkv[rows, :], x[...], preferred_element_type=F32).astype(BF16)
        rows = pl.ds(pl.multiple_of(i * head, head), head)
        turn[3 * head :, :] = jnp.dot(ctx[rows, :], r["gat"][...], preferred_element_type=F32).astype(BF16)
        ga[lax.rem(i, 2), :, pl.ds(pl.multiple_of(lax.div(i, 2) * each, each), each)] = turn[...].T

    def attend_head_back(i, _):
        q, k, v = set_head(i)
        own_rows = pl.ds(pl.multiple_of(i * head, head), head)
        gk = gv = None
        for j in range(2):
            span = slice(j * half, (j + 1) * half)
            scores = dots(ka[...], qa[:, span], 0, 0)
            probs = jnp.exp(scores - r["lse"][i, :, span])
            grad = gctx[own_rows, span]
            grad_probs = dots(qkv[v, :], grad, 0, 0)
            inner = jnp.sum(probs * grad_probs, 0, keepdims=True)
            grad_scores = (probs * (grad_probs - inner)).astype(BF16)
            qkv[q, span] = (jnp.dot(ka[0:head, :], grad_scores, preferred_element_type=F32) * scale).astype(BF16)
            dk = dots(qa[0:head, span], grad_scores, 1, 1)
            dv = dots(grad, probs.astype(BF16), 1, 1)
            gk, gv = (dk, dv) if gk is None else (gk + dk, gv + dv)
        qkv[k, :] = gk.astype(BF16)
        qkv[v, :] = gv.astype(BF16)

        grad_a(i)
        for k in range(heads):

            @pl.when(i == k)
            def _():
                if k == 1:
                    for u in uc:
                        u.third()
                if k == 3:
                    for u in ub:
                        u.second()
                    for u in uc:
                        u.line()
                start_all([ua[k]])
                if k == 4:
                    ua[0].second()
                    ua[1].second()
                if k == 5:
                    for u in ub:
                        u.third()
                if k in (2, 4):
                    sums.step(k // 2 - 1)

        return 0

    lax.fori_loop(0, heads, attend_head_back, 0)

    def tok_part(rows):
        total = None
        for i in range(heads):
            mine_rows = slice(i * 3 * head, (i + 1) * 3 * head)
            first = (i // 2) * each
            part = dots(qkv[mine_rows, rows], at[i % 2, first : first + 3 * head, :], 0, 0)
            total = part if total is None else total + part
        return total

    for i in range(2):
        r["send1"][i * rc : (i + 1) * rc, :] = tok_part(pl.ds(pl.multiple_of(theirs + i * rc, rc), rc)).astype(BF16)
        pair_gt.send(i)
    for u in ua[2:4]:
        u.second()
    for i in range(2):
        rows = pl.ds(pl.multiple_of(mine + i * rc, rc), rc)
        here = slice(i * rc, (i + 1) * rc)
        part = tok_part(rows)
        pair_gt.recv(i)
        r["gtokb"][here, :] = (r["res"][here, :] + part + r["recv1"][here, :].astype(F32)).astype(BF16)
        home_g.send(i)
    for u in ub:
        u.line()
    for u in ua[:2]:
        u.third()
    for u in ua[4:]:
        u.second()
    sums.step(2)
    for u in ua[2:4]:
        u.third()
    for u in ua[:2]:
        u.line()
    for u in ua[4:]:
        u.third()
    for u in ua[2:]:
        u.line()
    sums.finish()

    def settle(made, land, out):
        for u in made:
            if len(u.halves) == 2:
                u.owned()
            else:
                pl.when(p.a == u.halves[0])(u.owned)
        total = land[0].astype(F32)
        for z in range(1, 3):
            total = total + land[z].astype(F32)
        out[...] = total

    settle(uc, r["lc"], r["rc"])
    settle(ub, r["lb"], r["rb"])
    settle(ua, r["la"], r["ra"])
    home.finish()
    home_g.finish()
    tokens.finish(mp)
    for swap in (pair_gh, pair_ga, pair_gt):
        swap.finish()
    for u in ua + ub + uc:
        u.finish()
    for copy in vcopies[:-1] + pcopies:
        copy.wait_send()


def fused_layer(mp, tok, cot, pa, pb, pc, vec, pick, head, nblocks, picks):
    n, width = pa.shape
    quarter = tok.shape[1]
    seq = quarter * mp
    half = seq // 2
    per = width // 4 // head
    group = 3 * per * head
    shape = jax.ShapeDtypeStruct
    names = ["tok", "cot", "pa", "pb", "pc", "vec", "pick"]
    outs = {
        "hout": (shape((2, quarter, width), BF16), ANY),
        "hgtok": (shape((2, quarter, width), BF16), ANY),
        "ra": (shape((n, width), F32), VMEM),
        "rb": (shape((n, width), F32), VMEM),
        "rc": (shape((n, width), F32), VMEM),
        "sums": (shape((8, width), F32), VMEM),
    }
    weight = ((2, 8 * n, width), BF16)
    rows_b, half_b, half_f = ((seq, width), BF16), ((half, width), BF16), ((half, width), F32)
    bufs = {
        "x": rows_b, "ga": weight, "gb": weight, "gc": weight, "at": weight, "db": weight, "dc": weight,
        "qkv": ((2 * group, seq), BF16), "ctx": ((2 * per * head, seq), BF16), "gctx": ((2 * per * head, seq), BF16),
        "wo": ((2 * per * head, width), BF16), "lse": ((2 * per, 1, seq), F32), "n1": half_f, "inv1": ((half, 128), F32), "res": half_f,
        "hb": rows_b, "act": ((seq, 2 * width), BF16), "slope": ((seq, 2 * width), BF16), "gf": rows_b, "gat": rows_b,
        "send": half_b, "recv": half_b, "send1": half_b, "recv1": half_b, "outb": half_b, "gtokb": half_b, "ct": half_b,
        "gvec": ((8,) + vec.shape, BF16), "gpick": ((mp + 1,) + pick.shape, BF16), "norms": (vec.shape, F32),
        "bias": ((2 * per, nblocks, seq), BF16), "qa": ((head + nblocks + 16, seq), BF16), "ka": ((head + nblocks + 16, seq), BF16),
        "small": ((8, width), F32), "turn": ((4 * head, width), BF16),
        "la": ((3, n, width), BF16), "lb": ((3, n, width), BF16), "lc": ((3, n, width), BF16),
        "sumbuf.0": ((3, 8, width), F32), "sumbuf.1": ((3, 8, width), F32), "sumbuf.2": ((mp, 8, width), F32),
    }
    pieces = {"a": (4 * head, 2 * per, 1), "b": (width // 2, 2, 2), "c": (width // 2, 2, 2)}
    for w, (count, many, halves) in pieces.items():
        for i in range(many):
            for k in range(5):
                bufs[f"s{w}{i}b.{k}"] = ((halves, 2 * n, count), BF16)
    scratch = {k: pltpu.VMEM(*v) for k, v in bufs.items()}

    def add(key, specs):
        for i, spec in enumerate(specs):
            scratch[f"{key}.{i}"] = spec

    add("tok", [DMA((4,)), DMA((mp,)), DMA((mp,)), DMA((mp,))])
    for key in ("cot", "home", "homeg", *(f"sw{i}" for i in range(7))):
        add(key, [DMA((2,)), DMA((2,))])
    for w, (count, many, _) in pieces.items():
        for i in range(width // count):
            add(f"g{w}{i}", gather_sems())
        for i in range(many):
            add(f"s{w}{i}s", [DMA((3,)), DMA((3,)), DMA((4,)), DMA((4,))])
    add("vec", [DMA((7,)), DMA((8,)), DMA((mp,)), DMA((mp + 1,))])
    add("sum", [DMA((3,)), DMA((3,)), DMA((mp - 1,)), DMA((mp,))])
    names = names + list(outs) + list(scratch)
    return pl.pallas_call(
        lambda *refs: layer_kernel(mp, head, nblocks, picks, names, *refs),
        name="layer",
        out_shape=[o[0] for o in outs.values()],
        in_specs=[ANY] * 5 + [VMEM] * 2,
        out_specs=[o[1] for o in outs.values()],
        scratch_shapes=list(scratch.values()),
        compiler_params=pltpu.CompilerParams(collective_id=0, has_side_effects=True, vmem_limit_bytes=64 << 20),
    )(tok, cot, pa, pb, pc, vec, pick)


def attend_kernel(q_ref, k_ref, v_ref, bias_ref, hot_ref, ctx_ref, lse_ref, qa, ka):
    seq = q_ref.shape[2]
    head = q_ref.shape[1]
    scale = 1.0 / math.sqrt(head)
    blocks = bias_ref.shape[2]
    step = min(256, seq)
    qa[0:head, :] = (q_ref[0].astype(F32) * scale).astype(BF16)
    qa[head : head + blocks, :] = bias_ref[0, 0]
    low = lax.broadcasted_iota(jnp.int32, (qa.shape[0] - head - blocks, seq), 0)
    qa[head + blocks :, :] = jnp.where(low == 0, NEG, 0.0).astype(BF16)
    ka[0:head, :] = k_ref[0]
    ka[head:, :] = hot_ref[...]
    for i in range(seq // step):
        cols = slice(i * step, (i + 1) * step)
        scores = lax.dot_general(ka[...], qa[:, cols], (((0,), (0,)), ((), ())), preferred_element_type=F32)
        peak = jnp.max(scores, 0, keepdims=True)
        weights = jnp.exp(scores - peak)
        total = jnp.sum(weights, 0, keepdims=True)
        mixed = jnp.dot(v_ref[0], weights.astype(BF16), preferred_element_type=F32)
        ctx_ref[0, :, cols] = (mixed / total).astype(BF16)
        lse_ref[0, 0, :, cols] = peak + jnp.log(total)


def head_specs(head, seq, per, blocks, hot_rows):
    row = lambda part: pl.BlockSpec((1, head, seq), lambda m, h: (m, part * per + h, 0))
    return (
        [row(0), row(1), row(2)],
        pl.BlockSpec((1, 1, blocks, seq), lambda m, h: (m, h, 0, 0)),
        pl.BlockSpec((hot_rows, seq), lambda m, h: (0, 0)),
        pl.BlockSpec((1, 1, 1, seq), lambda m, h: (m, h, 0, 0)),
        row(0),
    )


def attend(qkv, bias, hot, head):
    groups, width, seq = qkv.shape
    per = width // (3 * head)
    rows, bias_spec, hot_spec, line, out = head_specs(head, seq, per, bias.shape[2], hot.shape[0])
    deep = head + hot.shape[0]
    return pl.pallas_call(
        attend_kernel,
        name="attend",
        grid=(groups, per),
        out_shape=[
            jax.ShapeDtypeStruct((groups, per * head, seq), BF16),
            jax.ShapeDtypeStruct((groups, per, 1, seq), F32),
        ],
        in_specs=rows + [bias_spec, hot_spec],
        out_specs=[out, line],
        scratch_shapes=[pltpu.VMEM((deep, seq), BF16), pltpu.VMEM((deep, seq), BF16)],
        compiler_params=pltpu.CompilerParams(vmem_limit_bytes=48 << 20),
    )(qkv, qkv, qkv, bias, hot)


def attend_back_kernel(q_ref, k_ref, v_ref, bias_ref, hot_ref, lse_ref, g_ref, dq_ref, dk_ref, dv_ref, qa, ka, ak, av):
    seq = q_ref.shape[2]
    head = q_ref.shape[1]
    scale = 1.0 / math.sqrt(head)
    blocks = bias_ref.shape[2]
    step = min(256, seq)
    qa[0:head, :] = (q_ref[0].astype(F32) * scale).astype(BF16)
    qa[head : head + blocks, :] = bias_ref[0, 0]
    low = lax.broadcasted_iota(jnp.int32, (qa.shape[0] - head - blocks, seq), 0)
    qa[head + blocks :, :] = jnp.where(low == 0, NEG, 0.0).astype(BF16)
    ka[0:head, :] = k_ref[0]
    ka[head:, :] = hot_ref[...]
    for i in range(seq // step):
        cols = slice(i * step, (i + 1) * step)
        scores = lax.dot_general(ka[...], qa[:, cols], (((0,), (0,)), ((), ())), preferred_element_type=F32)
        probs = jnp.exp(scores - lse_ref[0, 0, :, cols])
        grad = g_ref[0, :, cols]
        grad_probs = lax.dot_general(v_ref[0], grad, (((0,), (0,)), ((), ())), preferred_element_type=F32)
        inner = jnp.sum(probs * grad_probs, 0, keepdims=True)
        grad_scores = (probs * (grad_probs - inner)).astype(BF16)
        dq_ref[0, :, cols] = (jnp.dot(k_ref[0], grad_scores, preferred_element_type=F32) * scale).astype(BF16)
        gk = lax.dot_general(qa[0:head, cols], grad_scores, (((1,), (1,)), ((), ())), preferred_element_type=F32)
        gv = lax.dot_general(grad, probs.astype(BF16), (((1,), (1,)), ((), ())), preferred_element_type=F32)
        if i == 0:
            ak[...] = gk
            av[...] = gv
        else:
            ak[...] += gk
            av[...] += gv
    dk_ref[0] = ak[...].astype(BF16)
    dv_ref[0] = av[...].astype(BF16)


def attend_back(qkv, bias, hot, lse, grad, head):
    groups, width, seq = qkv.shape
    per = width // (3 * head)
    rows, bias_spec, hot_spec, line, out = head_specs(head, seq, per, bias.shape[2], hot.shape[0])
    deep = head + hot.shape[0]
    return pl.pallas_call(
        attend_back_kernel,
        name="attend_back",
        grid=(groups, per),
        out_shape=[jax.ShapeDtypeStruct((groups, per * head, seq), BF16)] * 3,
        in_specs=rows + [bias_spec, hot_spec, line, out],
        out_specs=[out] * 3,
        scratch_shapes=[
            pltpu.VMEM((deep, seq), BF16),
            pltpu.VMEM((deep, seq), BF16),
            pltpu.VMEM((head, seq), F32),
            pltpu.VMEM((head, seq), F32),
        ],
        compiler_params=pltpu.CompilerParams(vmem_limit_bytes=48 << 20),
    )(qkv, qkv, qkv, bias, hot, lse, grad)


def fetch_plain(dp, mp, tok, cot, pa, pb, pc, vec):
    d, m = lax.axis_index("dp"), lax.axis_index("mp")
    core = d % 2
    swap = [(i, i ^ 1) for i in range(dp)]

    def sequence(rows):
        whole = lax.all_gather(rows, "mp", axis=1, tiled=True)
        other = lax.ppermute(whole, "dp", swap)
        return jnp.where(m // 2 == core, whole, other)[m % 2]

    def weight(part):
        plane = lax.all_gather(part, "dp", axis=0, tiled=True)
        return lax.dynamic_slice_in_dim(lax.all_gather(plane, "mp"), 2 * core, 2, 0)

    half = tok.shape[1] * mp // 2
    ct = lax.dynamic_slice_in_dim(sequence(cot), core * half, half, 0)
    return (
        sequence(tok), ct, weight(pa), weight(pb), weight(pc), lax.all_gather(vec, "dp"), lax.all_gather(vec, "mp"),
    )


def deliver_plain(dp, mp, da, db, dc, out, gtok, rows, quarter):
    d, m = lax.axis_index("dp"), lax.axis_index("mp")
    core = d % 2
    swap = [(i, i ^ 1) for i in range(dp)]

    def grad(part):
        wide = jnp.zeros((mp,) + part.shape[1:], F32)
        wide = lax.dynamic_update_slice_in_dim(wide, part.astype(F32), 2 * core, 0)
        mine = lax.psum_scatter(wide, "mp", scatter_dimension=0, tiled=True)[0]
        return lax.psum_scatter(mine, "dp", scatter_dimension=0, tiled=True)[None]

    def home(half):
        both = jnp.zeros((2,) + half.shape, half.dtype)
        both = lax.dynamic_update_slice_in_dim(both, half[None], core, 0)
        both = lax.dynamic_update_slice_in_dim(both, lax.ppermute(half, "dp", swap)[None], 1 - core, 0)
        all_rows = lax.all_gather(both.reshape(mp, quarter, -1), "mp")
        mine = lax.dynamic_slice_in_dim(all_rows, 2 * core, 2, 0)
        return lax.dynamic_slice_in_dim(mine, m, 1, 1)[:, 0]

    return grad(da), grad(db), grad(dc), home(out), home(gtok)


def layer_plain(
    dp, mp, tokens, cotangent, w_query, w_key, w_value, w_out, w_inner, w_outer,
    gain_attn, shift_attn, gain_ffn, shift_ffn, seq_lengths, rand_blocks,
):
    d, m = lax.axis_index("dp"), lax.axis_index("mp")
    core = d % 2
    swap = [(i, i ^ 1) for i in range(dp)]
    quarter, width = tokens.shape[1:]
    seq = quarter * mp
    half = seq // 2
    per, nblocks, picks = rand_blocks.shape
    cols = w_query.shape[1]
    head = cols // per
    block = seq // nblocks
    rows = w_query.shape[0]
    vec_rows = [v.astype(F32) for v in (gain_attn, shift_attn, gain_ffn, shift_ffn)]
    vec_rows += [seq_lengths.astype(F32)]
    flat = rand_blocks.astype(F32).reshape(-1)
    vec_rows += [flat[:128], flat[128:]]
    vec = jnp.stack([jnp.pad(v, (0, 128 - v.shape[0])) for v in vec_rows] + [jnp.zeros(128, F32)])
    pa = jnp.concatenate([w_query, w_key, w_value, w_out.T], 1)
    pb, pc = w_inner, w_outer.T
    x, ct, ga, gb, gc, gvd, gvz = fetch_plain(dp, mp, tokens, cotangent, pa, pb, pc, vec)
    norms = jnp.swapaxes(gvd[:, :4, :rows], 0, 1).reshape(4, width)
    g1, b1, g2, b2 = (norms[i][None] for i in range(4))
    owner = d - core + m // 2
    lens = lax.dynamic_slice_in_dim(gvd[:, 4, :2], owner, 1, 0)[0]
    length = jnp.where(m % 2 == 0, lens[0], lens[1]).astype(jnp.int32)
    picked = lax.dynamic_slice_in_dim(gvz, 2 * core, 2, 0)
    picked = picked[:, 5:7].reshape(2, 256)[:, : per * nblocks * picks].astype(jnp.int32)
    picked = picked.reshape(2, per, nblocks, picks)

    r = jnp.arange(nblocks)
    near = (r[:, None] == 0) | (r[:, None] == nblocks - 1) | (r[None] == 0) | (r[None] == nblocks - 1)
    near = near | (jnp.abs(r[:, None] - r[None]) <= 1)
    hits = jnp.any(picked[:, :, :, :, None] == r, axis=3) | near
    bias = jnp.where(jnp.swapaxes(hits, 2, 3), 0.0, NEG).astype(BF16)
    bias = jnp.repeat(bias, block, axis=3)
    pos = jnp.arange(seq)
    hot = jnp.concatenate([pos[None] // block == r[:, None], pos[None] >= length, jnp.zeros((15, seq), bool)], 0)
    hot = hot.astype(BF16)

    def mine(values):
        return lax.dynamic_slice_in_dim(values, core * half, half, 0)

    def theirs(values):
        return lax.dynamic_slice_in_dim(values, (1 - core) * half, half, 0)

    def pair_sum(partial):
        return mine(partial) + lax.ppermute(theirs(partial).astype(BF16), "dp", swap).astype(F32)

    def pair_join(values):
        other = lax.ppermute(values, "dp", swap)
        lo = jnp.where(core == 0, values, other)
        hi = jnp.where(core == 0, other, values)
        return jnp.concatenate([lo, hi], 0)

    def dot(spec, a, b):
        return jnp.einsum(spec, a, b, preferred_element_type=F32)

    a_qkv, a_out = ga[:, :, : 3 * cols], ga[:, :, 3 * cols :]
    qkv = dot("mrc,tr->mct", a_qkv, x).astype(BF16)
    ctx, lse = attend(qkv, bias, hot, head)
    attn = pair_sum(dot("mct,mdc->td", ctx, a_out))
    x_mine = mine(x).astype(F32)

    def norm(z):
        centre = z - jnp.mean(z, -1, keepdims=True)
        inv = lax.rsqrt(jnp.mean(centre * centre, -1, keepdims=True) + EPS)
        return centre * inv, inv

    n1, inv1 = norm(x_mine + attn)
    hidden = n1 * g1 + b1
    hidden_b = pair_join(hidden.astype(BF16))
    inner = dot("td,mdk->tmk", hidden_b, gb)
    cumul = 0.5 * (1.0 + lax.erf(inner * (1.0 / math.sqrt(2.0))))
    active = (inner * cumul).astype(BF16)
    slope = cumul + inner * jnp.exp(-0.5 * inner * inner) * (1.0 / math.sqrt(2.0 * math.pi))
    n2, inv2 = norm(hidden + pair_sum(dot("tmk,mdk->td", active, gc)))
    valid = (core * half + jnp.arange(half) < length).astype(F32)[:, None]
    out = ((n2 * g2 + b2) * valid).astype(BF16)

    def norm_back(e, n, inv):
        return (e - jnp.mean(e, -1, keepdims=True) - n * jnp.mean(e * n, -1, keepdims=True)) * inv

    gy = ct.astype(F32) * valid
    g_mid = norm_back(gy * g2, n2, inv2)
    d_gain2, d_shift2 = jnp.sum(gy * n2, 0), jnp.sum(gy, 0)
    g_ffn = pair_join(g_mid.astype(BF16))
    d_c = dot("td,tmk->mdk", g_ffn, active).astype(BF16)
    g_inner = (dot("td,mdk->tmk", g_ffn, gc) * slope).astype(BF16)
    d_b = dot("td,tmk->mdk", hidden_b, g_inner).astype(BF16)
    g_hidden = g_mid + pair_sum(dot("tmk,mdk->td", g_inner, gb))
    d_gain1, d_shift1 = jnp.sum(g_hidden * n1, 0), jnp.sum(g_hidden, 0)
    g_res = norm_back(g_hidden * g1, n1, inv1)
    g_attn = pair_join(g_res.astype(BF16))
    d_out = dot("td,mct->mdc", g_attn, ctx).astype(BF16)
    g_ctx = dot("td,mdc->mct", g_attn, a_out).astype(BF16)
    sums = jnp.stack([d_gain1, d_shift1, d_gain2, d_shift2] + [jnp.zeros_like(d_gain1)] * 4)
    dq, dk, dv = attend_back(qkv, bias, hot, lse, g_ctx, head)
    dqkv = jnp.concatenate([dq, dk, dv], 1)
    d_qkv = dot("tr,mct->mrc", x, dqkv).astype(BF16)
    d_a = jnp.concatenate([d_qkv, d_out], 2)
    gtok = (g_res + pair_sum(dot("mct,mrc->tr", dqkv, a_qkv))).astype(BF16)
    ra, rb, rc, out, gtok = deliver_plain(dp, mp, d_a, d_b, d_c, out, gtok, rows, quarter)
    sums = lax.psum(sums, ("dp", "mp"))
    ra, rb, rc = (jnp.sum(v.astype(F32), 0) for v in (ra, rb, rc))
    sums = lax.dynamic_slice_in_dim(sums, d * rows, rows, 1)
    return (
        out, gtok, ra[:, :cols], ra[:, cols : 2 * cols], ra[:, 2 * cols : 3 * cols], ra[:, 3 * cols :].T, rb, rc.T,
        sums[0], sums[1], sums[2], sums[3],
    )


def layer(
    dp, mp, tokens, cotangent, w_query, w_key, w_value, w_out, w_inner, w_outer,
    gain_attn, shift_attn, gain_ffn, shift_ffn, seq_lengths, rand_blocks,
):
    rows, cols = w_query.shape
    per, nblocks, picks = rand_blocks.shape
    if not (dp == 8 and mp == 4 and rows % 16 == 0 and 4 * cols == 8 * rows and tokens.shape[0] == 2):
        return layer_plain(
            dp, mp, tokens, cotangent, w_query, w_key, w_value, w_out, w_inner, w_outer,
            gain_attn, shift_attn, gain_ffn, shift_ffn, seq_lengths, rand_blocks,
        )
    d = lax.axis_index("dp")
    pa = jnp.stack([w.reshape(rows, per, -1) for w in (w_query, w_key, w_value, w_out.T)], 2).reshape(rows, 4 * cols)
    lens = jnp.stack([seq_lengths // 32, seq_lengths % 32], 1).reshape(1, -1).astype(BF16)
    vec = jnp.stack([gain_attn, shift_attn, gain_ffn, shift_ffn])
    vec = lax.dynamic_update_slice(jnp.zeros((16, 4 * cols), BF16), vec, (0, d * rows))
    pick = jnp.swapaxes(rand_blocks, 1, 2).reshape(per * picks, nblocks).astype(BF16)
    pick = jnp.pad(pick, ((0, 15 - per * picks), (0, 128 - nblocks)))
    pick = jnp.concatenate([pick, jnp.pad(lens, ((0, 0), (0, 124)))])
    out, gtok, ra, rb, rc, sums = fused_layer(
        mp, tokens, cotangent, pa, w_inner, w_outer.T, vec, pick, cols // per, nblocks, picks
    )
    sums = lax.dynamic_slice_in_dim(sums, d * rows, rows, 1)
    ra = ra.reshape(rows, per, 4, -1)
    gq, gk, gv, go = (ra[:, :, i].reshape(rows, cols) for i in range(4))
    return out, gtok, gq, gk, gv, go.T, rb, rc.T, sums[0], sums[1], sums[2], sums[3]


def solution(mesh):
    dp, mp = mesh.shape["dp"], mesh.shape["mp"]
    act, vec = P("dp", "mp", None), P("dp")
    w_in, w_back = P("dp", "mp"), P("mp", "dp")

    def step(*args):
        return layer(dp, mp, *args)

    return jax.shard_map(
        step,
        mesh=mesh,
        in_specs=(act, act, w_in, w_in, w_in, w_back, w_in, w_back, vec, vec, vec, vec, vec, P("mp", None, None)),
        out_specs=(act, act, w_in, w_in, w_in, w_back, w_in, w_back, vec, vec, vec, vec),
        check_vma=False,
    )
```

```python
import math

import jax
import jax.numpy as jnp
from jax import lax
from jax.experimental import pallas as pl
from jax.experimental.pallas import tpu as pltpu
from jax.sharding import PartitionSpec as P

EPS = 1e-06
NEG = -1000000000.0
MESH = pl.DeviceIdType.MESH
F32 = jnp.float32
BF16 = jnp.bfloat16
ANY = pl.BlockSpec(memory_space=pl.ANY)
VMEM = pl.BlockSpec(memory_space=pltpu.VMEM)
DMA = pltpu.SemaphoreType.DMA


class Place:
    def __init__(self):
        self.d = lax.axis_index("dp")
        self.m = lax.axis_index("mp")
        self.c = lax.rem(self.d, 2)
        self.base = self.d - self.c
        self.sib = self.d + 1 - 2 * self.c
        bx = lax.rem(lax.div(self.d, 2), 2)
        by = lax.rem(lax.div(self.d, 4), 2)
        self.xp = self.d + 2 - 4 * bx
        self.yp = self.d + 4 - 8 * by
        self.bx = self.xp - self.c
        self.by = self.yp - self.c
        self.bd = self.bx + 4 - 8 * by
        self.h = lax.div(self.m, 2)
        self.a = lax.rem(self.m, 2)
        self.close = self.h == self.c
        self.inner = jnp.logical_and(self.h != self.c, self.a + self.h == 1)
        self.outer = jnp.logical_and(self.h != self.c, self.a + self.h != 1)


def remote(src, dst, ssem, rsem, dev):
    return pltpu.make_async_remote_copy(
        src_ref=src, dst_ref=dst, send_sem=ssem, recv_sem=rsem, device_id=dev, device_id_type=MESH
    )


def push(src, dst, ssem, rsem, dev, same):
    @pl.when(same)
    def _():
        pltpu.make_async_copy(src, dst, rsem).start()

    @pl.when(jnp.logical_not(same))
    def _():
        remote(src, dst, ssem, rsem, dev).start()


def pushed(src, dst, ssem, rsem, dev, same):
    @pl.when(jnp.logical_not(same))
    def _():
        remote(src, dst, ssem, rsem, dev).wait_send()


def got(dst, ssem, rsem, dev):
    remote(dst, dst, ssem, rsem, dev).wait_recv()


def greet(peers):
    barrier = pltpu.get_barrier_semaphore()
    for dev in peers:
        pl.semaphore_signal(barrier, inc=1, device_id=dev, device_id_type=MESH)
    pl.semaphore_wait(barrier, len(peers))


def dots(a, b, ca, cb):
    return lax.dot_general(a, b, (((ca,), (cb,)), ((), ())), preferred_element_type=F32)


def column_peers(p, mp):
    peers = []
    for k in range(1, mp):
        z = lax.rem(p.m + k, mp)
        peers += [(p.base, z), (p.base + 1, z)]
    return peers


class Gather:
    def __init__(self, p, src, dst, first, count, sems):
        self.p, self.src, self.dst = p, src, dst
        self.zs, self.zr, self.fs, self.fr, self.xs, self.xr, self.ys, self.yr = sems
        self.n = src.shape[0]
        self.cols = pl.ds(first, count)

    def rows(self, a, first, count):
        return self.dst.at[a, pl.ds(first * self.n, count * self.n), self.cols]

    def both(self, first):
        return self.dst.at[:, pl.ds(first * self.n, 2 * self.n), self.cols]

    def z_args(self, k):
        p = self.p
        z = (p.m, p.m + 1 - 2 * p.a, 2 - p.h)[k]
        src = self.src.at[:, self.cols]
        return src, self.rows(p.a, p.d, 1), self.zs.at[k], self.zr.at[2 * p.c + p.a], (p.base + p.h, z)

    def z_send(self):
        for k in (2, 1):
            remote(*self.z_args(k)).start()
        push(*self.z_args(0), self.p.close)

    def pass_on(self):
        p = self.p
        part = self.both(p.base)
        return remote(part, part, self.fs.at[0], self.fr.at[0], (p.d, 3 * p.h))

    def z_mid(self):
        p = self.p

        @pl.when(jnp.logical_not(p.outer))
        def _():
            for core in range(2):
                for a in range(2):
                    got(self.rows(a, p.base + core, 1), self.zs.at[0], self.zr.at[2 * core + a], (p.d, p.m))

        @pl.when(p.inner)
        def _():
            self.pass_on().start()

        @pl.when(p.outer)
        def _():
            self.pass_on().wait_recv()

        self.hop(0, 0).start()
        self.hop(1, 0).start()

    def hop(self, axis, step):
        p = self.p
        peer = p.xp if axis == 0 else p.yp
        s, r = (self.xs, self.xr) if axis == 0 else (self.ys, self.yr)
        part = self.both(p.base) if step == 0 else self.rows(1 - axis, p.by if axis == 0 else p.bx, 2)
        return remote(part, part, s.at[step], r.at[step], (peer, p.m))

    def arrived(self, axis, step):
        p = self.p
        s, r = (self.xs, self.xr) if axis == 0 else (self.ys, self.yr)
        part = self.both(p.bx if axis == 0 else p.by) if step == 0 else self.rows(1 - axis, p.bd, 2)
        got(part, s.at[step], r.at[step], (p.d, p.m))

    def forward(self):
        for axis in range(2):
            self.arrived(axis, 0)
            self.hop(1 - axis, 1).start()

    def land(self):
        self.arrived(1, 1)
        self.arrived(0, 1)

    def finish(self):
        for k in (1, 2):
            remote(*self.z_args(k)).wait_send()
        pushed(*self.z_args(0), self.p.close)

        @pl.when(self.p.inner)
        def _():
            self.pass_on().wait_send()

        for axis in range(2):
            for step in range(2):
                self.hop(axis, step).wait_send()


def gather_sems():
    return [DMA((3,)), DMA((4,)), DMA((1,)), DMA((1,)), DMA((2,)), DMA((2,)), DMA((2,)), DMA((2,))]


class Tokens:
    def __init__(self, p, tok, x, sems):
        self.p, self.tok, self.x = p, tok, x
        self.s, self.r, self.fs, self.fr = sems
        self.piece = tok.shape[1] // 2

    def args(self, i, half):
        p, n = self.p, self.piece
        z = 2 * p.c + i
        dev = (p.base + half, z)
        dst = self.x.at[pl.ds((2 * p.m + half) * n, n), :]
        src = self.tok.at[i, pl.ds(half * n, n), :]
        return (src, dst, self.s.at[2 * i + half], self.r.at[p.m], dev), jnp.logical_and(p.c == half, p.m == z)

    def send(self):
        for i in range(2):
            for half in range(2):
                args, same = self.args(i, half)
                push(*args, same)

    def part(self, q, core):
        return self.x.at[pl.ds((2 * q + core) * self.piece, self.piece), :]

    def forward(self, mp):
        p = self.p
        for q in range(mp):
            got(self.part(q, p.c), self.s.at[0], self.r.at[q], (p.d, p.m))
            remote(self.part(q, p.c), self.part(q, p.c), self.fs.at[q], self.fr.at[q], (p.sib, p.m)).start()

    def land(self, mp):
        p = self.p
        for q in range(mp):
            got(self.part(q, 1 - p.c), self.fs.at[q], self.fr.at[q], (p.d, p.m))

    def finish(self, mp):
        p = self.p
        for q in range(mp):
            remote(self.part(q, p.c), self.part(q, p.c), self.fs.at[q], self.fr.at[q], (p.sib, p.m)).wait_send()
        for i in range(2):
            for half in range(2):
                args, same = self.args(i, half)
                pushed(*args, same)


class Quarters:
    def __init__(self, p, src, dst, sems):
        self.p, self.src, self.dst = p, src, dst
        self.s, self.r = sems
        self.n = src.shape[1]

    def args(self, i):
        p = self.p
        z = 2 * p.c + i
        dst = self.dst.at[pl.ds(p.a * self.n, self.n), :]
        same = jnp.logical_and(p.h == p.c, p.m == z)
        return (self.src.at[i], dst, self.s.at[i], self.r.at[p.a], (p.base + p.h, z)), same

    def send(self):
        for i in range(2):
            args, same = self.args(i)
            push(*args, same)

    def finish(self):
        p = self.p
        for a in range(2):
            got(self.dst.at[pl.ds(a * self.n, self.n), :], self.s.at[a], self.r.at[a], (p.d, p.m))
        for i in range(2):
            args, same = self.args(i)
            pushed(*args, same)


class Homewards:
    def __init__(self, p, src, dst, sems):
        self.p, self.src, self.dst = p, src, dst
        self.s, self.r = sems
        self.n = dst.shape[1]

    def args(self, q):
        p = self.p
        src = self.src.at[pl.ds(q * self.n, self.n), :]
        owner = p.base + p.h
        same = jnp.logical_and(owner == p.d, p.m == 2 * p.c + q)
        return (src, self.dst.at[p.a], self.s.at[q], self.r.at[p.a], (owner, 2 * p.c + q)), same

    def send(self, q):
        args, same = self.args(q)
        push(*args, same)

    def finish(self):
        p = self.p
        for i in range(2):
            got(self.dst.at[i], self.s.at[i], self.r.at[i], (p.d, p.m))
        for q in range(2):
            args, same = self.args(q)
            pushed(*args, same)


class Scatter:
    def __init__(self, p, src, out, halves, first, count, axis, bufs, sems):
        self.p, self.src, self.out, self.halves = p, src, out, halves
        self.r1, self.r2, self.r3, self.total, self.met = bufs
        self.s, self.r, self.zs, self.zr = sems
        self.n = out.shape[1]
        self.first, self.count = first, count
        self.cols = pl.ds(first, count)
        self.near, self.far = ((p.xp, p.bx), (p.yp, p.by)) if axis == 0 else ((p.yp, p.by), (p.xp, p.bx))

    def rows(self, first):
        return self.src.at[pl.ds(self.halves[0], len(self.halves)), pl.ds(first * self.n, 2 * self.n), self.cols]

    def hop(self, kind):
        p = self.p
        if kind == 0:
            src, dst, peer = self.rows(p.bd), self.r1, self.near[0]
        elif kind == 1:
            src, dst, peer = self.rows(self.near[1]), self.r2, self.near[0]
        else:
            src, dst, peer = self.r1, self.r3, self.far[0]
        return remote(src, dst, self.s.at[kind], self.r.at[kind], (peer, p.m))

    def second(self):
        self.hop(0).wait_recv()
        self.r1[...] = (self.rows(self.far[1])[...].astype(F32) + self.r1[...].astype(F32)).astype(BF16)
        self.hop(2).start()

    def third(self):
        p = self.p
        self.hop(1).wait_recv()
        self.hop(2).wait_recv()
        self.total[...] = (
            self.rows(p.base)[...].astype(F32) + self.r2[...].astype(F32) + self.r3[...].astype(F32)
        ).astype(BF16)

        @pl.when(p.close)
        def _():
            for args in self.z_args():
                push(*args)

        @pl.when(p.outer)
        def _():
            self.meet().start()

    def meet(self):
        p = self.p
        return remote(self.total, self.met, self.zs.at[0], self.zr.at[3], (p.d, 1 + p.h))

    def z_args(self):
        p = self.p
        slot = jnp.where(p.close, p.a, 2)
        made = []
        for i, a in enumerate(self.halves):
            for core in range(2):
                same = jnp.logical_and(p.c == core, p.m == 2 * p.c + a)
                src = self.total.at[i, pl.ds(core * self.n, self.n), :]
                dst = self.out.at[slot, :, self.cols]
                made.append((src, dst, self.zs.at[2 * i + core], self.zr.at[slot], (p.base + core, 2 * p.c + a), same))
        return made

    def line(self):
        @pl.when(self.p.inner)
        def _():
            self.meet().wait_recv()
            self.total[...] = (self.total[...].astype(F32) + self.met[...].astype(F32)).astype(BF16)
            for args in self.z_args():
                remote(*args[:-1]).start()

    def owned(self):
        for slot in range(3):
            got(self.out.at[slot, :, self.cols], self.zs.at[0], self.zr.at[slot], (self.p.d, self.p.m))

    def finish(self):
        p = self.p
        for kind in range(3):
            self.hop(kind).wait_send()

        @pl.when(p.outer)
        def _():
            self.meet().wait_send()

        @pl.when(p.close)
        def _():
            for args in self.z_args():
                pushed(*args)

        @pl.when(p.inner)
        def _():
            for args in self.z_args():
                remote(*args[:-1]).wait_send()


def start_all(units):
    for kind in range(2):
        for u in units:
            u.hop(kind).start()


class Sums:
    def __init__(self, p, bufs, sems, mp):
        self.p, self.mp = p, mp
        self.mine, self.came, self.parts = bufs
        self.s, self.r, self.zs, self.zr = sems

    def hop(self, i):
        p = self.p
        dev = (p.sib, p.xp, p.yp)[i]
        return remote(self.mine.at[i], self.came.at[i], self.s.at[i], self.r.at[i], (dev, p.m))

    def start(self, values):
        self.mine[0] = values
        self.hop(0).start()

    def step(self, i):
        self.hop(i).wait_recv()
        total = self.mine[i] + self.came[i]
        if i < 2:
            self.mine[i + 1] = total
            self.hop(i + 1).start()
        else:
            self.parts[self.p.m] = total
            for k in range(1, self.mp):
                self.column(k).start()

    def column(self, k):
        p = self.p
        part = self.parts.at[p.m]
        return remote(part, part, self.zs.at[k - 1], self.zr.at[p.m], (p.d, lax.rem(p.m + k, self.mp)))

    def finish(self):
        p = self.p
        for k in range(1, self.mp):
            z = lax.rem(p.m + k, self.mp)
            got(self.parts.at[z], self.zs.at[0], self.zr.at[z], (p.d, p.m))
        total = self.parts[0]
        for z in range(1, self.mp):
            total = total + self.parts[z]
        for i in range(3):
            self.hop(i).wait_send()
        for k in range(1, self.mp):
            self.column(k).wait_send()
        return total


class Swap:
    def __init__(self, p, src, dst, sems, src_first=0, dst_first=0, came_first=0, count=256):
        self.p, self.src, self.dst = p, src, dst
        self.s, self.r = sems
        self.firsts = (src_first, dst_first, came_first)
        self.n = count

    def copy(self, i, side):
        p, n = self.p, self.n
        src_first, dst_first, came_first = self.firsts
        if side == 0:
            src = self.src.at[pl.ds(src_first + i * n, n), :]
            dst = self.dst.at[pl.ds(dst_first + i * n, n), :]
        else:
            src = dst = self.dst.at[pl.ds(came_first + i * n, n), :]
        return remote(src, dst, self.s.at[i], self.r.at[i], (p.sib, p.m))

    def send(self, i):
        self.copy(i, 0).start()

    def recv(self, i):
        self.copy(i, 1).wait_recv()

    def finish(self):
        for i in range(2):
            self.copy(i, 0).wait_send()


def gelu_pair(inner):
    cumul = 0.5 * (1.0 + lax.erf(inner * (1.0 / math.sqrt(2.0))))
    slope = cumul + inner * jnp.exp(-0.5 * inner * inner) * (1.0 / math.sqrt(2.0 * math.pi))
    return inner * cumul, slope


def norm_back(e, n, inv):
    return (e - jnp.mean(e, -1, keepdims=True) - n * jnp.mean(e * n, -1, keepdims=True)) * inv


def norm_rows(z):
    centre = z - jnp.mean(z, -1, keepdims=True)
    inv = lax.rsqrt(jnp.mean(centre * centre, -1, keepdims=True) + EPS)
    return centre * inv, inv


def layer_kernel(mp, head, nblocks, picks, names, *refs):
    r = dict(zip(names, refs, strict=True))
    p = Place()
    x, ga, gb, gc, at, qkv, ctx, gctx = (r[k] for k in ("x", "ga", "gb", "gc", "at", "qkv", "ctx", "gctx"))
    seq, width = x.shape
    half = seq // 2
    rc = half // 2
    group = qkv.shape[0] // 2
    cols = group // 3
    per = cols // head
    heads = 2 * per
    n, narrow = r["wq"].shape
    pa, pick, vec = r["pa"], r["pick"], r["vec"]
    scale = 1.0 / math.sqrt(head)
    mine = pl.multiple_of(p.c * half, half)
    theirs = pl.multiple_of(half - p.c * half, half)
    hw = width // 2

    def sems(key):
        return [v for k, v in r.items() if k.startswith(key + ".")]

    tokens = Tokens(p, r["tok"], x, sems("tok"))
    cots = Quarters(p, r["cot"], r["ct"], sems("cot"))
    each = 4 * head
    ga_parts = [Gather(p, r["pa"], ga, i * each, each, sems(f"ga{i}")) for i in range(per)]
    b0, b1, c0, c1 = (
        Gather(p, r["p" + w], r["g" + w], i * hw, hw, sems(f"g{w}{i}")) for w in "bc" for i in range(2)
    )
    gathers = ga_parts + [b0, b1, c0, c1]
    plane = [lax.rem(p.d + k, 8) for k in range(1, 8)]
    gvec, gpick = r["gvec"], r["gpick"]
    vs, vr, us, ur = sems("vec")
    sums = Sums(p, sems("sumbuf"), sems("sum"), mp)
    home = Homewards(p, r["outb"], r["hout"], sems("home"))
    home_g = Homewards(p, r["gtokb"], r["hgtok"], sems("homeg"))
    pair_attn = Swap(p, r["send"], r["recv"], sems("sw0"), count=rc)
    pair_hid = Swap(p, r["hb"], r["hb"], sems("sw1"), mine, mine, theirs, rc)
    pair_ffn = Swap(p, r["send1"], r["recv1"], sems("sw2"), count=rc)
    pair_gf = Swap(p, r["gf"], r["gf"], sems("sw3"), mine, mine, theirs, rc)
    pair_gh = Swap(p, r["send"], r["recv"], sems("sw4"), count=rc)
    pair_ga = Swap(p, r["gat"], r["gat"], sems("sw5"), mine, mine, theirs, rc)
    pair_gt = Swap(p, r["send1"], r["recv1"], sems("sw6"), count=rc)

    def unit(name, src, halves, first, count, axis):
        return Scatter(p, src, r["l" + name[0]], halves, first, count, axis, sems(f"s{name}b"), sems(f"s{name}s"))

    ua = [unit(f"a{i}", ga, (i % 2,), (i // 2) * each, each, i % 2) for i in range(heads)]
    ub, uc = ([unit(f"{w}{i}", r["d" + w], (0, 1), i * hw, hw, i) for i in range(2)] for w in "bc")

    for h in range(per):
        for i, w in enumerate(("wq", "wk", "wv")):
            pa[:, h * each + i * head : h * each + (i + 1) * head] = r[w][:, h * head : (h + 1) * head]
    flip = r["flip"]
    flip[:, :n] = r["wo_in"][...]
    turned = flip[...].T
    for h in range(per):
        pa[:, h * each + 3 * head : (h + 1) * each] = turned[:n, h * head : (h + 1) * head]
    sub16 = lax.broadcasted_iota(jnp.int32, (16, 128), 0)
    lane16 = lax.broadcasted_iota(jnp.int32, (16, 128), 1)
    table = jnp.zeros((16, 128), F32)
    for h in range(per):
        for j in range(picks):
            for b in range(nblocks):
                here = (sub16 == h * picks + j) & (lane16 == b)
                table = jnp.where(here, r["rand"][h, j, b].astype(F32), table)
    for i in range(2):
        count = r["lens"][i]
        high = lax.div(count, 32)
        table = jnp.where((sub16 == 15) & (lane16 == 2 * i), high.astype(F32), table)
        table = jnp.where((sub16 == 15) & (lane16 == 2 * i + 1), (count - 32 * high).astype(F32), table)
    pick[...] = table.astype(BF16)

    greet(column_peers(p, mp) + [(d, p.m) for d in plane])
    pcopies = [remote(pick, gpick.at[p.m], us.at[k - 1], ur.at[p.m], (p.d, lax.rem(p.m + k, mp))) for k in range(1, mp)]
    pcopies.append(remote(pick, gpick.at[mp], us.at[mp - 1], ur.at[mp], (p.sib, p.m)))
    mine_too = pltpu.make_async_copy(pick, gpick.at[p.m], ur.at[p.m])
    for copy in pcopies + [mine_too]:
        copy.start()
    for g in ga_parts:
        g.z_send()

    @pl.when(jnp.logical_not(p.inner))
    def _():
        b0.z_send()
        tokens.send()

    wide = lax.broadcasted_iota(jnp.int32, (128, width), 1) - p.d * n
    deep = lax.broadcasted_iota(jnp.int32, (128, width), 0)
    spots = jnp.where((wide == deep) & (deep < n), 1.0, 0.0).astype(BF16)
    vec[...] = dots(r["gains"][...], spots, 1, 0).astype(BF16)
    vcopies = [remote(vec, gvec.at[p.d], vs.at[k], vr.at[p.d], (d, p.m)) for k, d in enumerate(plane)]
    vcopies.append(pltpu.make_async_copy(vec, gvec.at[p.d], vr.at[p.d]))
    for g in ga_parts:
        g.z_mid()
    pl.when(p.inner)(b0.z_send)
    ga_parts[0].forward()
    b0.z_mid()
    pl.when(p.inner)(tokens.send)
    for copy in vcopies:
        copy.start()

    for z in range(mp + 1):
        got(gpick.at[z], us.at[0], ur.at[z], (p.d, p.m))
    row = jnp.where(p.close, gpick[p.m, 15:16, :].astype(F32), gpick[mp, 15:16, :].astype(F32))
    lane = lax.broadcasted_iota(jnp.int32, (1, 128), 1)
    high, low = (jnp.sum(jnp.where(lane == 2 * p.a + i, row, 0.0), 1, keepdims=True) for i in range(2))
    length = high * 32.0 + low
    block = seq // nblocks
    sub = lax.broadcasted_iota(jnp.int32, (nblocks, seq), 0)
    place = lax.broadcasted_iota(jnp.int32, (nblocks, seq), 1)
    rb = lax.div(place, block)
    near = (rb == 0) | (rb == nblocks - 1) | (sub == 0) | (sub == nblocks - 1) | (jnp.abs(rb - sub) <= 1)
    spread = lax.broadcasted_iota(jnp.int32, (128, seq), 0) == lax.div(lax.broadcasted_iota(jnp.int32, (128, seq), 1), block)
    spread = jnp.where(spread, 1.0, 0.0).astype(BF16)
    subf = sub.astype(F32)
    for a in range(2):
        wide = dots(gpick[2 * p.c + a], spread, 1, 0)
        for h in range(per):
            hit = near
            for j in range(picks):
                at_row = h * picks + j
                hit = hit | (wide[at_row : at_row + 1] == subf)
            r["bias"][2 * h + a] = jnp.where(hit, 0.0, NEG).astype(BF16)
    qa, ka = r["qa"], r["ka"]
    low = lax.broadcasted_iota(jnp.int32, (16, seq), 0)
    ka[head : head + nblocks, :] = jnp.where(rb == sub, 1.0, 0.0).astype(BF16)
    beyond = lax.broadcasted_iota(jnp.int32, (16, seq), 1).astype(F32) >= length
    ka[head + nblocks :, :] = jnp.where((low == 0) & beyond, 1.0, 0.0).astype(BF16)
    qa[head + nblocks :, :] = jnp.where(low == 0, NEG, 0.0).astype(BF16)

    for g in ga_parts[1:]:
        g.forward()
    tokens.forward(mp)
    b1.z_send()
    c0.z_send()
    c1.z_send()
    b0.forward()
    tokens.land(mp)

    def project(h):
        span = pl.ds(pl.multiple_of(h * each, each), each)
        for a in range(2):
            at[a, span, :] = ga[a, :, span].T
        own_rows = pl.ds(pl.multiple_of(h * each, each), 3 * head)

        def some(j, _):
            rows = pl.ds(pl.multiple_of(j * rc, rc), rc)
            for a in range(2):
                to = pl.ds(pl.multiple_of((2 * h + a) * 3 * head, head), 3 * head)
                qkv[to, rows] = dots(at[a, own_rows, :], x[rows, :], 1, 1).astype(BF16)
            return 0

        lax.fori_loop(0, seq // rc, some, 0)

    def parts(i):
        return [pl.ds(pl.multiple_of((3 * i + part) * head, head), head) for part in range(3)]

    def set_head(i):
        q, k, v = parts(i)
        qa[0:head, :] = (qkv[q, :].astype(F32) * scale).astype(BF16)
        qa[head : head + nblocks, :] = r["bias"][i]
        ka[0:head, :] = qkv[k, :]
        return q, k, v

    def attend_head(i, _):
        for h in range(per):

            @pl.when(i == 2 * h)
            def _():
                ga_parts[h].land()

        @pl.when(lax.rem(i, 2) == 0)
        def _():
            project(lax.div(i, 2))

        q, k, v = set_head(i)
        own_rows = pl.ds(pl.multiple_of(i * head, head), head)
        for j in range(2):
            span = slice(j * half, (j + 1) * half)
            scores = dots(ka[...], qa[:, span], 0, 0)
            peak = jnp.max(scores, 0, keepdims=True)
            weights = jnp.exp(scores - peak)
            total = jnp.sum(weights, 0, keepdims=True)
            mixed = jnp.dot(qkv[v, :], weights.astype(BF16), preferred_element_type=F32)
            ctx[own_rows, span] = (mixed / total).astype(BF16)
            r["lse"][i, :, span] = peak + jnp.log(total)

        late = jnp.where(p.outer, 1, 0)

        @pl.when(i == 0 + late)
        def _():
            b1.z_mid()

        @pl.when(i == 2 + late)
        def _():
            c0.z_mid()

        @pl.when(i == 3)
        def _():
            b1.forward()

        @pl.when(i == 4 + late)
        def _():
            c1.z_mid()
            cots.send()

        return 0

    lax.fori_loop(0, heads, attend_head, 0)

    wo = r["wo"]
    for i in range(heads):
        wo[i * head : (i + 1) * head, :] = at[i % 2, (i // 2) * each + 3 * head : (i // 2 + 1) * each, :]
    norms = r["norms"]
    for d in range(8):
        got(gvec.at[d], vs.at[0], vr.at[d], (p.d, p.m))
    vecs = gvec[0].astype(F32)
    for d in range(1, 8):
        vecs = vecs + gvec[d].astype(F32)
    norms[...] = vecs
    g1, s1, g2, s2 = (norms[i : i + 1] for i in range(4))

    def attn_part(first):
        return dots(ctx[:, pl.ds(first, rc)], wo[...], 0, 0)

    for i in range(2):
        r["send"][i * rc : (i + 1) * rc, :] = attn_part(pl.multiple_of(theirs + i * rc, rc)).astype(BF16)
        pair_attn.send(i)
    c0.forward()
    for i in range(2):
        rows = pl.ds(pl.multiple_of(mine + i * rc, rc), rc)
        here = slice(i * rc, (i + 1) * rc)
        part = attn_part(pl.multiple_of(mine + i * rc, rc))
        pair_attn.recv(i)
        n1, inv = norm_rows(x[rows, :].astype(F32) + part + r["recv"][here, :].astype(F32))
        hidden = n1 * g1 + s1
        r["n1"][here, :] = n1
        r["inv1"][here, :] = jnp.broadcast_to(inv, (rc, 128))
        r["res"][here, :] = hidden
        r["hb"][rows, :] = hidden.astype(BF16)
        pair_hid.send(i)

    b0.land()
    b1.land()

    def up(i, _):
        for k in range(2):

            @pl.when(i == 2 + k)
            def _():
                pair_hid.recv(k)

        rows = pl.ds(pl.multiple_of(lax.rem(2 * p.c + i, 4) * rc, rc), rc)
        for a in range(2):
            active, slope = gelu_pair(dots(r["hb"][rows, :], gb[a], 1, 0))
            r["act"][rows, a * width : (a + 1) * width] = active.astype(BF16)
            r["slope"][rows, a * width : (a + 1) * width] = slope.astype(BF16)
        return 0

    lax.fori_loop(0, 4, up, 0)
    c1.forward()
    c0.land()
    c1.land()

    def ffn_part(rows):
        return dots(r["act"][rows, :width], gc[0], 1, 1) + dots(r["act"][rows, width:], gc[1], 1, 1)

    for i in range(2):
        r["send1"][i * rc : (i + 1) * rc, :] = ffn_part(pl.ds(pl.multiple_of(theirs + i * rc, rc), rc)).astype(BF16)
        pair_ffn.send(i)
    cots.finish()
    small = r["small"]
    small[...] = jnp.zeros_like(small)
    for i in range(2):
        rows = pl.ds(pl.multiple_of(mine + i * rc, rc), rc)
        here = slice(i * rc, (i + 1) * rc)
        part = ffn_part(rows)
        pair_ffn.recv(i)
        n2, inv = norm_rows(r["res"][here, :] + part + r["recv1"][here, :].astype(F32))
        pos = (lax.broadcasted_iota(jnp.int32, (rc, 1), 0) + (mine + i * rc)).astype(F32)
        valid = jnp.where(pos < length, 1.0, 0.0)
        r["outb"][here, :] = ((n2 * g2 + s2) * valid).astype(BF16)
        gy = r["ct"][here, :].astype(F32) * valid
        small[2:3, :] += jnp.sum(gy * n2, 0, keepdims=True)
        small[3:4, :] += jnp.sum(gy, 0, keepdims=True)
        g_mid = norm_back(gy * g2, n2, inv)
        r["res"][here, :] = g_mid
        r["gf"][rows, :] = g_mid.astype(BF16)
        pair_gf.send(i)
        home.send(i)

    for g in gathers:
        g.finish()
    for swap in (pair_attn, pair_hid, pair_ffn, pair_gf):
        swap.finish()
    for i in range(2):
        pair_gf.recv(i)

    for k in range(2):

        def grad_c(j, _):
            span = pl.ds(pl.multiple_of(j * rc, rc), rc)
            for a in range(2):
                first = a * width + k * hw
                r["dc"][a, span, k * hw : (k + 1) * hw] = dots(
                    r["gf"][:, span], r["act"][:, first : first + hw], 0, 0
                ).astype(BF16)
            return 0

        lax.fori_loop(0, width // rc, grad_c, 0)
        start_all([uc[k]])

    def back(i, _):
        rows = pl.ds(pl.multiple_of(i * rc, rc), rc)
        for a in range(2):
            part = (rows, slice(a * width, (a + 1) * width))
            r["slope"][part] = (dots(r["gf"][rows, :], gc[a], 1, 0) * r["slope"][part].astype(F32)).astype(BF16)
        return 0

    lax.fori_loop(0, 4, back, 0)

    def hid_part(rows):
        return dots(r["slope"][rows, :width], gb[0], 1, 1) + dots(r["slope"][rows, width:], gb[1], 1, 1)

    for i in range(2):
        r["send"][i * rc : (i + 1) * rc, :] = hid_part(pl.ds(pl.multiple_of(theirs + i * rc, rc), rc)).astype(BF16)
        pair_gh.send(i)
    for u in uc:
        u.second()

    def grad_b(j, _):
        span = pl.ds(pl.multiple_of(j * rc, rc), rc)
        for a in range(2):
            r["db"][a, span, :] = dots(r["hb"][:, span], r["slope"][:, a * width : (a + 1) * width], 0, 0).astype(BF16)
        return 0

    lax.fori_loop(0, width // rc, grad_b, 0)
    start_all(ub)
    for i in range(2):
        rows = pl.ds(pl.multiple_of(mine + i * rc, rc), rc)
        here = slice(i * rc, (i + 1) * rc)
        part = hid_part(rows)
        pair_gh.recv(i)
        gh = r["res"][here, :] + part + r["recv"][here, :].astype(F32)
        n1 = r["n1"][here, :]
        small[0:1, :] += jnp.sum(gh * n1, 0, keepdims=True)
        small[1:2, :] += jnp.sum(gh, 0, keepdims=True)
        g_res = norm_back(gh * g1, n1, r["inv1"][here, 0:1])
        r["res"][here, :] = g_res
        r["gat"][rows, :] = g_res.astype(BF16)
        pair_ga.send(i)
    sums.start(small[...])
    for k in range(4):
        rows = pl.ds(pl.multiple_of(lax.rem(2 * p.c + k, 4) * rc, rc), rc)
        if k >= 2:
            pair_ga.recv(k - 2)
        gctx[:, rows] = dots(wo[...], r["gat"][rows, :], 1, 1).astype(BF16)

    def grad_a(i):
        turn = r["turn"]
        rows = pl.ds(pl.multiple_of(i * 3 * head, head), 3 * head)
        turn[: 3 * head, :] = jnp.dot(qkv[rows, :], x[...], preferred_element_type=F32).astype(BF16)
        rows = pl.ds(pl.multiple_of(i * head, head), head)
        turn[3 * head :, :] = jnp.dot(ctx[rows, :], r["gat"][...], preferred_element_type=F32).astype(BF16)
        ga[lax.rem(i, 2), :, pl.ds(pl.multiple_of(lax.div(i, 2) * each, each), each)] = turn[...].T

    def attend_head_back(i, _):
        q, k, v = set_head(i)
        own_rows = pl.ds(pl.multiple_of(i * head, head), head)
        gk = gv = None
        for j in range(2):
            span = slice(j * half, (j + 1) * half)
            scores = dots(ka[...], qa[:, span], 0, 0)
            probs = jnp.exp(scores - r["lse"][i, :, span])
            grad = gctx[own_rows, span]
            grad_probs = dots(qkv[v, :], grad, 0, 0)
            inner = jnp.sum(probs * grad_probs, 0, keepdims=True)
            grad_scores = (probs * (grad_probs - inner)).astype(BF16)
            qkv[q, span] = (jnp.dot(ka[0:head, :], grad_scores, preferred_element_type=F32) * scale).astype(BF16)
            dk = dots(qa[0:head, span], grad_scores, 1, 1)
            dv = dots(grad, probs.astype(BF16), 1, 1)
            gk, gv = (dk, dv) if gk is None else (gk + dk, gv + dv)
        qkv[k, :] = gk.astype(BF16)
        qkv[v, :] = gv.astype(BF16)

        grad_a(i)
        for k in range(1, heads):

            @pl.when(i == k)
            def _():
                if k == 1:
                    for u in uc:
                        u.third()
                if k == 2:
                    for u in ub:
                        u.second()
                    start_all(ua[:2])
                if k == 3:
                    for u in uc:
                        u.line()
                if k == 4:
                    for u in ub:
                        u.third()
                    for u in ua[:2]:
                        u.second()
                if k == 5:
                    for u in ub:
                        u.line()
                    for u in ua[2:4]:
                        u.second()
                if k % 2 == 1:
                    sums.step(k // 2)
                if k >= 2:
                    start_all([ua[k]])

        return 0

    lax.fori_loop(0, heads, attend_head_back, 0)

    def tok_part(rows):
        total = None
        for i in range(heads):
            mine_rows = slice(i * 3 * head, (i + 1) * 3 * head)
            first = (i // 2) * each
            part = dots(qkv[mine_rows, rows], at[i % 2, first : first + 3 * head, :], 0, 0)
            total = part if total is None else total + part
        return total

    for i in range(2):
        r["send1"][i * rc : (i + 1) * rc, :] = tok_part(pl.ds(pl.multiple_of(theirs + i * rc, rc), rc)).astype(BF16)
        pair_gt.send(i)
    for i in range(2):
        rows = pl.ds(pl.multiple_of(mine + i * rc, rc), rc)
        here = slice(i * rc, (i + 1) * rc)
        part = tok_part(rows)
        pair_gt.recv(i)
        r["gtokb"][here, :] = (r["res"][here, :] + part + r["recv1"][here, :].astype(F32)).astype(BF16)
        home_g.send(i)
    for u in ua[:2]:
        u.third()
    for u in ua[4:]:
        u.second()
    for u in ua[2:4]:
        u.third()
    for u in ua[:2]:
        u.line()
    for u in ua[4:]:
        u.third()
    for u in ua[2:]:
        u.line()
    summed = sums.finish()
    r["sums"][...] = pltpu.roll(summed, width - p.d * n, 1)[:, :128]

    for u in uc + ub:
        u.owned()
    for u in ua:
        pl.when(p.a == u.halves[0])(u.owned)
    home.finish()
    home_g.finish()
    tokens.finish(mp)
    for swap in (pair_gh, pair_ga, pair_gt):
        swap.finish()
    for u in ua + ub + uc:
        u.finish()
    for copy in vcopies[:-1] + pcopies:
        copy.wait_send()


def fused_layer(mp, tok, cot, wq, wk, wv, wo, w_inner, w_outer, gains, lens, rand):
    n, narrow = wq.shape
    quarter, width = tok.shape[1:]
    per, picks, nblocks = rand.shape
    head = narrow // per
    seq = quarter * mp
    half = seq // 2
    group = 3 * per * head
    shape = jax.ShapeDtypeStruct
    SMEM = pl.BlockSpec(memory_space=pltpu.SMEM)
    names = ["tok", "cot", "wq", "wk", "wv", "wo_in", "pb", "pc", "gains", "lens", "rand"]
    outs = {
        "hout": (shape((2, quarter, width), BF16), ANY),
        "hgtok": (shape((2, quarter, width), BF16), ANY),
        **{k: (shape((3, n, width), BF16), ANY) for k in ("la", "lb", "lc")},
        "sums": (shape((8, 128), F32), VMEM),
    }
    weight = ((2, 8 * n, width), BF16)
    rows_b, half_b, half_f = ((seq, width), BF16), ((half, width), BF16), ((half, width), F32)
    bufs = {
        "x": rows_b, "ga": weight, "gb": weight, "gc": weight, "at": weight, "db": weight, "dc": weight,
        "qkv": ((2 * group, seq), BF16), "ctx": ((2 * per * head, seq), BF16), "gctx": ((2 * per * head, seq), BF16),
        "wo": ((2 * per * head, width), BF16), "lse": ((2 * per, 1, seq), F32), "n1": half_f, "inv1": ((half, 128), F32), "res": half_f,
        "hb": rows_b, "act": ((seq, 2 * width), BF16), "slope": ((seq, 2 * width), BF16), "gf": rows_b, "gat": rows_b,
        "send": half_b, "recv": half_b, "send1": half_b, "recv1": half_b, "outb": half_b, "gtokb": half_b, "ct": half_b,
        "gvec": ((8, 16, width), BF16), "gpick": ((mp + 1, 16, 128), BF16), "norms": ((16, width), F32),
        "pa": ((n, width), BF16), "pick": ((16, 128), BF16), "vec": ((16, width), BF16),
        "flip": ((narrow, 128), BF16),
        "bias": ((2 * per, nblocks, seq), BF16), "qa": ((head + nblocks + 16, seq), BF16), "ka": ((head + nblocks + 16, seq), BF16),
        "small": ((8, width), F32), "turn": ((4 * head, width), BF16),
        "sumbuf.0": ((3, 8, width), F32), "sumbuf.1": ((3, 8, width), F32), "sumbuf.2": ((mp, 8, width), F32),
    }
    pieces = {"a": (4 * head, 2 * per, 1), "b": (width // 2, 2, 2), "c": (width // 2, 2, 2)}
    for w, (count, many, halves) in pieces.items():
        for i in range(many):
            for k in range(5):
                bufs[f"s{w}{i}b.{k}"] = ((halves, 2 * n, count), BF16)
    scratch = {k: pltpu.VMEM(*v) for k, v in bufs.items()}

    def add(key, specs):
        for i, spec in enumerate(specs):
            scratch[f"{key}.{i}"] = spec

    add("tok", [DMA((4,)), DMA((mp,)), DMA((mp,)), DMA((mp,))])
    for key in ("cot", "home", "homeg", *(f"sw{i}" for i in range(7))):
        add(key, [DMA((2,)), DMA((2,))])
    for w, (count, many, _) in pieces.items():
        for i in range(width // count):
            add(f"g{w}{i}", gather_sems())
        for i in range(many):
            add(f"s{w}{i}s", [DMA((3,)), DMA((3,)), DMA((4,)), DMA((4,))])
    add("vec", [DMA((7,)), DMA((8,)), DMA((mp,)), DMA((mp + 1,))])
    add("sum", [DMA((3,)), DMA((3,)), DMA((mp - 1,)), DMA((mp,))])
    names = names + list(outs) + list(scratch)
    return pl.pallas_call(
        lambda *refs: layer_kernel(mp, head, nblocks, picks, names, *refs),
        name="layer",
        out_shape=[o[0] for o in outs.values()],
        in_specs=[ANY] * 2 + [VMEM] * 4 + [ANY] * 2 + [VMEM] + [SMEM] * 2,
        out_specs=[o[1] for o in outs.values()],
        scratch_shapes=list(scratch.values()),
        compiler_params=pltpu.CompilerParams(collective_id=0, has_side_effects=True, vmem_limit_bytes=64 << 20),
    )(tok, cot, wq, wk, wv, wo, w_inner, w_outer, gains, lens, rand)


def attend_kernel(q_ref, k_ref, v_ref, bias_ref, hot_ref, ctx_ref, lse_ref, qa, ka):
    seq = q_ref.shape[2]
    head = q_ref.shape[1]
    scale = 1.0 / math.sqrt(head)
    blocks = bias_ref.shape[2]
    step = min(256, seq)
    qa[0:head, :] = (q_ref[0].astype(F32) * scale).astype(BF16)
    qa[head : head + blocks, :] = bias_ref[0, 0]
    low = lax.broadcasted_iota(jnp.int32, (qa.shape[0] - head - blocks, seq), 0)
    qa[head + blocks :, :] = jnp.where(low == 0, NEG, 0.0).astype(BF16)
    ka[0:head, :] = k_ref[0]
    ka[head:, :] = hot_ref[...]
    for i in range(seq // step):
        cols = slice(i * step, (i + 1) * step)
        scores = lax.dot_general(ka[...], qa[:, cols], (((0,), (0,)), ((), ())), preferred_element_type=F32)
        peak = jnp.max(scores, 0, keepdims=True)
        weights = jnp.exp(scores - peak)
        total = jnp.sum(weights, 0, keepdims=True)
        mixed = jnp.dot(v_ref[0], weights.astype(BF16), preferred_element_type=F32)
        ctx_ref[0, :, cols] = (mixed / total).astype(BF16)
        lse_ref[0, 0, :, cols] = peak + jnp.log(total)


def head_specs(head, seq, per, blocks, hot_rows):
    row = lambda part: pl.BlockSpec((1, head, seq), lambda m, h: (m, part * per + h, 0))
    return (
        [row(0), row(1), row(2)],
        pl.BlockSpec((1, 1, blocks, seq), lambda m, h: (m, h, 0, 0)),
        pl.BlockSpec((hot_rows, seq), lambda m, h: (0, 0)),
        pl.BlockSpec((1, 1, 1, seq), lambda m, h: (m, h, 0, 0)),
        row(0),
    )


def attend(qkv, bias, hot, head):
    groups, width, seq = qkv.shape
    per = width // (3 * head)
    rows, bias_spec, hot_spec, line, out = head_specs(head, seq, per, bias.shape[2], hot.shape[0])
    deep = head + hot.shape[0]
    return pl.pallas_call(
        attend_kernel,
        name="attend",
        grid=(groups, per),
        out_shape=[
            jax.ShapeDtypeStruct((groups, per * head, seq), BF16),
            jax.ShapeDtypeStruct((groups, per, 1, seq), F32),
        ],
        in_specs=rows + [bias_spec, hot_spec],
        out_specs=[out, line],
        scratch_shapes=[pltpu.VMEM((deep, seq), BF16), pltpu.VMEM((deep, seq), BF16)],
        compiler_params=pltpu.CompilerParams(vmem_limit_bytes=48 << 20),
    )(qkv, qkv, qkv, bias, hot)


def attend_back_kernel(q_ref, k_ref, v_ref, bias_ref, hot_ref, lse_ref, g_ref, dq_ref, dk_ref, dv_ref, qa, ka, ak, av):
    seq = q_ref.shape[2]
    head = q_ref.shape[1]
    scale = 1.0 / math.sqrt(head)
    blocks = bias_ref.shape[2]
    step = min(256, seq)
    qa[0:head, :] = (q_ref[0].astype(F32) * scale).astype(BF16)
    qa[head : head + blocks, :] = bias_ref[0, 0]
    low = lax.broadcasted_iota(jnp.int32, (qa.shape[0] - head - blocks, seq), 0)
    qa[head + blocks :, :] = jnp.where(low == 0, NEG, 0.0).astype(BF16)
    ka[0:head, :] = k_ref[0]
    ka[head:, :] = hot_ref[...]
    for i in range(seq // step):
        cols = slice(i * step, (i + 1) * step)
        scores = lax.dot_general(ka[...], qa[:, cols], (((0,), (0,)), ((), ())), preferred_element_type=F32)
        probs = jnp.exp(scores - lse_ref[0, 0, :, cols])
        grad = g_ref[0, :, cols]
        grad_probs = lax.dot_general(v_ref[0], grad, (((0,), (0,)), ((), ())), preferred_element_type=F32)
        inner = jnp.sum(probs * grad_probs, 0, keepdims=True)
        grad_scores = (probs * (grad_probs - inner)).astype(BF16)
        dq_ref[0, :, cols] = (jnp.dot(k_ref[0], grad_scores, preferred_element_type=F32) * scale).astype(BF16)
        gk = lax.dot_general(qa[0:head, cols], grad_scores, (((1,), (1,)), ((), ())), preferred_element_type=F32)
        gv = lax.dot_general(grad, probs.astype(BF16), (((1,), (1,)), ((), ())), preferred_element_type=F32)
        if i == 0:
            ak[...] = gk
            av[...] = gv
        else:
            ak[...] += gk
            av[...] += gv
    dk_ref[0] = ak[...].astype(BF16)
    dv_ref[0] = av[...].astype(BF16)


def attend_back(qkv, bias, hot, lse, grad, head):
    groups, width, seq = qkv.shape
    per = width // (3 * head)
    rows, bias_spec, hot_spec, line, out = head_specs(head, seq, per, bias.shape[2], hot.shape[0])
    deep = head + hot.shape[0]
    return pl.pallas_call(
        attend_back_kernel,
        name="attend_back",
        grid=(groups, per),
        out_shape=[jax.ShapeDtypeStruct((groups, per * head, seq), BF16)] * 3,
        in_specs=rows + [bias_spec, hot_spec, line, out],
        out_specs=[out] * 3,
        scratch_shapes=[
            pltpu.VMEM((deep, seq), BF16),
            pltpu.VMEM((deep, seq), BF16),
            pltpu.VMEM((head, seq), F32),
            pltpu.VMEM((head, seq), F32),
        ],
        compiler_params=pltpu.CompilerParams(vmem_limit_bytes=48 << 20),
    )(qkv, qkv, qkv, bias, hot, lse, grad)


def settle_kernel(head, out, gtok, la, lb, lc, out_to, gtok_to, gq, gk, gv, go, gb, gc, turn, sem):
    copies = [pltpu.make_async_copy(out, out_to, sem.at[0]), pltpu.make_async_copy(gtok, gtok_to, sem.at[1])]
    for copy in copies:
        copy.start()

    def total(land):
        return land[0].astype(F32) + land[1].astype(F32) + land[2].astype(F32)

    gb[...] = total(lb)
    gc[...] = total(lc)
    n = gb.shape[0]
    summed = total(la)
    turn[:n, :] = summed
    turned = turn[...].T
    for h in range(gq.shape[1] // head):
        each = 4 * head
        span = slice(h * head, (h + 1) * head)
        for i, to in enumerate((gq, gk, gv)):
            first = h * each + i * head
            to[:, span] = summed[:, first : first + head]
        go[span, :] = turned[h * each + 3 * head : (h + 1) * each, :n]
    for copy in copies:
        copy.wait()


def settle(head, narrow, out, gtok, la, lb, lc):
    _, n, width = la.shape
    shape = jax.ShapeDtypeStruct
    small, wide = shape((n, narrow), F32), shape((n, width), F32)
    return pl.pallas_call(
        lambda *refs: settle_kernel(head, *refs),
        name="settle",
        out_shape=[shape(out.shape, BF16)] * 2 + [small] * 3 + [shape((narrow, n), F32), wide, wide],
        in_specs=[ANY] * 2 + [VMEM] * 3,
        out_specs=[VMEM] * 8,
        scratch_shapes=[pltpu.VMEM((128, width), F32), DMA((2,))],
        compiler_params=pltpu.CompilerParams(vmem_limit_bytes=64 << 20),
    )(out, gtok, la, lb, lc)


def fetch_plain(dp, mp, tok, cot, pa, pb, pc, vec):
    d, m = lax.axis_index("dp"), lax.axis_index("mp")
    core = d % 2
    swap = [(i, i ^ 1) for i in range(dp)]

    def sequence(rows):
        whole = lax.all_gather(rows, "mp", axis=1, tiled=True)
        other = lax.ppermute(whole, "dp", swap)
        return jnp.where(m // 2 == core, whole, other)[m % 2]

    def weight(part):
        plane = lax.all_gather(part, "dp", axis=0, tiled=True)
        return lax.dynamic_slice_in_dim(lax.all_gather(plane, "mp"), 2 * core, 2, 0)

    half = tok.shape[1] * mp // 2
    ct = lax.dynamic_slice_in_dim(sequence(cot), core * half, half, 0)
    return (
        sequence(tok), ct, weight(pa), weight(pb), weight(pc), lax.all_gather(vec, "dp"), lax.all_gather(vec, "mp"),
    )


def deliver_plain(dp, mp, da, db, dc, out, gtok, rows, quarter):
    d, m = lax.axis_index("dp"), lax.axis_index("mp")
    core = d % 2
    swap = [(i, i ^ 1) for i in range(dp)]

    def grad(part):
        wide = jnp.zeros((mp,) + part.shape[1:], F32)
        wide = lax.dynamic_update_slice_in_dim(wide, part.astype(F32), 2 * core, 0)
        mine = lax.psum_scatter(wide, "mp", scatter_dimension=0, tiled=True)[0]
        return lax.psum_scatter(mine, "dp", scatter_dimension=0, tiled=True)[None]

    def home(half):
        both = jnp.zeros((2,) + half.shape, half.dtype)
        both = lax.dynamic_update_slice_in_dim(both, half[None], core, 0)
        both = lax.dynamic_update_slice_in_dim(both, lax.ppermute(half, "dp", swap)[None], 1 - core, 0)
        all_rows = lax.all_gather(both.reshape(mp, quarter, -1), "mp")
        mine = lax.dynamic_slice_in_dim(all_rows, 2 * core, 2, 0)
        return lax.dynamic_slice_in_dim(mine, m, 1, 1)[:, 0]

    return grad(da), grad(db), grad(dc), home(out), home(gtok)


def layer_plain(
    dp, mp, tokens, cotangent, w_query, w_key, w_value, w_out, w_inner, w_outer,
    gain_attn, shift_attn, gain_ffn, shift_ffn, seq_lengths, rand_blocks,
):
    d, m = lax.axis_index("dp"), lax.axis_index("mp")
    core = d % 2
    swap = [(i, i ^ 1) for i in range(dp)]
    quarter, width = tokens.shape[1:]
    seq = quarter * mp
    half = seq // 2
    per, nblocks, picks = rand_blocks.shape
    cols = w_query.shape[1]
    head = cols // per
    block = seq // nblocks
    rows = w_query.shape[0]
    vec_rows = [v.astype(F32) for v in (gain_attn, shift_attn, gain_ffn, shift_ffn)]
    vec_rows += [seq_lengths.astype(F32)]
    flat = rand_blocks.astype(F32).reshape(-1)
    vec_rows += [flat[:128], flat[128:]]
    vec = jnp.stack([jnp.pad(v, (0, 128 - v.shape[0])) for v in vec_rows] + [jnp.zeros(128, F32)])
    pa = jnp.concatenate([w_query, w_key, w_value, w_out.T], 1)
    pb, pc = w_inner, w_outer.T
    x, ct, ga, gb, gc, gvd, gvz = fetch_plain(dp, mp, tokens, cotangent, pa, pb, pc, vec)
    norms = jnp.swapaxes(gvd[:, :4, :rows], 0, 1).reshape(4, width)
    g1, b1, g2, b2 = (norms[i][None] for i in range(4))
    owner = d - core + m // 2
    lens = lax.dynamic_slice_in_dim(gvd[:, 4, :2], owner, 1, 0)[0]
    length = jnp.where(m % 2 == 0, lens[0], lens[1]).astype(jnp.int32)
    picked = lax.dynamic_slice_in_dim(gvz, 2 * core, 2, 0)
    picked = picked[:, 5:7].reshape(2, 256)[:, : per * nblocks * picks].astype(jnp.int32)
    picked = picked.reshape(2, per, nblocks, picks)

    r = jnp.arange(nblocks)
    near = (r[:, None] == 0) | (r[:, None] == nblocks - 1) | (r[None] == 0) | (r[None] == nblocks - 1)
    near = near | (jnp.abs(r[:, None] - r[None]) <= 1)
    hits = jnp.any(picked[:, :, :, :, None] == r, axis=3) | near
    bias = jnp.where(jnp.swapaxes(hits, 2, 3), 0.0, NEG).astype(BF16)
    bias = jnp.repeat(bias, block, axis=3)
    pos = jnp.arange(seq)
    hot = jnp.concatenate([pos[None] // block == r[:, None], pos[None] >= length, jnp.zeros((15, seq), bool)], 0)
    hot = hot.astype(BF16)

    def mine(values):
        return lax.dynamic_slice_in_dim(values, core * half, half, 0)

    def theirs(values):
        return lax.dynamic_slice_in_dim(values, (1 - core) * half, half, 0)

    def pair_sum(partial):
        return mine(partial) + lax.ppermute(theirs(partial).astype(BF16), "dp", swap).astype(F32)

    def pair_join(values):
        other = lax.ppermute(values, "dp", swap)
        lo = jnp.where(core == 0, values, other)
        hi = jnp.where(core == 0, other, values)
        return jnp.concatenate([lo, hi], 0)

    def dot(spec, a, b):
        return jnp.einsum(spec, a, b, preferred_element_type=F32)

    a_qkv, a_out = ga[:, :, : 3 * cols], ga[:, :, 3 * cols :]
    qkv = dot("mrc,tr->mct", a_qkv, x).astype(BF16)
    ctx, lse = attend(qkv, bias, hot, head)
    attn = pair_sum(dot("mct,mdc->td", ctx, a_out))
    x_mine = mine(x).astype(F32)

    def norm(z):
        centre = z - jnp.mean(z, -1, keepdims=True)
        inv = lax.rsqrt(jnp.mean(centre * centre, -1, keepdims=True) + EPS)
        return centre * inv, inv

    n1, inv1 = norm(x_mine + attn)
    hidden = n1 * g1 + b1
    hidden_b = pair_join(hidden.astype(BF16))
    inner = dot("td,mdk->tmk", hidden_b, gb)
    cumul = 0.5 * (1.0 + lax.erf(inner * (1.0 / math.sqrt(2.0))))
    active = (inner * cumul).astype(BF16)
    slope = cumul + inner * jnp.exp(-0.5 * inner * inner) * (1.0 / math.sqrt(2.0 * math.pi))
    n2, inv2 = norm(hidden + pair_sum(dot("tmk,mdk->td", active, gc)))
    valid = (core * half + jnp.arange(half) < length).astype(F32)[:, None]
    out = ((n2 * g2 + b2) * valid).astype(BF16)

    def norm_back(e, n, inv):
        return (e - jnp.mean(e, -1, keepdims=True) - n * jnp.mean(e * n, -1, keepdims=True)) * inv

    gy = ct.astype(F32) * valid
    g_mid = norm_back(gy * g2, n2, inv2)
    d_gain2, d_shift2 = jnp.sum(gy * n2, 0), jnp.sum(gy, 0)
    g_ffn = pair_join(g_mid.astype(BF16))
    d_c = dot("td,tmk->mdk", g_ffn, active).astype(BF16)
    g_inner = (dot("td,mdk->tmk", g_ffn, gc) * slope).astype(BF16)
    d_b = dot("td,tmk->mdk", hidden_b, g_inner).astype(BF16)
    g_hidden = g_mid + pair_sum(dot("tmk,mdk->td", g_inner, gb))
    d_gain1, d_shift1 = jnp.sum(g_hidden * n1, 0), jnp.sum(g_hidden, 0)
    g_res = norm_back(g_hidden * g1, n1, inv1)
    g_attn = pair_join(g_res.astype(BF16))
    d_out = dot("td,mct->mdc", g_attn, ctx).astype(BF16)
    g_ctx = dot("td,mdc->mct", g_attn, a_out).astype(BF16)
    sums = jnp.stack([d_gain1, d_shift1, d_gain2, d_shift2] + [jnp.zeros_like(d_gain1)] * 4)
    dq, dk, dv = attend_back(qkv, bias, hot, lse, g_ctx, head)
    dqkv = jnp.concatenate([dq, dk, dv], 1)
    d_qkv = dot("tr,mct->mrc", x, dqkv).astype(BF16)
    d_a = jnp.concatenate([d_qkv, d_out], 2)
    gtok = (g_res + pair_sum(dot("mct,mrc->tr", dqkv, a_qkv))).astype(BF16)
    ra, rb, rc, out, gtok = deliver_plain(dp, mp, d_a, d_b, d_c, out, gtok, rows, quarter)
    sums = lax.psum(sums, ("dp", "mp"))
    ra, rb, rc = (jnp.sum(v.astype(F32), 0) for v in (ra, rb, rc))
    sums = lax.dynamic_slice_in_dim(sums, d * rows, rows, 1)
    return (
        out, gtok, ra[:, :cols], ra[:, cols : 2 * cols], ra[:, 2 * cols : 3 * cols], ra[:, 3 * cols :].T, rb, rc.T,
        sums[0], sums[1], sums[2], sums[3],
    )


def layer(
    dp, mp, tokens, cotangent, w_query, w_key, w_value, w_out, w_inner, w_outer,
    gain_attn, shift_attn, gain_ffn, shift_ffn, seq_lengths, rand_blocks,
):
    rows, cols = w_query.shape
    per, nblocks, picks = rand_blocks.shape
    if not (dp == 8 and mp == 4 and rows % 16 == 0 and 4 * cols == 8 * rows and tokens.shape[0] == 2):
        return layer_plain(
            dp, mp, tokens, cotangent, w_query, w_key, w_value, w_out, w_inner, w_outer,
            gain_attn, shift_attn, gain_ffn, shift_ffn, seq_lengths, rand_blocks,
        )
    gains = jnp.pad(jnp.stack([gain_attn, shift_attn, gain_ffn, shift_ffn]), ((0, 12), (0, 128 - rows)))
    picked = jnp.swapaxes(rand_blocks, 1, 2)
    *landed, sums = fused_layer(
        mp, tokens, cotangent, w_query, w_key, w_value, w_out, w_inner, w_outer.T, gains, seq_lengths, picked
    )
    *grads, grad_outer = settle(cols // per, cols, *landed)
    return *grads, grad_outer.T, *(sums[i, :rows] for i in range(4))


def solution(mesh):
    dp, mp = mesh.shape["dp"], mesh.shape["mp"]
    act, vec = P("dp", "mp", None), P("dp")
    w_in, w_back = P("dp", "mp"), P("mp", "dp")

    def step(*args):
        return layer(dp, mp, *args)

    return jax.shard_map(
        step,
        mesh=mesh,
        in_specs=(act, act, w_in, w_in, w_in, w_back, w_in, w_back, vec, vec, vec, vec, vec, P("mp", None, None)),
        out_specs=(act, act, w_in, w_in, w_in, w_back, w_in, w_back, vec, vec, vec, vec),
        check_vma=False,
    )
```

```python
import math

import jax
import jax.numpy as jnp
from jax import lax
from jax.experimental import pallas as pl
from jax.experimental.pallas import tpu as pltpu
from jax.sharding import PartitionSpec as P

EPS = 1e-06
NEG = -1000000000.0
MESH = pl.DeviceIdType.MESH
F32 = jnp.float32
BF16 = jnp.bfloat16
ANY = pl.BlockSpec(memory_space=pl.ANY)
VMEM = pl.BlockSpec(memory_space=pltpu.VMEM)
DMA = pltpu.SemaphoreType.DMA


class Place:
    def __init__(self):
        self.d = lax.axis_index("dp")
        self.m = lax.axis_index("mp")
        self.c = lax.rem(self.d, 2)
        self.base = self.d - self.c
        self.sib = self.d + 1 - 2 * self.c
        bx = lax.rem(lax.div(self.d, 2), 2)
        by = lax.rem(lax.div(self.d, 4), 2)
        self.xp = self.d + 2 - 4 * bx
        self.yp = self.d + 4 - 8 * by
        self.bx = self.xp - self.c
        self.by = self.yp - self.c
        self.bd = self.bx + 4 - 8 * by
        self.h = lax.div(self.m, 2)
        self.a = lax.rem(self.m, 2)
        self.close = self.h == self.c
        self.inner = jnp.logical_and(self.h != self.c, self.a + self.h == 1)
        self.outer = jnp.logical_and(self.h != self.c, self.a + self.h != 1)


def remote(src, dst, ssem, rsem, dev):
    return pltpu.make_async_remote_copy(
        src_ref=src, dst_ref=dst, send_sem=ssem, recv_sem=rsem, device_id=dev, device_id_type=MESH
    )


def push(src, dst, ssem, rsem, dev, same):
    @pl.when(same)
    def _():
        pltpu.make_async_copy(src, dst, rsem).start()

    @pl.when(jnp.logical_not(same))
    def _():
        remote(src, dst, ssem, rsem, dev).start()


def pushed(src, dst, ssem, rsem, dev, same):
    @pl.when(jnp.logical_not(same))
    def _():
        remote(src, dst, ssem, rsem, dev).wait_send()


def got(dst, ssem, rsem, dev):
    remote(dst, dst, ssem, rsem, dev).wait_recv()


def greet(peers):
    barrier = pltpu.get_barrier_semaphore()
    for dev in peers:
        pl.semaphore_signal(barrier, inc=1, device_id=dev, device_id_type=MESH)
    pl.semaphore_wait(barrier, len(peers))


def dots(a, b, ca, cb):
    return lax.dot_general(a, b, (((ca,), (cb,)), ((), ())), preferred_element_type=F32)


def column_peers(p, mp):
    peers = []
    for k in range(1, mp):
        z = lax.rem(p.m + k, mp)
        peers += [(p.base, z), (p.base + 1, z)]
    return peers


class Gather:
    def __init__(self, p, src, dst, first, count, sems):
        self.p, self.src, self.dst = p, src, dst
        self.zs, self.zr, self.fs, self.fr, self.xs, self.xr, self.ys, self.yr = sems
        self.n = src.shape[0]
        self.cols = pl.ds(first, count)

    def rows(self, a, first, count):
        return self.dst.at[a, pl.ds(first * self.n, count * self.n), self.cols]

    def both(self, first):
        return self.dst.at[:, pl.ds(first * self.n, 2 * self.n), self.cols]

    def z_args(self, k):
        p = self.p
        z = (p.m, p.m + 1 - 2 * p.a, 2 - p.h)[k]
        src = self.src.at[:, self.cols]
        return src, self.rows(p.a, p.d, 1), self.zs.at[k], self.zr.at[2 * p.c + p.a], (p.base + p.h, z)

    def z_send(self):
        for k in (2, 1):
            remote(*self.z_args(k)).start()
        push(*self.z_args(0), self.p.close)

    def pass_on(self):
        p = self.p
        part = self.both(p.base)
        return remote(part, part, self.fs.at[0], self.fr.at[0], (p.d, 3 * p.h))

    def z_mid(self):
        p = self.p

        @pl.when(jnp.logical_not(p.outer))
        def _():
            for core in range(2):
                for a in range(2):
                    got(self.rows(a, p.base + core, 1), self.zs.at[0], self.zr.at[2 * core + a], (p.d, p.m))

        @pl.when(p.inner)
        def _():
            self.pass_on().start()

        @pl.when(p.outer)
        def _():
            self.pass_on().wait_recv()

        self.hop(0, 0).start()
        self.hop(1, 0).start()

    def hop(self, axis, step):
        p = self.p
        peer = p.xp if axis == 0 else p.yp
        s, r = (self.xs, self.xr) if axis == 0 else (self.ys, self.yr)
        part = self.both(p.base) if step == 0 else self.rows(1 - axis, p.by if axis == 0 else p.bx, 2)
        return remote(part, part, s.at[step], r.at[step], (peer, p.m))

    def arrived(self, axis, step):
        p = self.p
        s, r = (self.xs, self.xr) if axis == 0 else (self.ys, self.yr)
        part = self.both(p.bx if axis == 0 else p.by) if step == 0 else self.rows(1 - axis, p.bd, 2)
        got(part, s.at[step], r.at[step], (p.d, p.m))

    def forward(self):
        for axis in range(2):
            self.arrived(axis, 0)
            self.hop(1 - axis, 1).start()

    def land(self):
        self.arrived(1, 1)
        self.arrived(0, 1)

    def finish(self):
        for k in (1, 2):
            remote(*self.z_args(k)).wait_send()
        pushed(*self.z_args(0), self.p.close)

        @pl.when(self.p.inner)
        def _():
            self.pass_on().wait_send()

        for axis in range(2):
            for step in range(2):
                self.hop(axis, step).wait_send()


def gather_sems():
    return [DMA((3,)), DMA((4,)), DMA((1,)), DMA((1,)), DMA((2,)), DMA((2,)), DMA((2,)), DMA((2,))]


class Tokens:
    def __init__(self, p, tok, x, sems):
        self.p, self.tok, self.x = p, tok, x
        self.s, self.r, self.fs, self.fr = sems
        self.piece = tok.shape[1] // 2

    def args(self, i, half):
        p, n = self.p, self.piece
        z = 2 * p.c + i
        dev = (p.base + half, z)
        dst = self.x.at[pl.ds((2 * p.m + half) * n, n), :]
        src = self.tok.at[i, pl.ds(half * n, n), :]
        return (src, dst, self.s.at[2 * i + half], self.r.at[p.m], dev), jnp.logical_and(p.c == half, p.m == z)

    def send(self):
        for i in range(2):
            for half in range(2):
                args, same = self.args(i, half)
                push(*args, same)

    def part(self, q, core):
        return self.x.at[pl.ds((2 * q + core) * self.piece, self.piece), :]

    def forward(self, mp):
        p = self.p
        for q in range(mp):
            got(self.part(q, p.c), self.s.at[0], self.r.at[q], (p.d, p.m))
            remote(self.part(q, p.c), self.part(q, p.c), self.fs.at[q], self.fr.at[q], (p.sib, p.m)).start()

    def land(self, mp):
        p = self.p
        for q in range(mp):
            got(self.part(q, 1 - p.c), self.fs.at[q], self.fr.at[q], (p.d, p.m))

    def finish(self, mp):
        p = self.p
        for q in range(mp):
            remote(self.part(q, p.c), self.part(q, p.c), self.fs.at[q], self.fr.at[q], (p.sib, p.m)).wait_send()
        for i in range(2):
            for half in range(2):
                args, same = self.args(i, half)
                pushed(*args, same)


class Quarters:
    def __init__(self, p, src, dst, sems):
        self.p, self.src, self.dst = p, src, dst
        self.s, self.r = sems
        self.n = src.shape[1]

    def args(self, i):
        p = self.p
        z = 2 * p.c + i
        dst = self.dst.at[pl.ds(p.a * self.n, self.n), :]
        same = jnp.logical_and(p.h == p.c, p.m == z)
        return (self.src.at[i], dst, self.s.at[i], self.r.at[p.a], (p.base + p.h, z)), same

    def send(self):
        for i in range(2):
            args, same = self.args(i)
            push(*args, same)

    def finish(self):
        p = self.p
        for a in range(2):
            got(self.dst.at[pl.ds(a * self.n, self.n), :], self.s.at[a], self.r.at[a], (p.d, p.m))
        for i in range(2):
            args, same = self.args(i)
            pushed(*args, same)


class Homewards:
    def __init__(self, p, src, dst, sems):
        self.p, self.src, self.dst = p, src, dst
        self.s, self.r = sems
        self.n = dst.shape[1]

    def args(self, q):
        p = self.p
        src = self.src.at[pl.ds(q * self.n, self.n), :]
        owner = p.base + p.h
        same = jnp.logical_and(owner == p.d, p.m == 2 * p.c + q)
        return (src, self.dst.at[p.a], self.s.at[q], self.r.at[p.a], (owner, 2 * p.c + q)), same

    def send(self, q):
        args, same = self.args(q)
        push(*args, same)

    def finish(self):
        p = self.p
        for i in range(2):
            got(self.dst.at[i], self.s.at[i], self.r.at[i], (p.d, p.m))
        for q in range(2):
            args, same = self.args(q)
            pushed(*args, same)


class Scatter:
    def __init__(self, p, src, out, halves, first, count, axis, bufs, sems):
        self.p, self.src, self.out, self.halves = p, src, out, halves
        self.r1, self.r2, self.r3, self.total, self.met = bufs
        self.s, self.r, self.zs, self.zr = sems
        self.n = out.shape[1]
        self.first, self.count = first, count
        self.cols = pl.ds(first, count)
        self.near, self.far = ((p.xp, p.bx), (p.yp, p.by)) if axis == 0 else ((p.yp, p.by), (p.xp, p.bx))

    def rows(self, first):
        return self.src.at[pl.ds(self.halves[0], len(self.halves)), pl.ds(first * self.n, 2 * self.n), self.cols]

    def hop(self, kind):
        p = self.p
        if kind == 0:
            src, dst, peer = self.rows(p.bd), self.r1, self.near[0]
        elif kind == 1:
            src, dst, peer = self.rows(self.near[1]), self.r2, self.near[0]
        else:
            src, dst, peer = self.r1, self.r3, self.far[0]
        return remote(src, dst, self.s.at[kind], self.r.at[kind], (peer, p.m))

    def second(self):
        self.hop(0).wait_recv()
        self.r1[...] = (self.rows(self.far[1])[...].astype(F32) + self.r1[...].astype(F32)).astype(BF16)
        self.hop(2).start()

    def third(self):
        p = self.p
        self.hop(1).wait_recv()
        self.hop(2).wait_recv()
        self.total[...] = (
            self.rows(p.base)[...].astype(F32) + self.r2[...].astype(F32) + self.r3[...].astype(F32)
        ).astype(BF16)

        @pl.when(p.close)
        def _():
            for args in self.z_args():
                push(*args)

        @pl.when(p.outer)
        def _():
            self.meet().start()

    def meet(self):
        p = self.p
        return remote(self.total, self.met, self.zs.at[0], self.zr.at[3], (p.d, 1 + p.h))

    def z_args(self):
        p = self.p
        slot = jnp.where(p.close, p.a, 2)
        made = []
        for i, a in enumerate(self.halves):
            for core in range(2):
                same = jnp.logical_and(p.c == core, p.m == 2 * p.c + a)
                src = self.total.at[i, pl.ds(core * self.n, self.n), :]
                dst = self.out.at[slot, :, self.cols]
                made.append((src, dst, self.zs.at[2 * i + core], self.zr.at[slot], (p.base + core, 2 * p.c + a), same))
        return made

    def line(self):
        @pl.when(self.p.inner)
        def _():
            self.meet().wait_recv()
            self.total[...] = (self.total[...].astype(F32) + self.met[...].astype(F32)).astype(BF16)
            for args in self.z_args():
                remote(*args[:-1]).start()

    def owned(self):
        for slot in range(3):
            got(self.out.at[slot, :, self.cols], self.zs.at[0], self.zr.at[slot], (self.p.d, self.p.m))

    def finish(self):
        p = self.p
        for kind in range(3):
            self.hop(kind).wait_send()

        @pl.when(p.outer)
        def _():
            self.meet().wait_send()

        @pl.when(p.close)
        def _():
            for args in self.z_args():
                pushed(*args)

        @pl.when(p.inner)
        def _():
            for args in self.z_args():
                remote(*args[:-1]).wait_send()


def start_all(units):
    for kind in range(2):
        for u in units:
            u.hop(kind).start()


class Sums:
    def __init__(self, p, bufs, sems, mp):
        self.p, self.mp = p, mp
        self.mine, self.came, self.parts = bufs
        self.s, self.r, self.zs, self.zr = sems

    def hop(self, i):
        p = self.p
        dev = (p.sib, p.xp, p.yp)[i]
        return remote(self.mine.at[i], self.came.at[i], self.s.at[i], self.r.at[i], (dev, p.m))

    def start(self, values):
        self.mine[0] = values
        self.hop(0).start()

    def step(self, i):
        self.hop(i).wait_recv()
        total = self.mine[i] + self.came[i]
        if i < 2:
            self.mine[i + 1] = total
            self.hop(i + 1).start()
        else:
            self.parts[self.p.m] = total
            for k in range(1, self.mp):
                self.column(k).start()

    def column(self, k):
        p = self.p
        part = self.parts.at[p.m]
        return remote(part, part, self.zs.at[k - 1], self.zr.at[p.m], (p.d, lax.rem(p.m + k, self.mp)))

    def finish(self):
        p = self.p
        for k in range(1, self.mp):
            z = lax.rem(p.m + k, self.mp)
            got(self.parts.at[z], self.zs.at[0], self.zr.at[z], (p.d, p.m))
        total = self.parts[0]
        for z in range(1, self.mp):
            total = total + self.parts[z]
        for i in range(3):
            self.hop(i).wait_send()
        for k in range(1, self.mp):
            self.column(k).wait_send()
        return total


class Swap:
    def __init__(self, p, src, dst, sems, src_first=0, dst_first=0, came_first=0, count=256):
        self.p, self.src, self.dst = p, src, dst
        self.s, self.r = sems
        self.firsts = (src_first, dst_first, came_first)
        self.n = count

    def copy(self, i, side):
        p, n = self.p, self.n
        src_first, dst_first, came_first = self.firsts
        if side == 0:
            src = self.src.at[pl.ds(src_first + i * n, n), :]
            dst = self.dst.at[pl.ds(dst_first + i * n, n), :]
        else:
            src = dst = self.dst.at[pl.ds(came_first + i * n, n), :]
        return remote(src, dst, self.s.at[i], self.r.at[i], (p.sib, p.m))

    def send(self, i):
        self.copy(i, 0).start()

    def recv(self, i):
        self.copy(i, 1).wait_recv()

    def finish(self):
        for i in range(2):
            self.copy(i, 0).wait_send()


def gelu_pair(inner):
    cumul = 0.5 * (1.0 + lax.erf(inner * (1.0 / math.sqrt(2.0))))
    slope = cumul + inner * jnp.exp(-0.5 * inner * inner) * (1.0 / math.sqrt(2.0 * math.pi))
    return inner * cumul, slope


def norm_back(e, n, inv):
    return (e - jnp.mean(e, -1, keepdims=True) - n * jnp.mean(e * n, -1, keepdims=True)) * inv


def norm_rows(z):
    centre = z - jnp.mean(z, -1, keepdims=True)
    inv = lax.rsqrt(jnp.mean(centre * centre, -1, keepdims=True) + EPS)
    return centre * inv, inv


def layer_kernel(mp, head, nblocks, picks, names, *refs):
    r = dict(zip(names, refs, strict=True))
    p = Place()
    x, ga, gb, gc, at, qkv, ctx, gctx = (r[k] for k in ("x", "ga", "gb", "gc", "at", "qkv", "ctx", "gctx"))
    seq, width = x.shape
    half = seq // 2
    rc = half // 2
    group = qkv.shape[0] // 2
    cols = group // 3
    per = cols // head
    heads = 2 * per
    n, narrow = r["wq"].shape
    pa, pick, vec = r["pa"], r["pick"], r["vec"]
    scale = 1.0 / math.sqrt(head)
    mine = pl.multiple_of(p.c * half, half)
    theirs = pl.multiple_of(half - p.c * half, half)
    hw = width // 2

    def sems(key):
        return [v for k, v in r.items() if k.startswith(key + ".")]

    tokens = Tokens(p, r["tok"], x, sems("tok"))
    cots = Quarters(p, r["cot"], r["ct"], sems("cot"))
    each = 4 * head
    ga_parts = [Gather(p, r["pa"], ga, i * each, each, sems(f"ga{i}")) for i in range(per)]
    b0, b1, c0, c1 = (
        Gather(p, r["p" + w], r["g" + w], i * hw, hw, sems(f"g{w}{i}")) for w in "bc" for i in range(2)
    )
    gathers = ga_parts + [b0, b1, c0, c1]
    plane = [lax.rem(p.d + k, 8) for k in range(1, 8)]
    gvec, gpick = r["gvec"], r["gpick"]
    vs, vr, us, ur = sems("vec")
    sums = Sums(p, sems("sumbuf"), sems("sum"), mp)
    home = Homewards(p, r["outb"], r["hout"], sems("home"))
    home_g = Homewards(p, r["gtokb"], r["hgtok"], sems("homeg"))
    pair_attn = Swap(p, r["send"], r["recv"], sems("sw0"), count=rc)
    pair_hid = Swap(p, r["hb"], r["hb"], sems("sw1"), mine, mine, theirs, rc)
    pair_ffn = Swap(p, r["send1"], r["recv1"], sems("sw2"), count=rc)
    pair_gf = Swap(p, r["gf"], r["gf"], sems("sw3"), mine, mine, theirs, rc)
    pair_gh = Swap(p, r["send"], r["recv"], sems("sw4"), count=rc)
    pair_ga = Swap(p, r["gat"], r["gat"], sems("sw5"), mine, mine, theirs, rc)
    pair_gt = Swap(p, r["send1"], r["recv1"], sems("sw6"), count=rc)

    def unit(name, src, halves, first, count, axis):
        return Scatter(p, src, r["l" + name[0]], halves, first, count, axis, sems(f"s{name}b"), sems(f"s{name}s"))

    ua = [unit(f"a{i}", ga, (i % 2,), (i // 2) * each, each, i % 2) for i in range(heads)]
    ub, uc = ([unit(f"{w}{i}", r["d" + w], (0, 1), i * hw, hw, i) for i in range(2)] for w in "bc")

    for h in range(per):
        for i, w in enumerate(("wq", "wk", "wv")):
            pa[:, h * each + i * head : h * each + (i + 1) * head] = r[w][:, h * head : (h + 1) * head]
    flip = r["flip"]
    flip[:, :n] = r["wo_in"][...]
    turned = flip[...].T
    for h in range(per):
        pa[:, h * each + 3 * head : (h + 1) * each] = turned[:n, h * head : (h + 1) * head]
    sub16 = lax.broadcasted_iota(jnp.int32, (16, 128), 0)
    lane16 = lax.broadcasted_iota(jnp.int32, (16, 128), 1)
    table = jnp.zeros((16, 128), F32)
    for h in range(per):
        for j in range(picks):
            for b in range(nblocks):
                here = (sub16 == h * picks + j) & (lane16 == b)
                table = jnp.where(here, r["rand"][h, j, b].astype(F32), table)
    for i in range(2):
        count = r["lens"][i]
        high = lax.div(count, 32)
        table = jnp.where((sub16 == 15) & (lane16 == 2 * i), high.astype(F32), table)
        table = jnp.where((sub16 == 15) & (lane16 == 2 * i + 1), (count - 32 * high).astype(F32), table)
    pick[...] = table.astype(BF16)

    greet(column_peers(p, mp) + [(d, p.m) for d in plane])
    pcopies = [remote(pick, gpick.at[p.m], us.at[k - 1], ur.at[p.m], (p.d, lax.rem(p.m + k, mp))) for k in range(1, mp)]
    pcopies.append(remote(pick, gpick.at[mp], us.at[mp - 1], ur.at[mp], (p.sib, p.m)))
    mine_too = pltpu.make_async_copy(pick, gpick.at[p.m], ur.at[p.m])
    for copy in pcopies + [mine_too]:
        copy.start()
    for g in ga_parts:
        g.z_send()

    @pl.when(jnp.logical_not(p.inner))
    def _():
        b0.z_send()
        tokens.send()

    wide = lax.broadcasted_iota(jnp.int32, (128, width), 1) - p.d * n
    deep = lax.broadcasted_iota(jnp.int32, (128, width), 0)
    spots = jnp.where((wide == deep) & (deep < n), 1.0, 0.0).astype(BF16)
    vec[...] = dots(r["gains"][...], spots, 1, 0).astype(BF16)
    vcopies = [remote(vec, gvec.at[p.d], vs.at[k], vr.at[p.d], (d, p.m)) for k, d in enumerate(plane)]
    vcopies.append(pltpu.make_async_copy(vec, gvec.at[p.d], vr.at[p.d]))
    for g in ga_parts:
        g.z_mid()
    pl.when(p.inner)(b0.z_send)
    ga_parts[0].forward()
    b0.z_mid()
    pl.when(p.inner)(tokens.send)
    for copy in vcopies:
        copy.start()

    for z in range(mp + 1):
        got(gpick.at[z], us.at[0], ur.at[z], (p.d, p.m))
    row = jnp.where(p.close, gpick[p.m, 15:16, :].astype(F32), gpick[mp, 15:16, :].astype(F32))
    lane = lax.broadcasted_iota(jnp.int32, (1, 128), 1)
    high, low = (jnp.sum(jnp.where(lane == 2 * p.a + i, row, 0.0), 1, keepdims=True) for i in range(2))
    length = high * 32.0 + low
    block = seq // nblocks
    sub = lax.broadcasted_iota(jnp.int32, (nblocks, seq), 0)
    place = lax.broadcasted_iota(jnp.int32, (nblocks, seq), 1)
    rb = lax.div(place, block)
    near = (rb == 0) | (rb == nblocks - 1) | (sub == 0) | (sub == nblocks - 1) | (jnp.abs(rb - sub) <= 1)
    spread = lax.broadcasted_iota(jnp.int32, (128, seq), 0) == lax.div(lax.broadcasted_iota(jnp.int32, (128, seq), 1), block)
    spread = jnp.where(spread, 1.0, 0.0).astype(BF16)
    subf = sub.astype(F32)
    for a in range(2):
        wide = dots(gpick[2 * p.c + a], spread, 1, 0)
        for h in range(per):
            hit = near
            for j in range(picks):
                at_row = h * picks + j
                hit = hit | (wide[at_row : at_row + 1] == subf)
            r["bias"][2 * h + a] = jnp.where(hit, 0.0, NEG).astype(BF16)
    qa, ka = r["qa"], r["ka"]
    low = lax.broadcasted_iota(jnp.int32, (16, seq), 0)
    ka[head : head + nblocks, :] = jnp.where(rb == sub, 1.0, 0.0).astype(BF16)
    beyond = lax.broadcasted_iota(jnp.int32, (16, seq), 1).astype(F32) >= length
    ka[head + nblocks :, :] = jnp.where((low == 0) & beyond, 1.0, 0.0).astype(BF16)
    qa[head + nblocks :, :] = jnp.where(low == 0, NEG, 0.0).astype(BF16)

    for g in ga_parts[1:]:
        g.forward()
    tokens.forward(mp)
    b1.z_send()
    c0.z_send()
    c1.z_send()
    b0.forward()
    tokens.land(mp)

    def project(h):
        span = pl.ds(pl.multiple_of(h * each, each), each)
        for a in range(2):
            at[a, span, :] = ga[a, :, span].T
        own_rows = pl.ds(pl.multiple_of(h * each, each), 3 * head)

        def some(j, _):
            rows = pl.ds(pl.multiple_of(j * rc, rc), rc)
            for a in range(2):
                to = pl.ds(pl.multiple_of((2 * h + a) * 3 * head, head), 3 * head)
                qkv[to, rows] = dots(at[a, own_rows, :], x[rows, :], 1, 1).astype(BF16)
            return 0

        lax.fori_loop(0, seq // rc, some, 0)

    def parts(i):
        return [pl.ds(pl.multiple_of((3 * i + part) * head, head), head) for part in range(3)]

    def set_head(i):
        q, k, v = parts(i)
        qa[0:head, :] = (qkv[q, :].astype(F32) * scale).astype(BF16)
        qa[head : head + nblocks, :] = r["bias"][i]
        ka[0:head, :] = qkv[k, :]
        return q, k, v

    def attend_head(i, _):
        for h in range(per):

            @pl.when(i == 2 * h)
            def _():
                ga_parts[h].land()

        @pl.when(lax.rem(i, 2) == 0)
        def _():
            project(lax.div(i, 2))

        q, k, v = set_head(i)
        own_rows = pl.ds(pl.multiple_of(i * head, head), head)
        for j in range(2):
            span = slice(j * half, (j + 1) * half)
            scores = dots(ka[...], qa[:, span], 0, 0)
            peak = jnp.max(scores, 0, keepdims=True)
            weights = jnp.exp(scores - peak)
            total = jnp.sum(weights, 0, keepdims=True)
            mixed = jnp.dot(qkv[v, :], weights.astype(BF16), preferred_element_type=F32)
            ctx[own_rows, span] = (mixed / total).astype(BF16)
            r["lse"][i, :, span] = peak + jnp.log(total)

        late = jnp.where(p.outer, 1, 0)

        @pl.when(i == 0 + late)
        def _():
            b1.z_mid()

        @pl.when(i == 2 + late)
        def _():
            c0.z_mid()

        @pl.when(i == 3)
        def _():
            b1.forward()

        @pl.when(i == 4 + late)
        def _():
            c1.z_mid()
            cots.send()

        return 0

    lax.fori_loop(0, heads, attend_head, 0)

    wo = r["wo"]
    for i in range(heads):
        wo[i * head : (i + 1) * head, :] = at[i % 2, (i // 2) * each + 3 * head : (i // 2 + 1) * each, :]
    norms = r["norms"]
    for d in range(8):
        got(gvec.at[d], vs.at[0], vr.at[d], (p.d, p.m))
    vecs = gvec[0].astype(F32)
    for d in range(1, 8):
        vecs = vecs + gvec[d].astype(F32)
    norms[...] = vecs
    g1, s1, g2, s2 = (norms[i : i + 1] for i in range(4))

    def attn_part(first):
        return dots(ctx[:, pl.ds(first, rc)], wo[...], 0, 0)

    for i in range(2):
        r["send"][i * rc : (i + 1) * rc, :] = attn_part(pl.multiple_of(theirs + i * rc, rc)).astype(BF16)
        pair_attn.send(i)
    c0.forward()
    for i in range(2):
        rows = pl.ds(pl.multiple_of(mine + i * rc, rc), rc)
        here = slice(i * rc, (i + 1) * rc)
        part = attn_part(pl.multiple_of(mine + i * rc, rc))
        pair_attn.recv(i)
        n1, inv = norm_rows(x[rows, :].astype(F32) + part + r["recv"][here, :].astype(F32))
        hidden = n1 * g1 + s1
        r["n1"][here, :] = n1
        r["inv1"][here, :] = jnp.broadcast_to(inv, (rc, 128))
        r["res"][here, :] = hidden
        r["hb"][rows, :] = hidden.astype(BF16)
        pair_hid.send(i)

    b0.land()
    b1.land()

    def up(i, _):
        for k in range(2):

            @pl.when(i == 2 + k)
            def _():
                pair_hid.recv(k)

        rows = pl.ds(pl.multiple_of(lax.rem(2 * p.c + i, 4) * rc, rc), rc)
        for a in range(2):
            active, slope = gelu_pair(dots(r["hb"][rows, :], gb[a], 1, 0))
            r["act"][rows, a * width : (a + 1) * width] = active.astype(BF16)
            r["slope"][rows, a * width : (a + 1) * width] = slope.astype(BF16)
        return 0

    lax.fori_loop(0, 4, up, 0)
    c1.forward()
    c0.land()
    c1.land()

    def ffn_part(rows):
        return dots(r["act"][rows, :width], gc[0], 1, 1) + dots(r["act"][rows, width:], gc[1], 1, 1)

    for i in range(2):
        r["send1"][i * rc : (i + 1) * rc, :] = ffn_part(pl.ds(pl.multiple_of(theirs + i * rc, rc), rc)).astype(BF16)
        pair_ffn.send(i)
    cots.finish()
    small = r["small"]
    small[...] = jnp.zeros_like(small)
    for i in range(2):
        rows = pl.ds(pl.multiple_of(mine + i * rc, rc), rc)
        here = slice(i * rc, (i + 1) * rc)
        part = ffn_part(rows)
        pair_ffn.recv(i)
        n2, inv = norm_rows(r["res"][here, :] + part + r["recv1"][here, :].astype(F32))
        pos = (lax.broadcasted_iota(jnp.int32, (rc, 1), 0) + (mine + i * rc)).astype(F32)
        valid = jnp.where(pos < length, 1.0, 0.0)
        r["outb"][here, :] = ((n2 * g2 + s2) * valid).astype(BF16)
        gy = r["ct"][here, :].astype(F32) * valid
        small[2:3, :] += jnp.sum(gy * n2, 0, keepdims=True)
        small[3:4, :] += jnp.sum(gy, 0, keepdims=True)
        g_mid = norm_back(gy * g2, n2, inv)
        r["res"][here, :] = g_mid
        r["gf"][rows, :] = g_mid.astype(BF16)
        pair_gf.send(i)
        home.send(i)

    for g in gathers:
        g.finish()
    for swap in (pair_attn, pair_hid, pair_ffn, pair_gf):
        swap.finish()
    for i in range(2):
        pair_gf.recv(i)

    for k in range(2):

        def grad_c(j, _):
            span = pl.ds(pl.multiple_of(j * rc, rc), rc)
            for a in range(2):
                first = a * width + k * hw
                r["dc"][a, span, k * hw : (k + 1) * hw] = dots(
                    r["gf"][:, span], r["act"][:, first : first + hw], 0, 0
                ).astype(BF16)
            return 0

        lax.fori_loop(0, width // rc, grad_c, 0)
        start_all([uc[k]])

    def back(i, _):
        rows = pl.ds(pl.multiple_of(i * rc, rc), rc)
        for a in range(2):
            part = (rows, slice(a * width, (a + 1) * width))
            r["slope"][part] = (dots(r["gf"][rows, :], gc[a], 1, 0) * r["slope"][part].astype(F32)).astype(BF16)
        return 0

    lax.fori_loop(0, 4, back, 0)

    def hid_part(rows):
        return dots(r["slope"][rows, :width], gb[0], 1, 1) + dots(r["slope"][rows, width:], gb[1], 1, 1)

    for i in range(2):
        r["send"][i * rc : (i + 1) * rc, :] = hid_part(pl.ds(pl.multiple_of(theirs + i * rc, rc), rc)).astype(BF16)
        pair_gh.send(i)
    for u in uc:
        u.second()

    def grad_b(j, _):
        span = pl.ds(pl.multiple_of(j * rc, rc), rc)
        for a in range(2):
            r["db"][a, span, :] = dots(r["hb"][:, span], r["slope"][:, a * width : (a + 1) * width], 0, 0).astype(BF16)
        return 0

    lax.fori_loop(0, width // rc, grad_b, 0)
    start_all(ub)
    for i in range(2):
        rows = pl.ds(pl.multiple_of(mine + i * rc, rc), rc)
        here = slice(i * rc, (i + 1) * rc)
        part = hid_part(rows)
        pair_gh.recv(i)
        gh = r["res"][here, :] + part + r["recv"][here, :].astype(F32)
        n1 = r["n1"][here, :]
        small[0:1, :] += jnp.sum(gh * n1, 0, keepdims=True)
        small[1:2, :] += jnp.sum(gh, 0, keepdims=True)
        g_res = norm_back(gh * g1, n1, r["inv1"][here, 0:1])
        r["res"][here, :] = g_res
        r["gat"][rows, :] = g_res.astype(BF16)
        pair_ga.send(i)
    sums.start(small[...])
    for k in range(4):
        rows = pl.ds(pl.multiple_of(lax.rem(2 * p.c + k, 4) * rc, rc), rc)
        if k >= 2:
            pair_ga.recv(k - 2)
        gctx[:, rows] = dots(wo[...], r["gat"][rows, :], 1, 1).astype(BF16)

    def grad_a(i):
        turn = r["turn"]
        rows = pl.ds(pl.multiple_of(i * 3 * head, head), 3 * head)
        turn[: 3 * head, :] = jnp.dot(qkv[rows, :], x[...], preferred_element_type=F32).astype(BF16)
        rows = pl.ds(pl.multiple_of(i * head, head), head)
        turn[3 * head :, :] = jnp.dot(ctx[rows, :], r["gat"][...], preferred_element_type=F32).astype(BF16)
        ga[lax.rem(i, 2), :, pl.ds(pl.multiple_of(lax.div(i, 2) * each, each), each)] = turn[...].T

    def attend_head_back(i, _):
        q, k, v = set_head(i)
        own_rows = pl.ds(pl.multiple_of(i * head, head), head)
        gk = gv = None
        for j in range(2):
            span = slice(j * half, (j + 1) * half)
            scores = dots(ka[...], qa[:, span], 0, 0)
            probs = jnp.exp(scores - r["lse"][i, :, span])
            grad = gctx[own_rows, span]
            grad_probs = dots(qkv[v, :], grad, 0, 0)
            inner = jnp.sum(probs * grad_probs, 0, keepdims=True)
            grad_scores = (probs * (grad_probs - inner)).astype(BF16)
            qkv[q, span] = (jnp.dot(ka[0:head, :], grad_scores, preferred_element_type=F32) * scale).astype(BF16)
            dk = dots(qa[0:head, span], grad_scores, 1, 1)
            dv = dots(grad, probs.astype(BF16), 1, 1)
            gk, gv = (dk, dv) if gk is None else (gk + dk, gv + dv)
        qkv[k, :] = gk.astype(BF16)
        qkv[v, :] = gv.astype(BF16)

        grad_a(i)
        for k in range(1, heads):

            @pl.when(i == k)
            def _():
                if k == 1:
                    for u in uc:
                        u.third()
                if k == 2:
                    for u in ub:
                        u.second()
                    start_all(ua[:2])
                if k == 3:
                    for u in uc:
                        u.line()
                if k == 4:
                    for u in ub:
                        u.third()
                    for u in ua[:2]:
                        u.second()
                if k == 5:
                    for u in ub:
                        u.line()
                    for u in ua[2:4]:
                        u.second()
                if k % 2 == 1:
                    sums.step(k // 2)
                if k >= 2:
                    start_all([ua[k]])

        return 0

    lax.fori_loop(0, heads, attend_head_back, 0)

    def tok_part(rows):
        total = None
        for i in range(heads):
            mine_rows = slice(i * 3 * head, (i + 1) * 3 * head)
            first = (i // 2) * each
            part = dots(qkv[mine_rows, rows], at[i % 2, first : first + 3 * head, :], 0, 0)
            total = part if total is None else total + part
        return total

    for i in range(2):
        r["send1"][i * rc : (i + 1) * rc, :] = tok_part(pl.ds(pl.multiple_of(theirs + i * rc, rc), rc)).astype(BF16)
        pair_gt.send(i)
    for i in range(2):
        rows = pl.ds(pl.multiple_of(mine + i * rc, rc), rc)
        here = slice(i * rc, (i + 1) * rc)
        part = tok_part(rows)
        pair_gt.recv(i)
        r["gtokb"][here, :] = (r["res"][here, :] + part + r["recv1"][here, :].astype(F32)).astype(BF16)
        home_g.send(i)
    for u in ua[:2]:
        u.third()
    for u in ua[4:]:
        u.second()
    for u in ua[2:4]:
        u.third()
    for u in ua[:2]:
        u.line()
    for u in ua[4:]:
        u.third()
    for u in ua[2:]:
        u.line()
    summed = sums.finish()
    r["sums"][...] = pltpu.roll(summed, width - p.d * n, 1)[:, :128]

    for u in uc + ub:
        u.owned()
    for u in ua:
        pl.when(p.a == u.halves[0])(u.owned)
    home.finish()
    home_g.finish()
    tokens.finish(mp)
    for swap in (pair_gh, pair_ga, pair_gt):
        swap.finish()
    for u in ua + ub + uc:
        u.finish()
    for copy in vcopies[:-1] + pcopies:
        copy.wait_send()


def fused_layer(mp, tok, cot, wq, wk, wv, wo, w_inner, w_outer, gains, lens, rand):
    n, narrow = wq.shape
    quarter, width = tok.shape[1:]
    per, picks, nblocks = rand.shape
    head = narrow // per
    seq = quarter * mp
    half = seq // 2
    group = 3 * per * head
    shape = jax.ShapeDtypeStruct
    SMEM = pl.BlockSpec(memory_space=pltpu.SMEM)
    names = ["tok", "cot", "wq", "wk", "wv", "wo_in", "pb", "pc", "gains", "lens", "rand"]
    outs = {
        "hout": (shape((2, quarter, width), BF16), ANY),
        "hgtok": (shape((2, quarter, width), BF16), ANY),
        **{k: (shape((3, n, width), BF16), ANY) for k in ("la", "lb", "lc")},
        "sums": (shape((8, 128), F32), VMEM),
    }
    weight = ((2, 8 * n, width), BF16)
    rows_b, half_b, half_f = ((seq, width), BF16), ((half, width), BF16), ((half, width), F32)
    bufs = {
        "x": rows_b, "ga": weight, "gb": weight, "gc": weight, "at": weight, "db": weight, "dc": weight,
        "qkv": ((2 * group, seq), BF16), "ctx": ((2 * per * head, seq), BF16), "gctx": ((2 * per * head, seq), BF16),
        "wo": ((2 * per * head, width), BF16), "lse": ((2 * per, 1, seq), F32), "n1": half_f, "inv1": ((half, 128), F32), "res": half_f,
        "hb": rows_b, "act": ((seq, 2 * width), BF16), "slope": ((seq, 2 * width), BF16), "gf": rows_b, "gat": rows_b,
        "send": half_b, "recv": half_b, "send1": half_b, "recv1": half_b, "outb": half_b, "gtokb": half_b, "ct": half_b,
        "gvec": ((8, 16, width), BF16), "gpick": ((mp + 1, 16, 128), BF16), "norms": ((16, width), F32),
        "pa": ((n, width), BF16), "pick": ((16, 128), BF16), "vec": ((16, width), BF16),
        "flip": ((narrow, 128), BF16),
        "bias": ((2 * per, nblocks, seq), BF16), "qa": ((head + nblocks + 16, seq), BF16), "ka": ((head + nblocks + 16, seq), BF16),
        "small": ((8, width), F32), "turn": ((4 * head, width), BF16),
        "sumbuf.0": ((3, 8, width), F32), "sumbuf.1": ((3, 8, width), F32), "sumbuf.2": ((mp, 8, width), F32),
    }
    pieces = {"a": (4 * head, 2 * per, 1), "b": (width // 2, 2, 2), "c": (width // 2, 2, 2)}
    for w, (count, many, halves) in pieces.items():
        for i in range(many):
            for k in range(5):
                bufs[f"s{w}{i}b.{k}"] = ((halves, 2 * n, count), BF16)
    scratch = {k: pltpu.VMEM(*v) for k, v in bufs.items()}

    def add(key, specs):
        for i, spec in enumerate(specs):
            scratch[f"{key}.{i}"] = spec

    add("tok", [DMA((4,)), DMA((mp,)), DMA((mp,)), DMA((mp,))])
    for key in ("cot", "home", "homeg", *(f"sw{i}" for i in range(7))):
        add(key, [DMA((2,)), DMA((2,))])
    for w, (count, many, _) in pieces.items():
        for i in range(width // count):
            add(f"g{w}{i}", gather_sems())
        for i in range(many):
            add(f"s{w}{i}s", [DMA((3,)), DMA((3,)), DMA((4,)), DMA((4,))])
    add("vec", [DMA((7,)), DMA((8,)), DMA((mp,)), DMA((mp + 1,))])
    add("sum", [DMA((3,)), DMA((3,)), DMA((mp - 1,)), DMA((mp,))])
    names = names + list(outs) + list(scratch)
    return pl.pallas_call(
        lambda *refs: layer_kernel(mp, head, nblocks, picks, names, *refs),
        name="layer",
        out_shape=[o[0] for o in outs.values()],
        in_specs=[ANY] * 2 + [VMEM] * 4 + [ANY] * 2 + [VMEM] + [SMEM] * 2,
        out_specs=[o[1] for o in outs.values()],
        scratch_shapes=list(scratch.values()),
        compiler_params=pltpu.CompilerParams(collective_id=0, has_side_effects=True, vmem_limit_bytes=64 << 20),
    )(tok, cot, wq, wk, wv, wo, w_inner, w_outer, gains, lens, rand)


def attend_kernel(q_ref, k_ref, v_ref, bias_ref, hot_ref, ctx_ref, lse_ref, qa, ka):
    seq = q_ref.shape[2]
    head = q_ref.shape[1]
    scale = 1.0 / math.sqrt(head)
    blocks = bias_ref.shape[2]
    step = min(256, seq)
    qa[0:head, :] = (q_ref[0].astype(F32) * scale).astype(BF16)
    qa[head : head + blocks, :] = bias_ref[0, 0]
    low = lax.broadcasted_iota(jnp.int32, (qa.shape[0] - head - blocks, seq), 0)
    qa[head + blocks :, :] = jnp.where(low == 0, NEG, 0.0).astype(BF16)
    ka[0:head, :] = k_ref[0]
    ka[head:, :] = hot_ref[...]
    for i in range(seq // step):
        cols = slice(i * step, (i + 1) * step)
        scores = lax.dot_general(ka[...], qa[:, cols], (((0,), (0,)), ((), ())), preferred_element_type=F32)
        peak = jnp.max(scores, 0, keepdims=True)
        weights = jnp.exp(scores - peak)
        total = jnp.sum(weights, 0, keepdims=True)
        mixed = jnp.dot(v_ref[0], weights.astype(BF16), preferred_element_type=F32)
        ctx_ref[0, :, cols] = (mixed / total).astype(BF16)
        lse_ref[0, 0, :, cols] = peak + jnp.log(total)


def head_specs(head, seq, per, blocks, hot_rows):
    row = lambda part: pl.BlockSpec((1, head, seq), lambda m, h: (m, part * per + h, 0))
    return (
        [row(0), row(1), row(2)],
        pl.BlockSpec((1, 1, blocks, seq), lambda m, h: (m, h, 0, 0)),
        pl.BlockSpec((hot_rows, seq), lambda m, h: (0, 0)),
        pl.BlockSpec((1, 1, 1, seq), lambda m, h: (m, h, 0, 0)),
        row(0),
    )


def attend(qkv, bias, hot, head):
    groups, width, seq = qkv.shape
    per = width // (3 * head)
    rows, bias_spec, hot_spec, line, out = head_specs(head, seq, per, bias.shape[2], hot.shape[0])
    deep = head + hot.shape[0]
    return pl.pallas_call(
        attend_kernel,
        name="attend",
        grid=(groups, per),
        out_shape=[
            jax.ShapeDtypeStruct((groups, per * head, seq), BF16),
            jax.ShapeDtypeStruct((groups, per, 1, seq), F32),
        ],
        in_specs=rows + [bias_spec, hot_spec],
        out_specs=[out, line],
        scratch_shapes=[pltpu.VMEM((deep, seq), BF16), pltpu.VMEM((deep, seq), BF16)],
        compiler_params=pltpu.CompilerParams(vmem_limit_bytes=48 << 20),
    )(qkv, qkv, qkv, bias, hot)


def attend_back_kernel(q_ref, k_ref, v_ref, bias_ref, hot_ref, lse_ref, g_ref, dq_ref, dk_ref, dv_ref, qa, ka, ak, av):
    seq = q_ref.shape[2]
    head = q_ref.shape[1]
    scale = 1.0 / math.sqrt(head)
    blocks = bias_ref.shape[2]
    step = min(256, seq)
    qa[0:head, :] = (q_ref[0].astype(F32) * scale).astype(BF16)
    qa[head : head + blocks, :] = bias_ref[0, 0]
    low = lax.broadcasted_iota(jnp.int32, (qa.shape[0] - head - blocks, seq), 0)
    qa[head + blocks :, :] = jnp.where(low == 0, NEG, 0.0).astype(BF16)
    ka[0:head, :] = k_ref[0]
    ka[head:, :] = hot_ref[...]
    for i in range(seq // step):
        cols = slice(i * step, (i + 1) * step)
        scores = lax.dot_general(ka[...], qa[:, cols], (((0,), (0,)), ((), ())), preferred_element_type=F32)
        probs = jnp.exp(scores - lse_ref[0, 0, :, cols])
        grad = g_ref[0, :, cols]
        grad_probs = lax.dot_general(v_ref[0], grad, (((0,), (0,)), ((), ())), preferred_element_type=F32)
        inner = jnp.sum(probs * grad_probs, 0, keepdims=True)
        grad_scores = (probs * (grad_probs - inner)).astype(BF16)
        dq_ref[0, :, cols] = (jnp.dot(k_ref[0], grad_scores, preferred_element_type=F32) * scale).astype(BF16)
        gk = lax.dot_general(qa[0:head, cols], grad_scores, (((1,), (1,)), ((), ())), preferred_element_type=F32)
        gv = lax.dot_general(grad, probs.astype(BF16), (((1,), (1,)), ((), ())), preferred_element_type=F32)
        if i == 0:
            ak[...] = gk
            av[...] = gv
        else:
            ak[...] += gk
            av[...] += gv
    dk_ref[0] = ak[...].astype(BF16)
    dv_ref[0] = av[...].astype(BF16)


def attend_back(qkv, bias, hot, lse, grad, head):
    groups, width, seq = qkv.shape
    per = width // (3 * head)
    rows, bias_spec, hot_spec, line, out = head_specs(head, seq, per, bias.shape[2], hot.shape[0])
    deep = head + hot.shape[0]
    return pl.pallas_call(
        attend_back_kernel,
        name="attend_back",
        grid=(groups, per),
        out_shape=[jax.ShapeDtypeStruct((groups, per * head, seq), BF16)] * 3,
        in_specs=rows + [bias_spec, hot_spec, line, out],
        out_specs=[out] * 3,
        scratch_shapes=[
            pltpu.VMEM((deep, seq), BF16),
            pltpu.VMEM((deep, seq), BF16),
            pltpu.VMEM((head, seq), F32),
            pltpu.VMEM((head, seq), F32),
        ],
        compiler_params=pltpu.CompilerParams(vmem_limit_bytes=48 << 20),
    )(qkv, qkv, qkv, bias, hot, lse, grad)


def settle_kernel(
    head, out, gtok, la, lb, lc, sums, out_to, gtok_to, gq, gk, gv, go, gb, gc, s0, s1, s2, s3, va, vb, vc, turn, sem
):
    pairs = ((lc, vc), (lb, vb), (la, va), (out, out_to), (gtok, gtok_to))
    copies = [pltpu.make_async_copy(src, dst, sem.at[i]) for i, (src, dst) in enumerate(pairs)]
    for copy in copies:
        copy.start()

    def total(land):
        return land[0].astype(F32) + land[1].astype(F32) + land[2].astype(F32)

    n = gb.shape[0]
    for i, to in enumerate((s0, s1, s2, s3)):
        to[...] = sums[i, :n]
    copies[0].wait()
    gc[...] = total(vc)
    copies[1].wait()
    gb[...] = total(vb)
    copies[2].wait()
    summed = total(va)
    turn[:n, :] = summed
    turned = turn[...].T
    for h in range(gq.shape[1] // head):
        each = 4 * head
        span = slice(h * head, (h + 1) * head)
        for i, to in enumerate((gq, gk, gv)):
            first = h * each + i * head
            to[:, span] = summed[:, first : first + head]
        go[span, :] = turned[h * each + 3 * head : (h + 1) * each, :n]
    for copy in copies[3:]:
        copy.wait()


def settle(head, narrow, out, gtok, la, lb, lc, sums):
    _, n, width = la.shape
    shape = jax.ShapeDtypeStruct
    small, wide = shape((n, narrow), F32), shape((n, width), F32)
    land = pltpu.VMEM(la.shape, BF16)
    return pl.pallas_call(
        lambda *refs: settle_kernel(head, *refs),
        name="settle",
        out_shape=[shape(out.shape, BF16)] * 2 + [small] * 3 + [shape((narrow, n), F32), wide, wide] + [shape((n,), F32)] * 4,
        in_specs=[ANY] * 5 + [VMEM],
        out_specs=[VMEM] * 12,
        scratch_shapes=[land, land, land, pltpu.VMEM((128, width), F32), DMA((5,))],
        compiler_params=pltpu.CompilerParams(vmem_limit_bytes=64 << 20),
    )(out, gtok, la, lb, lc, sums)


def fetch_plain(dp, mp, tok, cot, pa, pb, pc, vec):
    d, m = lax.axis_index("dp"), lax.axis_index("mp")
    core = d % 2
    swap = [(i, i ^ 1) for i in range(dp)]

    def sequence(rows):
        whole = lax.all_gather(rows, "mp", axis=1, tiled=True)
        other = lax.ppermute(whole, "dp", swap)
        return jnp.where(m // 2 == core, whole, other)[m % 2]

    def weight(part):
        plane = lax.all_gather(part, "dp", axis=0, tiled=True)
        return lax.dynamic_slice_in_dim(lax.all_gather(plane, "mp"), 2 * core, 2, 0)

    half = tok.shape[1] * mp // 2
    ct = lax.dynamic_slice_in_dim(sequence(cot), core * half, half, 0)
    return (
        sequence(tok), ct, weight(pa), weight(pb), weight(pc), lax.all_gather(vec, "dp"), lax.all_gather(vec, "mp"),
    )


def deliver_plain(dp, mp, da, db, dc, out, gtok, rows, quarter):
    d, m = lax.axis_index("dp"), lax.axis_index("mp")
    core = d % 2
    swap = [(i, i ^ 1) for i in range(dp)]

    def grad(part):
        wide = jnp.zeros((mp,) + part.shape[1:], F32)
        wide = lax.dynamic_update_slice_in_dim(wide, part.astype(F32), 2 * core, 0)
        mine = lax.psum_scatter(wide, "mp", scatter_dimension=0, tiled=True)[0]
        return lax.psum_scatter(mine, "dp", scatter_dimension=0, tiled=True)[None]

    def home(half):
        both = jnp.zeros((2,) + half.shape, half.dtype)
        both = lax.dynamic_update_slice_in_dim(both, half[None], core, 0)
        both = lax.dynamic_update_slice_in_dim(both, lax.ppermute(half, "dp", swap)[None], 1 - core, 0)
        all_rows = lax.all_gather(both.reshape(mp, quarter, -1), "mp")
        mine = lax.dynamic_slice_in_dim(all_rows, 2 * core, 2, 0)
        return lax.dynamic_slice_in_dim(mine, m, 1, 1)[:, 0]

    return grad(da), grad(db), grad(dc), home(out), home(gtok)


def layer_plain(
    dp, mp, tokens, cotangent, w_query, w_key, w_value, w_out, w_inner, w_outer,
    gain_attn, shift_attn, gain_ffn, shift_ffn, seq_lengths, rand_blocks,
):
    d, m = lax.axis_index("dp"), lax.axis_index("mp")
    core = d % 2
    swap = [(i, i ^ 1) for i in range(dp)]
    quarter, width = tokens.shape[1:]
    seq = quarter * mp
    half = seq // 2
    per, nblocks, picks = rand_blocks.shape
    cols = w_query.shape[1]
    head = cols // per
    block = seq // nblocks
    rows = w_query.shape[0]
    vec_rows = [v.astype(F32) for v in (gain_attn, shift_attn, gain_ffn, shift_ffn)]
    vec_rows += [seq_lengths.astype(F32)]
    flat = rand_blocks.astype(F32).reshape(-1)
    vec_rows += [flat[:128], flat[128:]]
    vec = jnp.stack([jnp.pad(v, (0, 128 - v.shape[0])) for v in vec_rows] + [jnp.zeros(128, F32)])
    pa = jnp.concatenate([w_query, w_key, w_value, w_out.T], 1)
    pb, pc = w_inner, w_outer.T
    x, ct, ga, gb, gc, gvd, gvz = fetch_plain(dp, mp, tokens, cotangent, pa, pb, pc, vec)
    norms = jnp.swapaxes(gvd[:, :4, :rows], 0, 1).reshape(4, width)
    g1, b1, g2, b2 = (norms[i][None] for i in range(4))
    owner = d - core + m // 2
    lens = lax.dynamic_slice_in_dim(gvd[:, 4, :2], owner, 1, 0)[0]
    length = jnp.where(m % 2 == 0, lens[0], lens[1]).astype(jnp.int32)
    picked = lax.dynamic_slice_in_dim(gvz, 2 * core, 2, 0)
    picked = picked[:, 5:7].reshape(2, 256)[:, : per * nblocks * picks].astype(jnp.int32)
    picked = picked.reshape(2, per, nblocks, picks)

    r = jnp.arange(nblocks)
    near = (r[:, None] == 0) | (r[:, None] == nblocks - 1) | (r[None] == 0) | (r[None] == nblocks - 1)
    near = near | (jnp.abs(r[:, None] - r[None]) <= 1)
    hits = jnp.any(picked[:, :, :, :, None] == r, axis=3) | near
    bias = jnp.where(jnp.swapaxes(hits, 2, 3), 0.0, NEG).astype(BF16)
    bias = jnp.repeat(bias, block, axis=3)
    pos = jnp.arange(seq)
    hot = jnp.concatenate([pos[None] // block == r[:, None], pos[None] >= length, jnp.zeros((15, seq), bool)], 0)
    hot = hot.astype(BF16)

    def mine(values):
        return lax.dynamic_slice_in_dim(values, core * half, half, 0)

    def theirs(values):
        return lax.dynamic_slice_in_dim(values, (1 - core) * half, half, 0)

    def pair_sum(partial):
        return mine(partial) + lax.ppermute(theirs(partial).astype(BF16), "dp", swap).astype(F32)

    def pair_join(values):
        other = lax.ppermute(values, "dp", swap)
        lo = jnp.where(core == 0, values, other)
        hi = jnp.where(core == 0, other, values)
        return jnp.concatenate([lo, hi], 0)

    def dot(spec, a, b):
        return jnp.einsum(spec, a, b, preferred_element_type=F32)

    a_qkv, a_out = ga[:, :, : 3 * cols], ga[:, :, 3 * cols :]
    qkv = dot("mrc,tr->mct", a_qkv, x).astype(BF16)
    ctx, lse = attend(qkv, bias, hot, head)
    attn = pair_sum(dot("mct,mdc->td", ctx, a_out))
    x_mine = mine(x).astype(F32)

    def norm(z):
        centre = z - jnp.mean(z, -1, keepdims=True)
        inv = lax.rsqrt(jnp.mean(centre * centre, -1, keepdims=True) + EPS)
        return centre * inv, inv

    n1, inv1 = norm(x_mine + attn)
    hidden = n1 * g1 + b1
    hidden_b = pair_join(hidden.astype(BF16))
    inner = dot("td,mdk->tmk", hidden_b, gb)
    cumul = 0.5 * (1.0 + lax.erf(inner * (1.0 / math.sqrt(2.0))))
    active = (inner * cumul).astype(BF16)
    slope = cumul + inner * jnp.exp(-0.5 * inner * inner) * (1.0 / math.sqrt(2.0 * math.pi))
    n2, inv2 = norm(hidden + pair_sum(dot("tmk,mdk->td", active, gc)))
    valid = (core * half + jnp.arange(half) < length).astype(F32)[:, None]
    out = ((n2 * g2 + b2) * valid).astype(BF16)

    def norm_back(e, n, inv):
        return (e - jnp.mean(e, -1, keepdims=True) - n * jnp.mean(e * n, -1, keepdims=True)) * inv

    gy = ct.astype(F32) * valid
    g_mid = norm_back(gy * g2, n2, inv2)
    d_gain2, d_shift2 = jnp.sum(gy * n2, 0), jnp.sum(gy, 0)
    g_ffn = pair_join(g_mid.astype(BF16))
    d_c = dot("td,tmk->mdk", g_ffn, active).astype(BF16)
    g_inner = (dot("td,mdk->tmk", g_ffn, gc) * slope).astype(BF16)
    d_b = dot("td,tmk->mdk", hidden_b, g_inner).astype(BF16)
    g_hidden = g_mid + pair_sum(dot("tmk,mdk->td", g_inner, gb))
    d_gain1, d_shift1 = jnp.sum(g_hidden * n1, 0), jnp.sum(g_hidden, 0)
    g_res = norm_back(g_hidden * g1, n1, inv1)
    g_attn = pair_join(g_res.astype(BF16))
    d_out = dot("td,mct->mdc", g_attn, ctx).astype(BF16)
    g_ctx = dot("td,mdc->mct", g_attn, a_out).astype(BF16)
    sums = jnp.stack([d_gain1, d_shift1, d_gain2, d_shift2] + [jnp.zeros_like(d_gain1)] * 4)
    dq, dk, dv = attend_back(qkv, bias, hot, lse, g_ctx, head)
    dqkv = jnp.concatenate([dq, dk, dv], 1)
    d_qkv = dot("tr,mct->mrc", x, dqkv).astype(BF16)
    d_a = jnp.concatenate([d_qkv, d_out], 2)
    gtok = (g_res + pair_sum(dot("mct,mrc->tr", dqkv, a_qkv))).astype(BF16)
    ra, rb, rc, out, gtok = deliver_plain(dp, mp, d_a, d_b, d_c, out, gtok, rows, quarter)
    sums = lax.psum(sums, ("dp", "mp"))
    ra, rb, rc = (jnp.sum(v.astype(F32), 0) for v in (ra, rb, rc))
    sums = lax.dynamic_slice_in_dim(sums, d * rows, rows, 1)
    return (
        out, gtok, ra[:, :cols], ra[:, cols : 2 * cols], ra[:, 2 * cols : 3 * cols], ra[:, 3 * cols :].T, rb, rc.T,
        sums[0], sums[1], sums[2], sums[3],
    )


def layer(
    dp, mp, tokens, cotangent, w_query, w_key, w_value, w_out, w_inner, w_outer,
    gain_attn, shift_attn, gain_ffn, shift_ffn, seq_lengths, rand_blocks,
):
    rows, cols = w_query.shape
    per, nblocks, picks = rand_blocks.shape
    if not (dp == 8 and mp == 4 and rows % 16 == 0 and 4 * cols == 8 * rows and tokens.shape[0] == 2):
        return layer_plain(
            dp, mp, tokens, cotangent, w_query, w_key, w_value, w_out, w_inner, w_outer,
            gain_attn, shift_attn, gain_ffn, shift_ffn, seq_lengths, rand_blocks,
        )
    gains = jnp.pad(jnp.stack([gain_attn, shift_attn, gain_ffn, shift_ffn]), ((0, 12), (0, 128 - rows)))
    picked = jnp.swapaxes(rand_blocks, 1, 2)
    landed = fused_layer(
        mp, tokens, cotangent, w_query, w_key, w_value, w_out, w_inner, w_outer.T, gains, seq_lengths, picked
    )
    done = settle(cols // per, cols, *landed)
    return *done[:7], done[7].T, *done[8:]


def solution(mesh):
    dp, mp = mesh.shape["dp"], mesh.shape["mp"]
    act, vec = P("dp", "mp", None), P("dp")
    w_in, w_back = P("dp", "mp"), P("mp", "dp")

    def step(*args):
        return layer(dp, mp, *args)

    return jax.shard_map(
        step,
        mesh=mesh,
        in_specs=(act, act, w_in, w_in, w_in, w_back, w_in, w_back, vec, vec, vec, vec, vec, P("mp", None, None)),
        out_specs=(act, act, w_in, w_in, w_in, w_back, w_in, w_back, vec, vec, vec, vec),
        check_vma=False,
    )
```

```python
import math

import jax
import jax.numpy as jnp
from jax import lax
from jax.experimental import pallas as pl
from jax.experimental.pallas import tpu as pltpu
from jax.sharding import PartitionSpec as P

EPS = 1e-06
NEG = -1000000000.0
MESH = pl.DeviceIdType.MESH
F32 = jnp.float32
BF16 = jnp.bfloat16
ANY = pl.BlockSpec(memory_space=pl.ANY)
VMEM = pl.BlockSpec(memory_space=pltpu.VMEM)
DMA = pltpu.SemaphoreType.DMA


class Place:
    def __init__(self):
        self.d = lax.axis_index("dp")
        self.m = lax.axis_index("mp")
        self.c = lax.rem(self.d, 2)
        self.base = self.d - self.c
        self.sib = self.d + 1 - 2 * self.c
        bx = lax.rem(lax.div(self.d, 2), 2)
        by = lax.rem(lax.div(self.d, 4), 2)
        self.xp = self.d + 2 - 4 * bx
        self.yp = self.d + 4 - 8 * by
        self.bx = self.xp - self.c
        self.by = self.yp - self.c
        self.bd = self.bx + 4 - 8 * by
        self.h = lax.div(self.m, 2)
        self.a = lax.rem(self.m, 2)
        self.close = self.h == self.c
        self.inner = jnp.logical_and(self.h != self.c, self.a + self.h == 1)
        self.outer = jnp.logical_and(self.h != self.c, self.a + self.h != 1)


def remote(src, dst, ssem, rsem, dev):
    return pltpu.make_async_remote_copy(
        src_ref=src, dst_ref=dst, send_sem=ssem, recv_sem=rsem, device_id=dev, device_id_type=MESH
    )


def push(src, dst, ssem, rsem, dev, same):
    @pl.when(same)
    def _():
        pltpu.make_async_copy(src, dst, rsem).start()

    @pl.when(jnp.logical_not(same))
    def _():
        remote(src, dst, ssem, rsem, dev).start()


def pushed(src, dst, ssem, rsem, dev, same):
    @pl.when(jnp.logical_not(same))
    def _():
        remote(src, dst, ssem, rsem, dev).wait_send()


def got(dst, ssem, rsem, dev):
    remote(dst, dst, ssem, rsem, dev).wait_recv()


def greet(peers):
    barrier = pltpu.get_barrier_semaphore()
    for dev in peers:
        pl.semaphore_signal(barrier, inc=1, device_id=dev, device_id_type=MESH)
    pl.semaphore_wait(barrier, len(peers))


def dots(a, b, ca, cb):
    return lax.dot_general(a, b, (((ca,), (cb,)), ((), ())), preferred_element_type=F32)


def column_peers(p, mp):
    peers = []
    for k in range(1, mp):
        z = lax.rem(p.m + k, mp)
        peers += [(p.base, z), (p.base + 1, z)]
    return peers


class Gather:
    def __init__(self, p, src, dst, first, count, sems):
        self.p, self.src, self.dst = p, src, dst
        self.zs, self.zr, self.fs, self.fr, self.xs, self.xr, self.ys, self.yr = sems
        self.n = src.shape[0]
        self.cols = pl.ds(first, count)

    def rows(self, a, first, count):
        return self.dst.at[a, pl.ds(first * self.n, count * self.n), self.cols]

    def both(self, first):
        return self.dst.at[:, pl.ds(first * self.n, 2 * self.n), self.cols]

    def z_args(self, k):
        p = self.p
        z = (p.m, p.m + 1 - 2 * p.a, 2 - p.h)[k]
        src = self.src.at[:, self.cols]
        return src, self.rows(p.a, p.d, 1), self.zs.at[k], self.zr.at[2 * p.c + p.a], (p.base + p.h, z)

    def z_send(self):
        for k in (2, 1):
            remote(*self.z_args(k)).start()
        push(*self.z_args(0), self.p.close)

    def pass_on(self):
        p = self.p
        part = self.both(p.base)
        return remote(part, part, self.fs.at[0], self.fr.at[0], (p.d, 3 * p.h))

    def z_mid(self):
        p = self.p

        @pl.when(jnp.logical_not(p.outer))
        def _():
            for core in range(2):
                for a in range(2):
                    got(self.rows(a, p.base + core, 1), self.zs.at[0], self.zr.at[2 * core + a], (p.d, p.m))

        @pl.when(p.inner)
        def _():
            self.pass_on().start()

        @pl.when(p.outer)
        def _():
            self.pass_on().wait_recv()

        self.hop(0, 0).start()
        self.hop(1, 0).start()

    def hop(self, axis, step):
        p = self.p
        peer = p.xp if axis == 0 else p.yp
        s, r = (self.xs, self.xr) if axis == 0 else (self.ys, self.yr)
        part = self.both(p.base) if step == 0 else self.rows(1 - axis, p.by if axis == 0 else p.bx, 2)
        return remote(part, part, s.at[step], r.at[step], (peer, p.m))

    def arrived(self, axis, step):
        p = self.p
        s, r = (self.xs, self.xr) if axis == 0 else (self.ys, self.yr)
        part = self.both(p.bx if axis == 0 else p.by) if step == 0 else self.rows(1 - axis, p.bd, 2)
        got(part, s.at[step], r.at[step], (p.d, p.m))

    def forward(self):
        for axis in range(2):
            self.arrived(axis, 0)
            self.hop(1 - axis, 1).start()

    def land(self):
        self.arrived(1, 1)
        self.arrived(0, 1)

    def finish(self):
        for k in (1, 2):
            remote(*self.z_args(k)).wait_send()
        pushed(*self.z_args(0), self.p.close)

        @pl.when(self.p.inner)
        def _():
            self.pass_on().wait_send()

        for axis in range(2):
            for step in range(2):
                self.hop(axis, step).wait_send()


def gather_sems():
    return [DMA((3,)), DMA((4,)), DMA((1,)), DMA((1,)), DMA((2,)), DMA((2,)), DMA((2,)), DMA((2,))]


class Tokens:
    def __init__(self, p, tok, x, sems):
        self.p, self.tok, self.x = p, tok, x
        self.s, self.r, self.fs, self.fr = sems
        self.piece = tok.shape[1] // 2

    def args(self, i, half):
        p, n = self.p, self.piece
        z = 2 * p.c + i
        dev = (p.base + half, z)
        dst = self.x.at[pl.ds((2 * p.m + half) * n, n), :]
        src = self.tok.at[i, pl.ds(half * n, n), :]
        return (src, dst, self.s.at[2 * i + half], self.r.at[p.m], dev), jnp.logical_and(p.c == half, p.m == z)

    def send(self):
        for i in range(2):
            for half in range(2):
                args, same = self.args(i, half)
                push(*args, same)

    def part(self, q, core):
        return self.x.at[pl.ds((2 * q + core) * self.piece, self.piece), :]

    def forward(self, mp):
        p = self.p
        for q in range(mp):
            got(self.part(q, p.c), self.s.at[0], self.r.at[q], (p.d, p.m))
            remote(self.part(q, p.c), self.part(q, p.c), self.fs.at[q], self.fr.at[q], (p.sib, p.m)).start()

    def land(self, mp):
        p = self.p
        for q in range(mp):
            got(self.part(q, 1 - p.c), self.fs.at[q], self.fr.at[q], (p.d, p.m))

    def finish(self, mp):
        p = self.p
        for q in range(mp):
            remote(self.part(q, p.c), self.part(q, p.c), self.fs.at[q], self.fr.at[q], (p.sib, p.m)).wait_send()
        for i in range(2):
            for half in range(2):
                args, same = self.args(i, half)
                pushed(*args, same)


class Quarters:
    def __init__(self, p, src, dst, sems):
        self.p, self.src, self.dst = p, src, dst
        self.s, self.r = sems
        self.n = src.shape[1]

    def args(self, i):
        p = self.p
        z = 2 * p.c + i
        dst = self.dst.at[pl.ds(p.a * self.n, self.n), :]
        same = jnp.logical_and(p.h == p.c, p.m == z)
        return (self.src.at[i], dst, self.s.at[i], self.r.at[p.a], (p.base + p.h, z)), same

    def send(self):
        for i in range(2):
            args, same = self.args(i)
            push(*args, same)

    def finish(self):
        p = self.p
        for a in range(2):
            got(self.dst.at[pl.ds(a * self.n, self.n), :], self.s.at[a], self.r.at[a], (p.d, p.m))
        for i in range(2):
            args, same = self.args(i)
            pushed(*args, same)


class Homewards:
    def __init__(self, p, src, dst, sems):
        self.p, self.src, self.dst = p, src, dst
        self.s, self.r = sems
        self.n = dst.shape[1]

    def args(self, q):
        p = self.p
        src = self.src.at[pl.ds(q * self.n, self.n), :]
        owner = p.base + p.h
        same = jnp.logical_and(owner == p.d, p.m == 2 * p.c + q)
        return (src, self.dst.at[p.a], self.s.at[q], self.r.at[p.a], (owner, 2 * p.c + q)), same

    def send(self, q):
        args, same = self.args(q)
        push(*args, same)

    def finish(self):
        p = self.p
        for i in range(2):
            got(self.dst.at[i], self.s.at[i], self.r.at[i], (p.d, p.m))
        for q in range(2):
            args, same = self.args(q)
            pushed(*args, same)


class Scatter:
    def __init__(self, p, src, out, halves, first, count, axis, bufs, sems):
        self.p, self.src, self.out, self.halves = p, src, out, halves
        self.r1, self.r2, self.r3, self.total, self.met = bufs
        self.s, self.r, self.zs, self.zr = sems
        self.n = out.shape[1]
        self.first, self.count = first, count
        self.cols = pl.ds(first, count)
        self.near, self.far = ((p.xp, p.bx), (p.yp, p.by)) if axis == 0 else ((p.yp, p.by), (p.xp, p.bx))

    def rows(self, first):
        return self.src.at[pl.ds(self.halves[0], len(self.halves)), pl.ds(first * self.n, 2 * self.n), self.cols]

    def hop(self, kind):
        p = self.p
        if kind == 0:
            src, dst, peer = self.rows(p.bd), self.r1, self.near[0]
        elif kind == 1:
            src, dst, peer = self.rows(self.near[1]), self.r2, self.near[0]
        else:
            src, dst, peer = self.r1, self.r3, self.far[0]
        return remote(src, dst, self.s.at[kind], self.r.at[kind], (peer, p.m))

    def second(self):
        self.hop(0).wait_recv()
        self.r1[...] = (self.rows(self.far[1])[...].astype(F32) + self.r1[...].astype(F32)).astype(BF16)
        self.hop(2).start()

    def third(self):
        p = self.p
        self.hop(1).wait_recv()
        self.hop(2).wait_recv()
        self.total[...] = (
            self.rows(p.base)[...].astype(F32) + self.r2[...].astype(F32) + self.r3[...].astype(F32)
        ).astype(BF16)

        @pl.when(p.close)
        def _():
            for args in self.z_args():
                push(*args)

        @pl.when(p.outer)
        def _():
            self.meet().start()

    def meet(self):
        p = self.p
        return remote(self.total, self.met, self.zs.at[0], self.zr.at[3], (p.d, 1 + p.h))

    def z_args(self):
        p = self.p
        slot = jnp.where(p.close, p.a, 2)
        made = []
        for i, a in enumerate(self.halves):
            for core in range(2):
                same = jnp.logical_and(p.c == core, p.m == 2 * p.c + a)
                src = self.total.at[i, pl.ds(core * self.n, self.n), :]
                dst = self.out.at[slot, :, self.cols]
                made.append((src, dst, self.zs.at[2 * i + core], self.zr.at[slot], (p.base + core, 2 * p.c + a), same))
        return made

    def line(self):
        @pl.when(self.p.inner)
        def _():
            self.meet().wait_recv()
            self.total[...] = (self.total[...].astype(F32) + self.met[...].astype(F32)).astype(BF16)
            for args in self.z_args():
                remote(*args[:-1]).start()

    def owned(self):
        for slot in range(3):
            got(self.out.at[slot, :, self.cols], self.zs.at[0], self.zr.at[slot], (self.p.d, self.p.m))

    def finish(self):
        p = self.p
        for kind in range(3):
            self.hop(kind).wait_send()

        @pl.when(p.outer)
        def _():
            self.meet().wait_send()

        @pl.when(p.close)
        def _():
            for args in self.z_args():
                pushed(*args)

        @pl.when(p.inner)
        def _():
            for args in self.z_args():
                remote(*args[:-1]).wait_send()


def start_all(units):
    for kind in range(2):
        for u in units:
            u.hop(kind).start()


class Sums:
    def __init__(self, p, bufs, sems, mp):
        self.p, self.mp = p, mp
        self.mine, self.came, self.parts = bufs
        self.s, self.r, self.zs, self.zr = sems

    def hop(self, i):
        p = self.p
        dev = (p.sib, p.xp, p.yp)[i]
        return remote(self.mine.at[i], self.came.at[i], self.s.at[i], self.r.at[i], (dev, p.m))

    def start(self, values):
        self.mine[0] = values
        self.hop(0).start()

    def step(self, i):
        self.hop(i).wait_recv()
        total = self.mine[i] + self.came[i]
        if i < 2:
            self.mine[i + 1] = total
            self.hop(i + 1).start()
        else:
            self.parts[self.p.m] = total
            for k in range(1, self.mp):
                self.column(k).start()

    def column(self, k):
        p = self.p
        part = self.parts.at[p.m]
        return remote(part, part, self.zs.at[k - 1], self.zr.at[p.m], (p.d, lax.rem(p.m + k, self.mp)))

    def finish(self):
        p = self.p
        for k in range(1, self.mp):
            z = lax.rem(p.m + k, self.mp)
            got(self.parts.at[z], self.zs.at[0], self.zr.at[z], (p.d, p.m))
        total = self.parts[0]
        for z in range(1, self.mp):
            total = total + self.parts[z]
        for i in range(3):
            self.hop(i).wait_send()
        for k in range(1, self.mp):
            self.column(k).wait_send()
        return total


class Swap:
    def __init__(self, p, src, dst, sems, src_first=0, dst_first=0, came_first=0, count=256):
        self.p, self.src, self.dst = p, src, dst
        self.s, self.r = sems
        self.firsts = (src_first, dst_first, came_first)
        self.n = count

    def copy(self, i, side):
        p, n = self.p, self.n
        src_first, dst_first, came_first = self.firsts
        if side == 0:
            src = self.src.at[pl.ds(src_first + i * n, n), :]
            dst = self.dst.at[pl.ds(dst_first + i * n, n), :]
        else:
            src = dst = self.dst.at[pl.ds(came_first + i * n, n), :]
        return remote(src, dst, self.s.at[i], self.r.at[i], (p.sib, p.m))

    def send(self, i):
        self.copy(i, 0).start()

    def recv(self, i):
        self.copy(i, 1).wait_recv()

    def finish(self):
        for i in range(2):
            self.copy(i, 0).wait_send()


def gelu_pair(inner):
    cumul = 0.5 * (1.0 + lax.erf(inner * (1.0 / math.sqrt(2.0))))
    slope = cumul + inner * jnp.exp(-0.5 * inner * inner) * (1.0 / math.sqrt(2.0 * math.pi))
    return inner * cumul, slope


def norm_back(e, n, inv):
    return (e - jnp.mean(e, -1, keepdims=True) - n * jnp.mean(e * n, -1, keepdims=True)) * inv


def norm_rows(z):
    centre = z - jnp.mean(z, -1, keepdims=True)
    inv = lax.rsqrt(jnp.mean(centre * centre, -1, keepdims=True) + EPS)
    return centre * inv, inv


def layer_kernel(mp, head, nblocks, picks, names, *refs):
    r = dict(zip(names, refs, strict=True))
    p = Place()
    x, ga, gb, gc, at, qkv, ctx, gctx = (r[k] for k in ("x", "ga", "gb", "gc", "at", "qkv", "ctx", "gctx"))
    seq, width = x.shape
    half = seq // 2
    rc = half // 2
    group = qkv.shape[0] // 2
    cols = group // 3
    per = cols // head
    heads = 2 * per
    n, narrow = r["wq"].shape
    pa, pick, vec = r["pa"], r["pick"], r["vec"]
    scale = 1.0 / math.sqrt(head)
    mine = pl.multiple_of(p.c * half, half)
    theirs = pl.multiple_of(half - p.c * half, half)
    hw = width // 2

    def sems(key):
        return [v for k, v in r.items() if k.startswith(key + ".")]

    tokens = Tokens(p, r["tok"], x, sems("tok"))
    cots = Quarters(p, r["cot"], r["ct"], sems("cot"))
    each = 4 * head
    ga_parts = [Gather(p, r["pa"], ga, i * each, each, sems(f"ga{i}")) for i in range(per)]
    b0, b1, c0, c1 = (
        Gather(p, r["p" + w], r["g" + w], i * hw, hw, sems(f"g{w}{i}")) for w in "bc" for i in range(2)
    )
    gathers = ga_parts + [b0, b1, c0, c1]
    plane = [lax.rem(p.d + k, 8) for k in range(1, 8)]
    gvec, gpick = r["gvec"], r["gpick"]
    vs, vr, us, ur = sems("vec")
    sums = Sums(p, sems("sumbuf"), sems("sum"), mp)
    home = Homewards(p, r["outb"], r["hout"], sems("home"))
    home_g = Homewards(p, r["gtokb"], r["hgtok"], sems("homeg"))
    pair_attn = Swap(p, r["send"], r["recv"], sems("sw0"), count=rc)
    pair_hid = Swap(p, r["hb"], r["hb"], sems("sw1"), mine, mine, theirs, rc)
    pair_ffn = Swap(p, r["send1"], r["recv1"], sems("sw2"), count=rc)
    pair_gf = Swap(p, r["gf"], r["gf"], sems("sw3"), mine, mine, theirs, rc)
    pair_gh = Swap(p, r["send"], r["recv"], sems("sw4"), count=rc)
    pair_ga = Swap(p, r["gat"], r["gat"], sems("sw5"), mine, mine, theirs, rc)
    pair_gt = Swap(p, r["send1"], r["recv1"], sems("sw6"), count=rc)

    def unit(name, src, halves, first, count, axis):
        return Scatter(p, src, r["l" + name[0]], halves, first, count, axis, sems(f"s{name}b"), sems(f"s{name}s"))

    ua = [unit(f"a{i}", ga, (i % 2,), (i // 2) * each, each, i % 2) for i in range(heads)]
    ub, uc = ([unit(f"{w}{i}", r["d" + w], (0, 1), i * hw, hw, i) for i in range(2)] for w in "bc")

    for h in range(per):
        for i, w in enumerate(("wq", "wk", "wv")):
            pa[:, h * each + i * head : h * each + (i + 1) * head] = r[w][:, h * head : (h + 1) * head]
    flip = r["flip"]
    flip[:, :n] = r["wo_in"][...]
    turned = flip[...].T
    for h in range(per):
        pa[:, h * each + 3 * head : (h + 1) * each] = turned[:n, h * head : (h + 1) * head]
    sub16 = lax.broadcasted_iota(jnp.int32, (16, 128), 0)
    lane16 = lax.broadcasted_iota(jnp.int32, (16, 128), 1)
    table = jnp.zeros((16, 128), F32)
    for h in range(per):
        for j in range(picks):
            for b in range(nblocks):
                here = (sub16 == h * picks + j) & (lane16 == b)
                table = jnp.where(here, r["rand"][h, j, b].astype(F32), table)
    for i in range(2):
        count = r["lens"][i]
        high = lax.div(count, 32)
        table = jnp.where((sub16 == 15) & (lane16 == 2 * i), high.astype(F32), table)
        table = jnp.where((sub16 == 15) & (lane16 == 2 * i + 1), (count - 32 * high).astype(F32), table)
    pick[...] = table.astype(BF16)

    greet(column_peers(p, mp) + [(d, p.m) for d in plane])
    pcopies = [remote(pick, gpick.at[p.m], us.at[k - 1], ur.at[p.m], (p.d, lax.rem(p.m + k, mp))) for k in range(1, mp)]
    pcopies.append(remote(pick, gpick.at[mp], us.at[mp - 1], ur.at[mp], (p.sib, p.m)))
    mine_too = pltpu.make_async_copy(pick, gpick.at[p.m], ur.at[p.m])
    for copy in pcopies + [mine_too]:
        copy.start()
    for g in ga_parts:
        g.z_send()

    @pl.when(jnp.logical_not(p.inner))
    def _():
        b0.z_send()
        tokens.send()

    wide = lax.broadcasted_iota(jnp.int32, (128, width), 1) - p.d * n
    deep = lax.broadcasted_iota(jnp.int32, (128, width), 0)
    spots = jnp.where((wide == deep) & (deep < n), 1.0, 0.0).astype(BF16)
    vec[...] = dots(r["gains"][...], spots, 1, 0).astype(BF16)
    vcopies = [remote(vec, gvec.at[p.d], vs.at[k], vr.at[p.d], (d, p.m)) for k, d in enumerate(plane)]
    vcopies.append(pltpu.make_async_copy(vec, gvec.at[p.d], vr.at[p.d]))
    for g in ga_parts:
        g.z_mid()
    pl.when(p.inner)(b0.z_send)
    ga_parts[0].forward()
    b0.z_mid()
    pl.when(p.inner)(tokens.send)
    for copy in vcopies:
        copy.start()

    for z in range(mp + 1):
        got(gpick.at[z], us.at[0], ur.at[z], (p.d, p.m))
    row = jnp.where(p.close, gpick[p.m, 15:16, :].astype(F32), gpick[mp, 15:16, :].astype(F32))
    lane = lax.broadcasted_iota(jnp.int32, (1, 128), 1)
    high, low = (jnp.sum(jnp.where(lane == 2 * p.a + i, row, 0.0), 1, keepdims=True) for i in range(2))
    length = high * 32.0 + low
    block = seq // nblocks
    sub = lax.broadcasted_iota(jnp.int32, (nblocks, seq), 0)
    place = lax.broadcasted_iota(jnp.int32, (nblocks, seq), 1)
    rb = lax.div(place, block)
    near = (rb == 0) | (rb == nblocks - 1) | (sub == 0) | (sub == nblocks - 1) | (jnp.abs(rb - sub) <= 1)
    spread = lax.broadcasted_iota(jnp.int32, (128, seq), 0) == lax.div(lax.broadcasted_iota(jnp.int32, (128, seq), 1), block)
    spread = jnp.where(spread, 1.0, 0.0).astype(BF16)
    subf = sub.astype(F32)
    for a in range(2):
        wide = dots(gpick[2 * p.c + a], spread, 1, 0)
        for h in range(per):
            hit = near
            for j in range(picks):
                at_row = h * picks + j
                hit = hit | (wide[at_row : at_row + 1] == subf)
            r["bias"][2 * h + a] = jnp.where(hit, 0.0, NEG).astype(BF16)
    qa, ka = r["qa"], r["ka"]
    low = lax.broadcasted_iota(jnp.int32, (16, seq), 0)
    ka[head : head + nblocks, :] = jnp.where(rb == sub, 1.0, 0.0).astype(BF16)
    beyond = lax.broadcasted_iota(jnp.int32, (16, seq), 1).astype(F32) >= length
    ka[head + nblocks :, :] = jnp.where((low == 0) & beyond, 1.0, 0.0).astype(BF16)
    qa[head + nblocks :, :] = jnp.where(low == 0, NEG, 0.0).astype(BF16)

    for g in ga_parts[1:]:
        g.forward()
    tokens.forward(mp)
    b1.z_send()
    c0.z_send()
    c1.z_send()
    b0.forward()
    tokens.land(mp)

    def project(h):
        span = pl.ds(pl.multiple_of(h * each, each), each)
        for a in range(2):
            at[a, span, :] = ga[a, :, span].T
        own_rows = pl.ds(pl.multiple_of(h * each, each), 3 * head)

        def some(j, _):
            rows = pl.ds(pl.multiple_of(j * rc, rc), rc)
            for a in range(2):
                to = pl.ds(pl.multiple_of((2 * h + a) * 3 * head, head), 3 * head)
                qkv[to, rows] = dots(at[a, own_rows, :], x[rows, :], 1, 1).astype(BF16)
            return 0

        lax.fori_loop(0, seq // rc, some, 0)

    def parts(i):
        return [pl.ds(pl.multiple_of((3 * i + part) * head, head), head) for part in range(3)]

    def set_head(i):
        q, k, v = parts(i)
        qa[0:head, :] = (qkv[q, :].astype(F32) * scale).astype(BF16)
        qa[head : head + nblocks, :] = r["bias"][i]
        ka[0:head, :] = qkv[k, :]
        return q, k, v

    def attend_head(i, _):
        for h in range(per):

            @pl.when(i == 2 * h)
            def _():
                ga_parts[h].land()

        @pl.when(lax.rem(i, 2) == 0)
        def _():
            project(lax.div(i, 2))

        q, k, v = set_head(i)
        own_rows = pl.ds(pl.multiple_of(i * head, head), head)
        for span in (slice(0, seq),):
            scores = dots(ka[...], qa[:, span], 0, 0)
            peak = jnp.max(scores, 0, keepdims=True)
            weights = jnp.exp(scores - peak)
            total = jnp.sum(weights, 0, keepdims=True)
            mixed = jnp.dot(qkv[v, :], weights.astype(BF16), preferred_element_type=F32)
            ctx[own_rows, span] = (mixed / total).astype(BF16)
            r["lse"][i, :, span] = peak + jnp.log(total)

        late = jnp.where(p.outer, 1, 0)

        @pl.when(i == 0 + late)
        def _():
            b1.z_mid()

        @pl.when(i == 2 + late)
        def _():
            c0.z_mid()

        @pl.when(i == 3)
        def _():
            b1.forward()

        @pl.when(i == 4 + late)
        def _():
            c1.z_mid()
            cots.send()

        return 0

    lax.fori_loop(0, heads, attend_head, 0)

    wo = r["wo"]
    for i in range(heads):
        wo[i * head : (i + 1) * head, :] = at[i % 2, (i // 2) * each + 3 * head : (i // 2 + 1) * each, :]
    norms = r["norms"]
    for d in range(8):
        got(gvec.at[d], vs.at[0], vr.at[d], (p.d, p.m))
    vecs = gvec[0].astype(F32)
    for d in range(1, 8):
        vecs = vecs + gvec[d].astype(F32)
    norms[...] = vecs
    g1, s1, g2, s2 = (norms[i : i + 1] for i in range(4))

    def attn_part(first):
        return dots(ctx[:, pl.ds(first, rc)], wo[...], 0, 0)

    for i in range(2):
        r["send"][i * rc : (i + 1) * rc, :] = attn_part(pl.multiple_of(theirs + i * rc, rc)).astype(BF16)
        pair_attn.send(i)
    c0.forward()
    for i in range(2):
        rows = pl.ds(pl.multiple_of(mine + i * rc, rc), rc)
        here = slice(i * rc, (i + 1) * rc)
        part = attn_part(pl.multiple_of(mine + i * rc, rc))
        pair_attn.recv(i)
        n1, inv = norm_rows(x[rows, :].astype(F32) + part + r["recv"][here, :].astype(F32))
        hidden = n1 * g1 + s1
        r["n1"][here, :] = n1
        r["inv1"][here, :] = jnp.broadcast_to(inv, (rc, 128))
        r["res"][here, :] = hidden
        r["hb"][rows, :] = hidden.astype(BF16)
        pair_hid.send(i)

    b0.land()
    b1.land()

    def up(i, _):
        for k in range(2):

            @pl.when(i == 2 + k)
            def _():
                pair_hid.recv(k)

        rows = pl.ds(pl.multiple_of(lax.rem(2 * p.c + i, 4) * rc, rc), rc)
        for a in range(2):
            active, slope = gelu_pair(dots(r["hb"][rows, :], gb[a], 1, 0))
            r["act"][rows, a * width : (a + 1) * width] = active.astype(BF16)
            r["slope"][rows, a * width : (a + 1) * width] = slope.astype(BF16)
        return 0

    lax.fori_loop(0, 4, up, 0)
    c1.forward()
    c0.land()
    c1.land()

    def ffn_part(rows):
        return dots(r["act"][rows, :width], gc[0], 1, 1) + dots(r["act"][rows, width:], gc[1], 1, 1)

    for i in range(2):
        r["send1"][i * rc : (i + 1) * rc, :] = ffn_part(pl.ds(pl.multiple_of(theirs + i * rc, rc), rc)).astype(BF16)
        pair_ffn.send(i)
    cots.finish()
    small = r["small"]
    small[...] = jnp.zeros_like(small)
    for i in range(2):
        rows = pl.ds(pl.multiple_of(mine + i * rc, rc), rc)
        here = slice(i * rc, (i + 1) * rc)
        part = ffn_part(rows)
        pair_ffn.recv(i)
        n2, inv = norm_rows(r["res"][here, :] + part + r["recv1"][here, :].astype(F32))
        pos = (lax.broadcasted_iota(jnp.int32, (rc, 1), 0) + (mine + i * rc)).astype(F32)
        valid = jnp.where(pos < length, 1.0, 0.0)
        r["outb"][here, :] = ((n2 * g2 + s2) * valid).astype(BF16)
        gy = r["ct"][here, :].astype(F32) * valid
        small[2:3, :] += jnp.sum(gy * n2, 0, keepdims=True)
        small[3:4, :] += jnp.sum(gy, 0, keepdims=True)
        g_mid = norm_back(gy * g2, n2, inv)
        r["res"][here, :] = g_mid
        r["gf"][rows, :] = g_mid.astype(BF16)
        pair_gf.send(i)
        home.send(i)

    for g in gathers:
        g.finish()
    for swap in (pair_attn, pair_hid, pair_ffn, pair_gf):
        swap.finish()
    for i in range(2):
        pair_gf.recv(i)

    for k in range(2):

        def grad_c(j, _):
            span = pl.ds(pl.multiple_of(j * rc, rc), rc)
            for a in range(2):
                first = a * width + k * hw
                r["dc"][a, span, k * hw : (k + 1) * hw] = dots(
                    r["gf"][:, span], r["act"][:, first : first + hw], 0, 0
                ).astype(BF16)
            return 0

        lax.fori_loop(0, width // rc, grad_c, 0)
        start_all([uc[k]])

    def back(i, _):
        rows = pl.ds(pl.multiple_of(i * rc, rc), rc)
        for a in range(2):
            part = (rows, slice(a * width, (a + 1) * width))
            r["slope"][part] = (dots(r["gf"][rows, :], gc[a], 1, 0) * r["slope"][part].astype(F32)).astype(BF16)
        return 0

    lax.fori_loop(0, 4, back, 0)

    def hid_part(rows):
        return dots(r["slope"][rows, :width], gb[0], 1, 1) + dots(r["slope"][rows, width:], gb[1], 1, 1)

    for i in range(2):
        r["send"][i * rc : (i + 1) * rc, :] = hid_part(pl.ds(pl.multiple_of(theirs + i * rc, rc), rc)).astype(BF16)
        pair_gh.send(i)
    for u in uc:
        u.second()

    def grad_b(j, _):
        span = pl.ds(pl.multiple_of(j * rc, rc), rc)
        for a in range(2):
            r["db"][a, span, :] = dots(r["hb"][:, span], r["slope"][:, a * width : (a + 1) * width], 0, 0).astype(BF16)
        return 0

    lax.fori_loop(0, width // rc, grad_b, 0)
    start_all(ub)
    for i in range(2):
        rows = pl.ds(pl.multiple_of(mine + i * rc, rc), rc)
        here = slice(i * rc, (i + 1) * rc)
        part = hid_part(rows)
        pair_gh.recv(i)
        gh = r["res"][here, :] + part + r["recv"][here, :].astype(F32)
        n1 = r["n1"][here, :]
        small[0:1, :] += jnp.sum(gh * n1, 0, keepdims=True)
        small[1:2, :] += jnp.sum(gh, 0, keepdims=True)
        g_res = norm_back(gh * g1, n1, r["inv1"][here, 0:1])
        r["res"][here, :] = g_res
        r["gat"][rows, :] = g_res.astype(BF16)
        pair_ga.send(i)
    sums.start(small[...])
    for k in range(4):
        rows = pl.ds(pl.multiple_of(lax.rem(2 * p.c + k, 4) * rc, rc), rc)
        if k >= 2:
            pair_ga.recv(k - 2)
        gctx[:, rows] = dots(wo[...], r["gat"][rows, :], 1, 1).astype(BF16)

    def grad_a(i):
        turn = r["turn"]
        rows = pl.ds(pl.multiple_of(i * 3 * head, head), 3 * head)
        turn[: 3 * head, :] = jnp.dot(qkv[rows, :], x[...], preferred_element_type=F32).astype(BF16)
        rows = pl.ds(pl.multiple_of(i * head, head), head)
        turn[3 * head :, :] = jnp.dot(ctx[rows, :], r["gat"][...], preferred_element_type=F32).astype(BF16)
        ga[lax.rem(i, 2), :, pl.ds(pl.multiple_of(lax.div(i, 2) * each, each), each)] = turn[...].T

    def attend_head_back(i, _):
        q, k, v = set_head(i)
        own_rows = pl.ds(pl.multiple_of(i * head, head), head)
        gk = gv = None
        for j in range(2):
            span = slice(j * half, (j + 1) * half)
            scores = dots(ka[...], qa[:, span], 0, 0)
            probs = jnp.exp(scores - r["lse"][i, :, span])
            grad = gctx[own_rows, span]
            grad_probs = dots(qkv[v, :], grad, 0, 0)
            inner = jnp.sum(probs * grad_probs, 0, keepdims=True)
            grad_scores = (probs * (grad_probs - inner)).astype(BF16)
            qkv[q, span] = (jnp.dot(ka[0:head, :], grad_scores, preferred_element_type=F32) * scale).astype(BF16)
            dk = dots(qa[0:head, span], grad_scores, 1, 1)
            dv = dots(grad, probs.astype(BF16), 1, 1)
            gk, gv = (dk, dv) if gk is None else (gk + dk, gv + dv)
        qkv[k, :] = gk.astype(BF16)
        qkv[v, :] = gv.astype(BF16)

        grad_a(i)
        for k in range(1, heads):

            @pl.when(i == k)
            def _():
                if k == 1:
                    for u in uc:
                        u.third()
                if k == 2:
                    for u in ub:
                        u.second()
                    start_all(ua[:2])
                if k == 3:
                    for u in uc:
                        u.line()
                if k == 4:
                    for u in ub:
                        u.third()
                    for u in ua[:2]:
                        u.second()
                if k == 5:
                    for u in ub:
                        u.line()
                    for u in ua[2:4]:
                        u.second()
                if k % 2 == 1:
                    sums.step(k // 2)
                if k >= 2:
                    start_all([ua[k]])

        return 0

    lax.fori_loop(0, heads, attend_head_back, 0)

    def tok_part(rows):
        total = None
        for i in range(heads):
            mine_rows = slice(i * 3 * head, (i + 1) * 3 * head)
            first = (i // 2) * each
            part = dots(qkv[mine_rows, rows], at[i % 2, first : first + 3 * head, :], 0, 0)
            total = part if total is None else total + part
        return total

    for i in range(2):
        r["send1"][i * rc : (i + 1) * rc, :] = tok_part(pl.ds(pl.multiple_of(theirs + i * rc, rc), rc)).astype(BF16)
        pair_gt.send(i)
    for i in range(2):
        rows = pl.ds(pl.multiple_of(mine + i * rc, rc), rc)
        here = slice(i * rc, (i + 1) * rc)
        part = tok_part(rows)
        pair_gt.recv(i)
        r["gtokb"][here, :] = (r["res"][here, :] + part + r["recv1"][here, :].astype(F32)).astype(BF16)
        home_g.send(i)
    for u in ua[:2]:
        u.third()
    for u in ua[4:]:
        u.second()
    for u in ua[2:4]:
        u.third()
    for u in ua[:2]:
        u.line()
    for u in ua[4:]:
        u.third()
    for u in ua[2:]:
        u.line()
    summed = sums.finish()
    r["sums"][...] = pltpu.roll(summed, width - p.d * n, 1)[:, :128]

    for u in uc + ub:
        u.owned()
    for u in ua:
        pl.when(p.a == u.halves[0])(u.owned)
    home.finish()
    home_g.finish()
    tokens.finish(mp)
    for swap in (pair_gh, pair_ga, pair_gt):
        swap.finish()
    for u in ua + ub + uc:
        u.finish()
    for copy in vcopies[:-1] + pcopies:
        copy.wait_send()


def fused_layer(mp, tok, cot, wq, wk, wv, wo, w_inner, w_outer, gains, lens, rand):
    n, narrow = wq.shape
    quarter, width = tok.shape[1:]
    per, picks, nblocks = rand.shape
    head = narrow // per
    seq = quarter * mp
    half = seq // 2
    group = 3 * per * head
    shape = jax.ShapeDtypeStruct
    SMEM = pl.BlockSpec(memory_space=pltpu.SMEM)
    names = ["tok", "cot", "wq", "wk", "wv", "wo_in", "pb", "pc", "gains", "lens", "rand"]
    outs = {
        "hout": (shape((2, quarter, width), BF16), ANY),
        "hgtok": (shape((2, quarter, width), BF16), ANY),
        **{k: (shape((3, n, width), BF16), ANY) for k in ("la", "lb", "lc")},
        "sums": (shape((8, 128), F32), VMEM),
    }
    weight = ((2, 8 * n, width), BF16)
    rows_b, half_b, half_f = ((seq, width), BF16), ((half, width), BF16), ((half, width), F32)
    bufs = {
        "x": rows_b, "ga": weight, "gb": weight, "gc": weight, "at": weight, "db": weight, "dc": weight,
        "qkv": ((2 * group, seq), BF16), "ctx": ((2 * per * head, seq), BF16), "gctx": ((2 * per * head, seq), BF16),
        "wo": ((2 * per * head, width), BF16), "lse": ((2 * per, 1, seq), F32), "n1": half_f, "inv1": ((half, 128), F32), "res": half_f,
        "hb": rows_b, "act": ((seq, 2 * width), BF16), "slope": ((seq, 2 * width), BF16), "gf": rows_b, "gat": rows_b,
        "send": half_b, "recv": half_b, "send1": half_b, "recv1": half_b, "outb": half_b, "gtokb": half_b, "ct": half_b,
        "gvec": ((8, 16, width), BF16), "gpick": ((mp + 1, 16, 128), BF16), "norms": ((16, width), F32),
        "pa": ((n, width), BF16), "pick": ((16, 128), BF16), "vec": ((16, width), BF16),
        "flip": ((narrow, 128), BF16),
        "bias": ((2 * per, nblocks, seq), BF16), "qa": ((head + nblocks + 16, seq), BF16), "ka": ((head + nblocks + 16, seq), BF16),
        "small": ((8, width), F32), "turn": ((4 * head, width), BF16),
        "sumbuf.0": ((3, 8, width), F32), "sumbuf.1": ((3, 8, width), F32), "sumbuf.2": ((mp, 8, width), F32),
    }
    pieces = {"a": (4 * head, 2 * per, 1), "b": (width // 2, 2, 2), "c": (width // 2, 2, 2)}
    for w, (count, many, halves) in pieces.items():
        for i in range(many):
            for k in range(5):
                bufs[f"s{w}{i}b.{k}"] = ((halves, 2 * n, count), BF16)
    scratch = {k: pltpu.VMEM(*v) for k, v in bufs.items()}

    def add(key, specs):
        for i, spec in enumerate(specs):
            scratch[f"{key}.{i}"] = spec

    add("tok", [DMA((4,)), DMA((mp,)), DMA((mp,)), DMA((mp,))])
    for key in ("cot", "home", "homeg", *(f"sw{i}" for i in range(7))):
        add(key, [DMA((2,)), DMA((2,))])
    for w, (count, many, _) in pieces.items():
        for i in range(width // count):
            add(f"g{w}{i}", gather_sems())
        for i in range(many):
            add(f"s{w}{i}s", [DMA((3,)), DMA((3,)), DMA((4,)), DMA((4,))])
    add("vec", [DMA((7,)), DMA((8,)), DMA((mp,)), DMA((mp + 1,))])
    add("sum", [DMA((3,)), DMA((3,)), DMA((mp - 1,)), DMA((mp,))])
    names = names + list(outs) + list(scratch)
    return pl.pallas_call(
        lambda *refs: layer_kernel(mp, head, nblocks, picks, names, *refs),
        name="layer",
        out_shape=[o[0] for o in outs.values()],
        in_specs=[ANY] * 2 + [VMEM] * 4 + [ANY] * 2 + [VMEM] + [SMEM] * 2,
        out_specs=[o[1] for o in outs.values()],
        scratch_shapes=list(scratch.values()),
        compiler_params=pltpu.CompilerParams(collective_id=0, has_side_effects=True, vmem_limit_bytes=64 << 20),
    )(tok, cot, wq, wk, wv, wo, w_inner, w_outer, gains, lens, rand)


def attend_kernel(q_ref, k_ref, v_ref, bias_ref, hot_ref, ctx_ref, lse_ref, qa, ka):
    seq = q_ref.shape[2]
    head = q_ref.shape[1]
    scale = 1.0 / math.sqrt(head)
    blocks = bias_ref.shape[2]
    step = min(256, seq)
    qa[0:head, :] = (q_ref[0].astype(F32) * scale).astype(BF16)
    qa[head : head + blocks, :] = bias_ref[0, 0]
    low = lax.broadcasted_iota(jnp.int32, (qa.shape[0] - head - blocks, seq), 0)
    qa[head + blocks :, :] = jnp.where(low == 0, NEG, 0.0).astype(BF16)
    ka[0:head, :] = k_ref[0]
    ka[head:, :] = hot_ref[...]
    for i in range(seq // step):
        cols = slice(i * step, (i + 1) * step)
        scores = lax.dot_general(ka[...], qa[:, cols], (((0,), (0,)), ((), ())), preferred_element_type=F32)
        peak = jnp.max(scores, 0, keepdims=True)
        weights = jnp.exp(scores - peak)
        total = jnp.sum(weights, 0, keepdims=True)
        mixed = jnp.dot(v_ref[0], weights.astype(BF16), preferred_element_type=F32)
        ctx_ref[0, :, cols] = (mixed / total).astype(BF16)
        lse_ref[0, 0, :, cols] = peak + jnp.log(total)


def head_specs(head, seq, per, blocks, hot_rows):
    row = lambda part: pl.BlockSpec((1, head, seq), lambda m, h: (m, part * per + h, 0))
    return (
        [row(0), row(1), row(2)],
        pl.BlockSpec((1, 1, blocks, seq), lambda m, h: (m, h, 0, 0)),
        pl.BlockSpec((hot_rows, seq), lambda m, h: (0, 0)),
        pl.BlockSpec((1, 1, 1, seq), lambda m, h: (m, h, 0, 0)),
        row(0),
    )


def attend(qkv, bias, hot, head):
    groups, width, seq = qkv.shape
    per = width // (3 * head)
    rows, bias_spec, hot_spec, line, out = head_specs(head, seq, per, bias.shape[2], hot.shape[0])
    deep = head + hot.shape[0]
    return pl.pallas_call(
        attend_kernel,
        name="attend",
        grid=(groups, per),
        out_shape=[
            jax.ShapeDtypeStruct((groups, per * head, seq), BF16),
            jax.ShapeDtypeStruct((groups, per, 1, seq), F32),
        ],
        in_specs=rows + [bias_spec, hot_spec],
        out_specs=[out, line],
        scratch_shapes=[pltpu.VMEM((deep, seq), BF16), pltpu.VMEM((deep, seq), BF16)],
        compiler_params=pltpu.CompilerParams(vmem_limit_bytes=48 << 20),
    )(qkv, qkv, qkv, bias, hot)


def attend_back_kernel(q_ref, k_ref, v_ref, bias_ref, hot_ref, lse_ref, g_ref, dq_ref, dk_ref, dv_ref, qa, ka, ak, av):
    seq = q_ref.shape[2]
    head = q_ref.shape[1]
    scale = 1.0 / math.sqrt(head)
    blocks = bias_ref.shape[2]
    step = min(256, seq)
    qa[0:head, :] = (q_ref[0].astype(F32) * scale).astype(BF16)
    qa[head : head + blocks, :] = bias_ref[0, 0]
    low = lax.broadcasted_iota(jnp.int32, (qa.shape[0] - head - blocks, seq), 0)
    qa[head + blocks :, :] = jnp.where(low == 0, NEG, 0.0).astype(BF16)
    ka[0:head, :] = k_ref[0]
    ka[head:, :] = hot_ref[...]
    for i in range(seq // step):
        cols = slice(i * step, (i + 1) * step)
        scores = lax.dot_general(ka[...], qa[:, cols], (((0,), (0,)), ((), ())), preferred_element_type=F32)
        probs = jnp.exp(scores - lse_ref[0, 0, :, cols])
        grad = g_ref[0, :, cols]
        grad_probs = lax.dot_general(v_ref[0], grad, (((0,), (0,)), ((), ())), preferred_element_type=F32)
        inner = jnp.sum(probs * grad_probs, 0, keepdims=True)
        grad_scores = (probs * (grad_probs - inner)).astype(BF16)
        dq_ref[0, :, cols] = (jnp.dot(k_ref[0], grad_scores, preferred_element_type=F32) * scale).astype(BF16)
        gk = lax.dot_general(qa[0:head, cols], grad_scores, (((1,), (1,)), ((), ())), preferred_element_type=F32)
        gv = lax.dot_general(grad, probs.astype(BF16), (((1,), (1,)), ((), ())), preferred_element_type=F32)
        if i == 0:
            ak[...] = gk
            av[...] = gv
        else:
            ak[...] += gk
            av[...] += gv
    dk_ref[0] = ak[...].astype(BF16)
    dv_ref[0] = av[...].astype(BF16)


def attend_back(qkv, bias, hot, lse, grad, head):
    groups, width, seq = qkv.shape
    per = width // (3 * head)
    rows, bias_spec, hot_spec, line, out = head_specs(head, seq, per, bias.shape[2], hot.shape[0])
    deep = head + hot.shape[0]
    return pl.pallas_call(
        attend_back_kernel,
        name="attend_back",
        grid=(groups, per),
        out_shape=[jax.ShapeDtypeStruct((groups, per * head, seq), BF16)] * 3,
        in_specs=rows + [bias_spec, hot_spec, line, out],
        out_specs=[out] * 3,
        scratch_shapes=[
            pltpu.VMEM((deep, seq), BF16),
            pltpu.VMEM((deep, seq), BF16),
            pltpu.VMEM((head, seq), F32),
            pltpu.VMEM((head, seq), F32),
        ],
        compiler_params=pltpu.CompilerParams(vmem_limit_bytes=48 << 20),
    )(qkv, qkv, qkv, bias, hot, lse, grad)


def settle_kernel(
    head, out, gtok, la, lb, lc, sums, out_to, gtok_to, gq, gk, gv, go, gb, gc, s0, s1, s2, s3, va, vb, vc, turn, sem
):
    pairs = ((lc, vc), (lb, vb), (la, va), (out, out_to), (gtok, gtok_to))
    copies = [pltpu.make_async_copy(src, dst, sem.at[i]) for i, (src, dst) in enumerate(pairs)]
    for copy in copies:
        copy.start()

    def total(land):
        return land[0].astype(F32) + land[1].astype(F32) + land[2].astype(F32)

    n = gb.shape[0]
    for i, to in enumerate((s0, s1, s2, s3)):
        to[...] = sums[i, :n]
    copies[0].wait()
    gc[...] = total(vc)
    copies[1].wait()
    gb[...] = total(vb)
    copies[2].wait()
    summed = total(va)
    turn[:n, :] = summed
    turned = turn[...].T
    for h in range(gq.shape[1] // head):
        each = 4 * head
        span = slice(h * head, (h + 1) * head)
        for i, to in enumerate((gq, gk, gv)):
            first = h * each + i * head
            to[:, span] = summed[:, first : first + head]
        go[span, :] = turned[h * each + 3 * head : (h + 1) * each, :n]
    for copy in copies[3:]:
        copy.wait()


def settle(head, narrow, out, gtok, la, lb, lc, sums):
    _, n, width = la.shape
    shape = jax.ShapeDtypeStruct
    small, wide = shape((n, narrow), F32), shape((n, width), F32)
    land = pltpu.VMEM(la.shape, BF16)
    return pl.pallas_call(
        lambda *refs: settle_kernel(head, *refs),
        name="settle",
        out_shape=[shape(out.shape, BF16)] * 2 + [small] * 3 + [shape((narrow, n), F32), wide, wide] + [shape((n,), F32)] * 4,
        in_specs=[ANY] * 5 + [VMEM],
        out_specs=[VMEM] * 12,
        scratch_shapes=[land, land, land, pltpu.VMEM((128, width), F32), DMA((5,))],
        compiler_params=pltpu.CompilerParams(vmem_limit_bytes=64 << 20),
    )(out, gtok, la, lb, lc, sums)


def fetch_plain(dp, mp, tok, cot, pa, pb, pc, vec):
    d, m = lax.axis_index("dp"), lax.axis_index("mp")
    core = d % 2
    swap = [(i, i ^ 1) for i in range(dp)]

    def sequence(rows):
        whole = lax.all_gather(rows, "mp", axis=1, tiled=True)
        other = lax.ppermute(whole, "dp", swap)
        return jnp.where(m // 2 == core, whole, other)[m % 2]

    def weight(part):
        plane = lax.all_gather(part, "dp", axis=0, tiled=True)
        return lax.dynamic_slice_in_dim(lax.all_gather(plane, "mp"), 2 * core, 2, 0)

    half = tok.shape[1] * mp // 2
    ct = lax.dynamic_slice_in_dim(sequence(cot), core * half, half, 0)
    return (
        sequence(tok), ct, weight(pa), weight(pb), weight(pc), lax.all_gather(vec, "dp"), lax.all_gather(vec, "mp"),
    )


def deliver_plain(dp, mp, da, db, dc, out, gtok, rows, quarter):
    d, m = lax.axis_index("dp"), lax.axis_index("mp")
    core = d % 2
    swap = [(i, i ^ 1) for i in range(dp)]

    def grad(part):
        wide = jnp.zeros((mp,) + part.shape[1:], F32)
        wide = lax.dynamic_update_slice_in_dim(wide, part.astype(F32), 2 * core, 0)
        mine = lax.psum_scatter(wide, "mp", scatter_dimension=0, tiled=True)[0]
        return lax.psum_scatter(mine, "dp", scatter_dimension=0, tiled=True)[None]

    def home(half):
        both = jnp.zeros((2,) + half.shape, half.dtype)
        both = lax.dynamic_update_slice_in_dim(both, half[None], core, 0)
        both = lax.dynamic_update_slice_in_dim(both, lax.ppermute(half, "dp", swap)[None], 1 - core, 0)
        all_rows = lax.all_gather(both.reshape(mp, quarter, -1), "mp")
        mine = lax.dynamic_slice_in_dim(all_rows, 2 * core, 2, 0)
        return lax.dynamic_slice_in_dim(mine, m, 1, 1)[:, 0]

    return grad(da), grad(db), grad(dc), home(out), home(gtok)


def layer_plain(
    dp, mp, tokens, cotangent, w_query, w_key, w_value, w_out, w_inner, w_outer,
    gain_attn, shift_attn, gain_ffn, shift_ffn, seq_lengths, rand_blocks,
):
    d, m = lax.axis_index("dp"), lax.axis_index("mp")
    core = d % 2
    swap = [(i, i ^ 1) for i in range(dp)]
    quarter, width = tokens.shape[1:]
    seq = quarter * mp
    half = seq // 2
    per, nblocks, picks = rand_blocks.shape
    cols = w_query.shape[1]
    head = cols // per
    block = seq // nblocks
    rows = w_query.shape[0]
    vec_rows = [v.astype(F32) for v in (gain_attn, shift_attn, gain_ffn, shift_ffn)]
    vec_rows += [seq_lengths.astype(F32)]
    flat = rand_blocks.astype(F32).reshape(-1)
    vec_rows += [flat[:128], flat[128:]]
    vec = jnp.stack([jnp.pad(v, (0, 128 - v.shape[0])) for v in vec_rows] + [jnp.zeros(128, F32)])
    pa = jnp.concatenate([w_query, w_key, w_value, w_out.T], 1)
    pb, pc = w_inner, w_outer.T
    x, ct, ga, gb, gc, gvd, gvz = fetch_plain(dp, mp, tokens, cotangent, pa, pb, pc, vec)
    norms = jnp.swapaxes(gvd[:, :4, :rows], 0, 1).reshape(4, width)
    g1, b1, g2, b2 = (norms[i][None] for i in range(4))
    owner = d - core + m // 2
    lens = lax.dynamic_slice_in_dim(gvd[:, 4, :2], owner, 1, 0)[0]
    length = jnp.where(m % 2 == 0, lens[0], lens[1]).astype(jnp.int32)
    picked = lax.dynamic_slice_in_dim(gvz, 2 * core, 2, 0)
    picked = picked[:, 5:7].reshape(2, 256)[:, : per * nblocks * picks].astype(jnp.int32)
    picked = picked.reshape(2, per, nblocks, picks)

    r = jnp.arange(nblocks)
    near = (r[:, None] == 0) | (r[:, None] == nblocks - 1) | (r[None] == 0) | (r[None] == nblocks - 1)
    near = near | (jnp.abs(r[:, None] - r[None]) <= 1)
    hits = jnp.any(picked[:, :, :, :, None] == r, axis=3) | near
    bias = jnp.where(jnp.swapaxes(hits, 2, 3), 0.0, NEG).astype(BF16)
    bias = jnp.repeat(bias, block, axis=3)
    pos = jnp.arange(seq)
    hot = jnp.concatenate([pos[None] // block == r[:, None], pos[None] >= length, jnp.zeros((15, seq), bool)], 0)
    hot = hot.astype(BF16)

    def mine(values):
        return lax.dynamic_slice_in_dim(values, core * half, half, 0)

    def theirs(values):
        return lax.dynamic_slice_in_dim(values, (1 - core) * half, half, 0)

    def pair_sum(partial):
        return mine(partial) + lax.ppermute(theirs(partial).astype(BF16), "dp", swap).astype(F32)

    def pair_join(values):
        other = lax.ppermute(values, "dp", swap)
        lo = jnp.where(core == 0, values, other)
        hi = jnp.where(core == 0, other, values)
        return jnp.concatenate([lo, hi], 0)

    def dot(spec, a, b):
        return jnp.einsum(spec, a, b, preferred_element_type=F32)

    a_qkv, a_out = ga[:, :, : 3 * cols], ga[:, :, 3 * cols :]
    qkv = dot("mrc,tr->mct", a_qkv, x).astype(BF16)
    ctx, lse = attend(qkv, bias, hot, head)
    attn = pair_sum(dot("mct,mdc->td", ctx, a_out))
    x_mine = mine(x).astype(F32)

    def norm(z):
        centre = z - jnp.mean(z, -1, keepdims=True)
        inv = lax.rsqrt(jnp.mean(centre * centre, -1, keepdims=True) + EPS)
        return centre * inv, inv

    n1, inv1 = norm(x_mine + attn)
    hidden = n1 * g1 + b1
    hidden_b = pair_join(hidden.astype(BF16))
    inner = dot("td,mdk->tmk", hidden_b, gb)
    cumul = 0.5 * (1.0 + lax.erf(inner * (1.0 / math.sqrt(2.0))))
    active = (inner * cumul).astype(BF16)
    slope = cumul + inner * jnp.exp(-0.5 * inner * inner) * (1.0 / math.sqrt(2.0 * math.pi))
    n2, inv2 = norm(hidden + pair_sum(dot("tmk,mdk->td", active, gc)))
    valid = (core * half + jnp.arange(half) < length).astype(F32)[:, None]
    out = ((n2 * g2 + b2) * valid).astype(BF16)

    def norm_back(e, n, inv):
        return (e - jnp.mean(e, -1, keepdims=True) - n * jnp.mean(e * n, -1, keepdims=True)) * inv

    gy = ct.astype(F32) * valid
    g_mid = norm_back(gy * g2, n2, inv2)
    d_gain2, d_shift2 = jnp.sum(gy * n2, 0), jnp.sum(gy, 0)
    g_ffn = pair_join(g_mid.astype(BF16))
    d_c = dot("td,tmk->mdk", g_ffn, active).astype(BF16)
    g_inner = (dot("td,mdk->tmk", g_ffn, gc) * slope).astype(BF16)
    d_b = dot("td,tmk->mdk", hidden_b, g_inner).astype(BF16)
    g_hidden = g_mid + pair_sum(dot("tmk,mdk->td", g_inner, gb))
    d_gain1, d_shift1 = jnp.sum(g_hidden * n1, 0), jnp.sum(g_hidden, 0)
    g_res = norm_back(g_hidden * g1, n1, inv1)
    g_attn = pair_join(g_res.astype(BF16))
    d_out = dot("td,mct->mdc", g_attn, ctx).astype(BF16)
    g_ctx = dot("td,mdc->mct", g_attn, a_out).astype(BF16)
    sums = jnp.stack([d_gain1, d_shift1, d_gain2, d_shift2] + [jnp.zeros_like(d_gain1)] * 4)
    dq, dk, dv = attend_back(qkv, bias, hot, lse, g_ctx, head)
    dqkv = jnp.concatenate([dq, dk, dv], 1)
    d_qkv = dot("tr,mct->mrc", x, dqkv).astype(BF16)
    d_a = jnp.concatenate([d_qkv, d_out], 2)
    gtok = (g_res + pair_sum(dot("mct,mrc->tr", dqkv, a_qkv))).astype(BF16)
    ra, rb, rc, out, gtok = deliver_plain(dp, mp, d_a, d_b, d_c, out, gtok, rows, quarter)
    sums = lax.psum(sums, ("dp", "mp"))
    ra, rb, rc = (jnp.sum(v.astype(F32), 0) for v in (ra, rb, rc))
    sums = lax.dynamic_slice_in_dim(sums, d * rows, rows, 1)
    return (
        out, gtok, ra[:, :cols], ra[:, cols : 2 * cols], ra[:, 2 * cols : 3 * cols], ra[:, 3 * cols :].T, rb, rc.T,
        sums[0], sums[1], sums[2], sums[3],
    )


def layer(
    dp, mp, tokens, cotangent, w_query, w_key, w_value, w_out, w_inner, w_outer,
    gain_attn, shift_attn, gain_ffn, shift_ffn, seq_lengths, rand_blocks,
):
    rows, cols = w_query.shape
    per, nblocks, picks = rand_blocks.shape
    if not (dp == 8 and mp == 4 and rows % 16 == 0 and 4 * cols == 8 * rows and tokens.shape[0] == 2):
        return layer_plain(
            dp, mp, tokens, cotangent, w_query, w_key, w_value, w_out, w_inner, w_outer,
            gain_attn, shift_attn, gain_ffn, shift_ffn, seq_lengths, rand_blocks,
        )
    gains = jnp.pad(jnp.stack([gain_attn, shift_attn, gain_ffn, shift_ffn]), ((0, 12), (0, 128 - rows)))
    picked = jnp.swapaxes(rand_blocks, 1, 2)
    landed = fused_layer(
        mp, tokens, cotangent, w_query, w_key, w_value, w_out, w_inner, w_outer.T, gains, seq_lengths, picked
    )
    done = settle(cols // per, cols, *landed)
    return *done[:7], done[7].T, *done[8:]


def solution(mesh):
    dp, mp = mesh.shape["dp"], mesh.shape["mp"]
    act, vec = P("dp", "mp", None), P("dp")
    w_in, w_back = P("dp", "mp"), P("mp", "dp")

    def step(*args):
        return layer(dp, mp, *args)

    return jax.shard_map(
        step,
        mesh=mesh,
        in_specs=(act, act, w_in, w_in, w_in, w_back, w_in, w_back, vec, vec, vec, vec, vec, P("mp", None, None)),
        out_specs=(act, act, w_in, w_in, w_in, w_back, w_in, w_back, vec, vec, vec, vec),
        check_vma=False,
    )
```
